128 devices in a mesh: gy: 8 (over z_hi, y), gx: 16 (over x, z_lo, core).
Axes of the slice: x: 4, y: 4, z: 4 (z_hi: 2, z_lo: 2; z = z_hi * 2 + z_lo), core: 2. Of those that a mesh axis runs over, the one named last changes fastest.
Arguments:
- ocean_state: bfloat16 [3072, 16, 4096], P('gy', None, 'gx'), may hold values from -6 to 6
- atm_blocks: bfloat16 [24576, 16, 128], P(('gy', 'gx')), may hold values from -6 to 6
- dest_tile: int32 [24576, 1], P(('gy', 'gx')), may hold values from 0 to 127; in each aligned block of 192 rows (0 to 191, 192 to 383, ...) at most 3 rows name the same one
- dest_row: int32 [24576], P(('gy', 'gx')), may hold values from 0 to 191
- live_entry: int32 [24576], P(('gy', 'gx')), may hold values 0 or 1
- land_mask: int32 [3072, 4096], P('gy', 'gx'), may hold values 0 or 1
- fold_pair: int32 [16], replicated, may hold values from 0 to 15, as said below
- first_weight: bfloat16 [3, 3, 64, 32], replicated, may hold values from -0.375 to 0.375
- first_bias: float32 [64], replicated, may hold values from -3 to 3
- second_weight: bfloat16 [3, 3, 8, 64], replicated, may hold values from -0.25 to 0.25
- second_bias: float32 [8], replicated, may hold values from -3 to 3
Outputs:
- eddy_forcing: bfloat16 [3072, 8, 4096], P('gy', None, 'gx')
The draws below stay inside these ranges and needn't reach their ends.
Inputs may be any that keep to these rules, and one draw needn't show every extreme that they name: `dest_tile`: at most 3 of the 192 entries held by one device name the same tile, and some device names some tile exactly 3 times. fold_pair[fold_pair[t]] = t and fold_pair[t] != t for every tile t.
All inputs are finite; a program needn't handle non-finite values. No bound on the sum of `live_entry` or of `land_mask` on one device may be relied on, other than what follows from the above.
Results may differ from the reference program's by a relative error of at most 0.005.
Values may be sent and summed in bfloat16 or wider, within the bound.
No kernel may reach another device: no remote copies, remote signals or barrier semaphores. Data moves between devices by JAX's collectives and lax.ppermute only.
A program may use at most 192 MiB of HBM per device.

```python
import math
import jax
import jax.numpy as jnp
import numpy as np
from jax import lax

LEV = 4
F = 16
HID = 64
BLOCK = 128
CX = 256
CYH = 192
CAP = 3
BLOCKS = 24576
NLAT = 3072
NLON = 4096
LON_TILES = 16
CIN = 32
OUT = 8
N_GY = 8
N_GX = 16
DEVICES = 128


def draw_fold_pair(key, part):
    order = jax.random.permutation(key, LON_TILES).astype(jnp.int32)
    first_half = order[0::2]
    second_half = order[1::2]
    paired = jnp.zeros((LON_TILES,), jnp.int32)
    paired = paired.at[first_half].set(second_half).at[second_half].set(first_half)
    return paired.astype(jnp.int32)


def place_ends(drawn, own_key, smallest, high):
    longest = drawn.shape.index(max(drawn.shape))
    spots = []
    for shift in (0, 1):
        where = [jax.random.randint(jax.random.fold_in(own_key, axis), (), 0, length) for axis, length in enumerate(drawn.shape)]
        where[longest] = (where[longest] + shift) % drawn.shape[longest]
        spots.append(tuple(where))
    return drawn.at[spots[0]].set(smallest).at[spots[1]].set(high)


def block_scale(key, dims, shards, least, largest):
    gain, own = 1.0, jax.random.fold_in(key, 6)
    for axis_at, blocks in shards:
        heights = jnp.exp(jax.random.uniform(jax.random.fold_in(own, axis_at), (blocks,), jnp.float32, least / len(shards), largest / len(shards)))
        gain = gain * jnp.repeat(heights, dims[axis_at] // blocks).reshape([-1 if axis == axis_at else 1 for axis in range(len(dims))])
    return gain


def routed_block(key, own, number, rows, count, top, limit, slope):
    ranking = jax.random.permutation(key, count)
    packed, common = shares(count, rows * top, limit, slope, True), shares(count, rows * top, limit, slope, False)
    places = jnp.arange(count)

    def named(sizes, turn):
        used = int((sizes > 0).sum())
        fixed = max(1, used // 4)
        moved = fixed + (places - fixed + turn * (used - fixed)) % max(1, count - fixed)
        return jnp.zeros((count,), jnp.int32).at[ranking[jnp.where(places < fixed, places, moved)]].set(jnp.asarray(sizes, jnp.int32))

    sizes = jnp.where(number % 4 == 0, named(packed, number // 4), named(common, number - number // 4 - 1))
    mixed = jax.random.permutation(jax.random.fold_in(own, 3), count)
    donor, taker = mixed[0:count // 2 * 2:2], mixed[1:count // 2 * 2:2]
    slack = jnp.minimum(sizes[donor] - 1, limit - sizes[taker]) // 2
    slack = jnp.where((donor == ranking[0]) | (taker == ranking[0]) | (sizes[taker] == 0), 0, jnp.maximum(slack, 0))
    moved = jax.random.randint(jax.random.fold_in(own, 4), (count // 2,), 0, 1 << 20) % (slack + 1)
    sizes = sizes.at[donor].add(-moved).at[taker].add(moved)
    members = jnp.searchsorted(jnp.cumsum(sizes), jnp.arange(rows * top), side="right").astype(jnp.int32)
    table = members.reshape(top, rows).T
    table = table[jax.random.permutation(jax.random.fold_in(own, 1), rows)]
    turn = jax.random.randint(jax.random.fold_in(own, 2), (rows, 1), 0, top)
    return jnp.take_along_axis(table, (jnp.arange(top)[None, :] + turn) % top, axis=1)


def shares(count, total, most, slope, full):
    portions = [(1 << 20) // math.isqrt(standing ** slope) + 1 for standing in range(1, count + 1)]
    largest = most if full else min(most, max(-(-total // count), total * portions[0] // sum(portions)))
    least = 1 if total - largest >= count - 1 else 0
    holding, rest = [largest] + [least] * (count - 1), total - largest - least * (count - 1)
    while rest > 0:
        movable = [i for i in range(1, count) if holding[i] < largest] or [i for i in range(1, count) if holding[i] < most]
        pool, budget = sum([portions[i] for i in movable]), rest
        for i in movable:
            extra = min(most - holding[i], max(1, budget * portions[i] // pool), rest)
            holding[i] = holding[i] + extra
            rest = rest - extra
    return np.array(holding)


def centred(rng, extent, scale, most, shards=(), kind=jnp.bfloat16):
    entries = jax.random.normal(rng, extent, jnp.float32) * scale
    if len(shards) > 0:
        entries = block_scale(rng, extent, shards, -0.22, 0.18) * entries
    return jnp.clip(entries, min=-most, max=most).astype(kind)


def setup_inputs(seed: int = 0) -> dict:
    arg_keys = jax.random.split(jax.random.key(seed), 12)
    ocean_state = centred(arg_keys[0], (NLAT, 4 * LEV, NLON), 1.0, 6.0, ((0, 8), (2, 16)))
    atm_blocks = centred(arg_keys[1], (BLOCKS, F, BLOCK), 1.0, 6.0, ((0, 128),))
    dest_tile_keys = jax.random.split(jax.random.fold_in(arg_keys[2], 1), BLOCKS // CYH)
    dest_tile_turns = jax.random.permutation(jax.random.fold_in(arg_keys[2], 3), BLOCKS // CYH)
    dest_tile = jax.vmap(lambda own, number: routed_block(jax.random.fold_in(arg_keys[2], 2), own, number, CYH, DEVICES, 1, CAP, 2))(dest_tile_keys, dest_tile_turns).reshape((BLOCKS, 1))
    dest_row = place_ends(jax.random.randint(arg_keys[3], (BLOCKS,), 0, CYH), jax.random.fold_in(arg_keys[3], 1), 0, CYH - 1).astype(jnp.int32)
    live_entry = place_ends((jax.random.randint(arg_keys[4], (BLOCKS,), 0, 8) < 7).astype(jnp.int32), jax.random.fold_in(arg_keys[4], 1), 0, 1)
    land_mask = place_ends((jax.random.randint(arg_keys[5], (NLAT, NLON), 0, 4) < 3).astype(jnp.int32), jax.random.fold_in(arg_keys[5], 1), 0, 1)
    fold_pair = draw_fold_pair(jax.random.fold_in(arg_keys[11], 71), 0)
    first_weight = centred(arg_keys[7], (3, 3, HID, CIN), (9 * CIN) ** -0.5, 0.375)
    first_bias = centred(arg_keys[8], (HID,), 0.5, 3.0, (), jnp.float32)
    second_weight = centred(arg_keys[9], (3, 3, OUT, HID), (9 * HID) ** -0.5, 0.25)
    second_bias = centred(arg_keys[10], (OUT,), 0.5, 3.0, (), jnp.float32)
    return dict(ocean_state=ocean_state, atm_blocks=atm_blocks, dest_tile=dest_tile, dest_row=dest_row, live_entry=live_entry, land_mask=land_mask, fold_pair=fold_pair, first_weight=first_weight, first_bias=first_bias, second_weight=second_weight, second_bias=second_bias)


row_step = 64


def fold_columns(fold_pair):
    columns = (jnp.arange(-1, NLON + 1) % NLON).astype(jnp.int32)
    tiles = (columns // CX).astype(jnp.int32)
    return (jnp.take(fold_pair, tiles) * CX + CX - 1 - columns % CX).astype(jnp.int32)


def convolve(padded, weight):
    count = padded.shape[0] - 2
    total = jnp.zeros((count, weight.shape[2], NLON), jnp.float32)
    for shift_y in range(3):
        for shift_x in range(3):
            total = total + jnp.einsum("oc,ycx->yox", weight[shift_y, shift_x].astype(jnp.float32), padded[shift_y:shift_y + count, :, shift_x:shift_x + NLON].astype(jnp.float32))
    return total


def reference(ocean_state, atm_blocks, dest_tile, dest_row, live_entry, land_mask, fold_pair, first_weight, first_bias, second_weight, second_bias):
    flat_blocks = atm_blocks.reshape(BLOCKS, F * BLOCK).astype(jnp.float32)
    segment = jnp.where(live_entry == 1, dest_tile[:, 0] * CYH + dest_row, N_GY * N_GX * CYH).astype(jnp.int32)
    summed = jax.ops.segment_sum(flat_blocks, segment, num_segments=N_GY * N_GX * CYH + 1)[:-1]
    coarse = summed.astype(jnp.bfloat16).reshape(N_GY, N_GX, CYH, F, BLOCK)
    coarse = coarse.transpose(0, 2, 3, 1, 4).reshape(N_GY * CYH, F, N_GX * BLOCK)
    channel = jnp.arange(CIN)
    in_signs = jnp.where((channel < 2 * LEV) | (channel == 4 * LEV) | (channel == 4 * LEV + 1), -1.0, 1.0).astype(jnp.bfloat16)
    hidden_signs = jnp.ones((HID,), jnp.bfloat16)
    partner = fold_columns(fold_pair)
    mask_values = land_mask.astype(jnp.bfloat16)

    def input_rows(start, count):
        index = (start + jnp.arange(count)).astype(jnp.int32)
        clipped = jnp.clip(index, 0, NLAT - 1).astype(jnp.int32)
        states = jnp.take(ocean_state, clipped, axis=0)
        forcing = jnp.repeat(jnp.take(coarse, (clipped // 2).astype(jnp.int32), axis=0), 2, axis=2)
        mixed = jnp.concatenate([states, forcing], axis=1) * jnp.take(mask_values, clipped, axis=0)[:, None, :]
        return index, mixed

    def pad_rows(index, field_rows, top_row, signs):
        wrapped = jnp.concatenate([field_rows[:, :, -1:], field_rows, field_rows[:, :, :1]], axis=2)
        folded = jnp.take(top_row, partner, axis=1) * signs[:, None]
        inside = ((index >= 0) & (index < NLAT))[:, None, None]
        above = (index == NLAT)[:, None, None]
        return jnp.where(inside, wrapped, jnp.where(above, folded[None], jnp.zeros_like(wrapped)))

    top_index, top_rows = input_rows(NLAT - 1, 1)
    top_input = top_rows[0]
    near_index, near_rows = input_rows(NLAT - 2, 3)
    near_hidden = convolve(pad_rows(near_index, near_rows, top_input, in_signs), first_weight)
    hidden_top = jnp.maximum(near_hidden + first_bias[None, :, None], 0.0).astype(jnp.bfloat16)[0]

    def one_block(number):
        start = (number * row_step).astype(jnp.int32)
        index, field_rows = input_rows(start - 2, row_step + 4)
        hidden = convolve(pad_rows(index, field_rows, top_input, in_signs), first_weight)
        hidden = jnp.maximum(hidden + first_bias[None, :, None], 0.0).astype(jnp.bfloat16)
        hidden_index = (start - 1 + jnp.arange(row_step + 2)).astype(jnp.int32)
        padded_hidden = pad_rows(hidden_index, hidden, hidden_top, hidden_signs)
        result = convolve(padded_hidden, second_weight) + second_bias[None, :, None]
        mask_rows = lax.dynamic_slice_in_dim(mask_values, start, row_step, 0)
        return (result * mask_rows[:, None, :]).astype(jnp.bfloat16)

    blocks = lax.map(one_block, jnp.arange(NLAT // row_step, dtype=jnp.int32))
    return blocks.reshape(NLAT, OUT, NLON)
```

```python
import functools

import jax
import jax.numpy as jnp
from jax import lax
from jax.experimental import pallas as pl
from jax.experimental.pallas import tpu as pltpu
from jax.sharding import PartitionSpec as P

BF = jnp.bfloat16
F32 = jnp.float32
I32 = jnp.int32
VMEM_LIMIT = 56 << 20
ROWS = 384
COLS = 256
HALF = 192
DEV = 128
CAP = 3
FLD = 16
HID = 64
OUT = 8


def lanes(shape):
    return lax.broadcasted_iota(I32, shape, len(shape) - 1)


def subs(shape):
    return lax.broadcasted_iota(I32, shape, len(shape) - 2)


def pack_kernel(code_ref, atm_ref, out_ref, rows_ref, count_ref):
    def clear(t, carry):
        count_ref[t] = 0
        for k in range(CAP):
            rows_ref[t, k] = HALF
        return carry

    lax.fori_loop(0, DEV, clear, 0, unroll=8)

    def place(i, carry):
        code = code_ref[i]

        @pl.when(code >= 0)
        def _():
            tile = code // 256
            rank = count_ref[tile]
            count_ref[tile] = rank + 1
            rows_ref[tile, rank] = code - tile * 256
            out_ref[tile * CAP + rank] = atm_ref[i]

        return carry

    lax.fori_loop(0, HALF, place, 0, unroll=4)


def pack(code, atm):
    return pl.pallas_call(
        pack_kernel,
        out_shape=(
            jax.ShapeDtypeStruct((DEV * CAP, FLD, 128), BF),
            jax.ShapeDtypeStruct((DEV, CAP), I32),
        ),
        in_specs=[
            pl.BlockSpec(memory_space=pltpu.SMEM),
            pl.BlockSpec(memory_space=pltpu.VMEM),
        ],
        out_specs=(
            pl.BlockSpec(memory_space=pltpu.VMEM),
            pl.BlockSpec(memory_space=pltpu.SMEM),
        ),
        scratch_shapes=[pltpu.SMEM((DEV,), I32)],
        name="pack",
    )(code, atm)


def coarse_kernel(rows_ref, inc_ref, out_ref, cols_ref, acc_ref):
    acc_ref[...] = jnp.zeros_like(acc_ref)

    def add(s, carry):
        for k in range(CAP):
            r = rows_ref[s, k]
            acc_ref[k, r] = acc_ref[k, r] + inc_ref[s * CAP + k].astype(F32)
        return carry

    lax.fori_loop(0, DEV, add, 0, unroll=4)
    lane = lanes((FLD, 128))
    for chunk, count in ((0, 128), (128, 64)):

        def finish(i, carry):
            first, last = carry
            r = chunk + i
            total = (acc_ref[0, r] + acc_ref[1, r] + acc_ref[2, r]).astype(BF)
            out_ref[r] = total
            total = total.astype(F32)
            here = lane == i
            first = jnp.where(here, pltpu.roll(total, i, 1), first)
            last = jnp.where(here, pltpu.roll(total, i + 1, 1), last)
            return first, last

        zero = jnp.zeros((FLD, 128), F32)
        first, last = lax.fori_loop(0, count, finish, (zero, zero), unroll=4)
        cols_ref[0, :, chunk : chunk + 128] = first.astype(BF)
        cols_ref[1, :, chunk : chunk + 128] = last.astype(BF)


def coarse_sums(rows, incoming):
    return pl.pallas_call(
        coarse_kernel,
        out_shape=(
            jax.ShapeDtypeStruct((HALF, FLD, 128), BF),
            jax.ShapeDtypeStruct((2, FLD, 256), BF),
        ),
        in_specs=[
            pl.BlockSpec(memory_space=pltpu.SMEM),
            pl.BlockSpec(memory_space=pltpu.VMEM),
        ],
        out_specs=(
            pl.BlockSpec(memory_space=pltpu.VMEM),
            pl.BlockSpec(memory_space=pltpu.VMEM),
        ),
        scratch_shapes=[pltpu.VMEM((CAP, HALF + 1, FLD, 128), F32)],
        compiler_params=pltpu.CompilerParams(vmem_limit_bytes=VMEM_LIMIT),
        name="coarse",
    )(rows, incoming)


def edge_kernel(ocean_ref, mask_ref, out_ref):
    lane = lanes((2 * FLD, 128))
    for chunk in range(3):

        def take(i, carry):
            y = chunk * 128 + i
            m = mask_ref[pl.ds(y, 1), :].astype(F32)
            m = jnp.broadcast_to(m, (FLD, COLS))
            x = jnp.concatenate([ocean_ref[y].astype(F32) * m, m], axis=0)
            left, right = x[:, :128], x[:, 128:]
            here = lane == i
            c0, c1, c2, c3 = carry
            c0 = jnp.where(here, pltpu.roll(left, i, 1), c0)
            c1 = jnp.where(here, pltpu.roll(left, i + 127, 1), c1)
            c2 = jnp.where(here, pltpu.roll(right, i + 2, 1), c2)
            c3 = jnp.where(here, pltpu.roll(right, i + 1, 1), c3)
            return c0, c1, c2, c3

        zero = jnp.zeros((2 * FLD, 128), F32)
        got = lax.fori_loop(0, 128, take, (zero,) * 4, unroll=2)
        for k in range(4):
            out_ref[k, :, chunk * 128 : chunk * 128 + 128] = got[k].astype(BF)


def edge_columns(ocean, mask):
    return pl.pallas_call(
        edge_kernel,
        out_shape=jax.ShapeDtypeStruct((4, 2 * FLD, ROWS), BF),
        compiler_params=pltpu.CompilerParams(vmem_limit_bytes=VMEM_LIMIT),
        name="edges",
    )(ocean, mask)


def main_kernel(
    ocean_ref, mask_ref, coarse_ref, own_ref, west_ref, east_ref, cown_ref, cwest_ref, ceast_ref,
    w1_ref, w1t_ref, b1_ref, w2_ref, w2l_ref, w2r_ref, b2_ref, out_ref,
    fine_ref, xs_ref, h_ref, side_ref, add_ref,
):
    rep = (subs((256, ROWS)) == lanes((256, ROWS)) // 2).astype(BF)

    def column(coarse_t, strip):
        fine = jnp.dot(coarse_t, rep, preferred_element_type=F32)
        return jnp.concatenate([strip[:FLD], (fine * strip[FLD:].astype(F32)).astype(BF)], axis=0)

    w2c = column(cwest_ref[...], west_ref[0])
    w1c = column(cwest_ref[...], west_ref[1])
    o0c = column(cown_ref[0], own_ref[0])
    o255c = column(cown_ref[1], own_ref[3])
    e1c = column(ceast_ref[...], east_ref[0])
    e2c = column(ceast_ref[...], east_ref[1])
    side_ref[0] = w1c.astype(F32)
    side_ref[1] = e1c.astype(F32)
    b1 = b1_ref[...]
    for side, cols, w2s in ((0, (w2c, w1c, o0c), w2l_ref), (1, (o255c, e1c, e2c), w2r_ref)):
        x = jnp.concatenate([c.astype(F32) for c in cols], axis=0)
        xt = jnp.concatenate([pltpu.roll(x, 1, 1), x, pltpu.roll(x, ROWS - 1, 1)], axis=0).astype(BF)
        hid = jnp.dot(w1t_ref[...], xt, preferred_element_type=F32)
        hid = jnp.maximum(hid + b1[:HID], 0.0).astype(BF).astype(F32)
        ht = jnp.concatenate([pltpu.roll(hid, 1, 1), hid, pltpu.roll(hid, ROWS - 1, 1)], axis=0)
        add_ref[side] = jnp.dot(w2s[...], ht.astype(BF), preferred_element_type=F32)

    spread = (subs((128, COLS)) == lanes((128, COLS)) // 2).astype(BF)
    for k in range(6):
        part = coarse_ref[k * 32 : k * 32 + 32].reshape(512, 128)
        fine = jnp.dot(part, spread, preferred_element_type=F32)
        fine_ref[k * 32 : k * 32 + 32] = fine.astype(BF).reshape(32, FLD, COLS)

    lane = lanes((2 * FLD, 128))
    zero = jnp.zeros((96, COLS), BF)
    xs_ref[0] = zero
    xs_ref[ROWS + 1] = zero
    for chunk in range(3):

        def build(i, carry):
            y = chunk * 128 + i
            m = jnp.broadcast_to(mask_ref[pl.ds(y, 1), :].astype(F32), (FLD, COLS))
            x = jnp.concatenate(
                [ocean_ref[y].astype(F32) * m, fine_ref[y // 2].astype(F32) * m], axis=0
            )
            west = pltpu.roll(side_ref[0, :, chunk * 128 : chunk * 128 + 128], 128 - i, 1)
            east = pltpu.roll(side_ref[1, :, chunk * 128 : chunk * 128 + 128], 127 - i, 1)
            up = pltpu.roll(x, 1, 1)
            down = pltpu.roll(x, COLS - 1, 1)
            up0 = jnp.where(lane == 0, west, up[:, :128])
            down1 = jnp.where(lane == 127, east, down[:, 128:])
            xs_ref[y + 1, 0:32, 0:128] = up0.astype(BF)
            xs_ref[y + 1, 0:32, 128:256] = up[:, 128:].astype(BF)
            xs_ref[y + 1, 32:64, :] = x.astype(BF)
            xs_ref[y + 1, 64:96, 0:128] = down[:, :128].astype(BF)
            xs_ref[y + 1, 64:96, 128:256] = down1.astype(BF)
            return carry

        lax.fori_loop(0, 128, build, 0, unroll=2)

    hzero = jnp.zeros((HID, COLS), BF)
    h_ref[0] = hzero
    h_ref[ROWS + 1] = hzero

    def conv1(block, carry):
        for k in range(8):
            g = block * 8 + k
            x = xs_ref[pl.ds(3 * g, 5)].reshape(480, COLS)
            t = jnp.dot(w1_ref[...], x, preferred_element_type=F32)
            t = jnp.maximum(t + b1, 0.0).astype(BF)
            h_ref[pl.ds(3 * g + 1, 3)] = t.reshape(3, HID, COLS)
        return carry

    lax.fori_loop(0, 16, conv1, 0)

    b2 = b2_ref[...]
    lane8 = lanes((OUT, 128))

    def conv2(block, carry):
        for k in range(4):
            j = block * 4 + k
            x = h_ref[pl.ds(6 * j, 8)].reshape(512, COLS)
            t = jnp.dot(w2_ref[...], x, preferred_element_type=F32).reshape(6, 3, OUT, COLS)
            for r in range(6):
                y = 6 * j + r
                base = pl.multiple_of((y // 128) * 128, 128)
                i = y % 128
                west = pltpu.roll(add_ref[0, :, pl.ds(base, 128)], 128 - i, 1)
                east = pltpu.roll(add_ref[1, :, pl.ds(base, 128)], 127 - i, 1)
                up = pltpu.roll(t[r, 0], 1, 1)
                down = pltpu.roll(t[r, 2], COLS - 1, 1)
                mid = t[r, 1] + b2
                m = mask_ref[pl.ds(y, 1), :].astype(F32)
                lo = mid[:, :128] + jnp.where(lane8 == 0, west, up[:, :128]) + down[:, :128]
                hi = mid[:, 128:] + up[:, 128:] + jnp.where(lane8 == 127, east, down[:, 128:])
                out_ref[y, :, 0:128] = (lo * m[:, :128]).astype(BF)
                out_ref[y, :, 128:256] = (hi * m[:, 128:]).astype(BF)
        return carry

    lax.fori_loop(0, 16, conv2, 0)


def main_conv(*args):
    return pl.pallas_call(
        main_kernel,
        out_shape=jax.ShapeDtypeStruct((ROWS, OUT, COLS), BF),
        scratch_shapes=[
            pltpu.VMEM((HALF, FLD, COLS), BF),
            pltpu.VMEM((ROWS + 2, 96, COLS), BF),
            pltpu.VMEM((ROWS + 2, HID, COLS), BF),
            pltpu.VMEM((2, 2 * FLD, ROWS), F32),
            pltpu.VMEM((2, OUT, ROWS), F32),
        ],
        compiler_params=pltpu.CompilerParams(vmem_limit_bytes=VMEM_LIMIT),
        name="convs",
    )(*args)


PAD = 384
SHIFT = 2


def onehot(pairs, rows, cols):
    src = subs((rows, cols))
    dst = lanes((rows, cols))
    hit = jnp.zeros((rows, cols), jnp.bool_)
    for source, cond in pairs:
        hit = hit | ((src == source(dst)) & cond(dst))
    return hit.astype(BF)


def patch_kernel(
    pos_ref, fold_ref, ocean_ref, coarse_ref, tops_ref, ctops_ref, w1_ref, b1_ref, w2_ref, b2_ref, main_ref,
    out_ref, in_ref, res_ref, sem,
):
    gy, gx = pos_ref[0], pos_ref[1]
    spread = (subs((256, PAD)) == lanes((256, PAD)) // 2).astype(BF)
    spread = jnp.where(lanes((256, PAD)) < COLS + 4, spread, jnp.zeros_like(spread))
    signs = jnp.where(
        (subs((2 * FLD, PAD)) < 8) | (subs((2 * FLD, PAD)) == 16) | (subs((2 * FLD, PAD)) == 17), -1.0, 1.0
    )

    def inputs(strip, coarse):
        fine = jnp.dot(coarse, spread, preferred_element_type=F32)
        return jnp.concatenate(
            [strip[:FLD], (fine * strip[FLD:].astype(F32)).astype(BF)], axis=0
        )

    for k in range(12):
        in_ref[k] = inputs(ocean_ref[k], coarse_ref[k // 2]).astype(F32)
    for k in range(3):
        in_ref[12 + k] = jnp.zeros((2 * FLD, PAD), F32)

    wrap = lambda t: jnp.where(t < 0, t + 16, jnp.where(t > 15, t - 16, t))
    near = wrap(gx - 1)
    far = wrap(gx + 1)
    p = fold_ref[gx]
    a = fold_ref[near]
    b = fold_ref[far]

    @pl.when(gy == 7)
    def _():
        def tile(t, row):
            return inputs(tops_ref[t, row], ctops_ref[t])

        def move(x, pairs):
            return jnp.dot(x, onehot(pairs, PAD, PAD), preferred_element_type=F32)

        def inside(lo, hi):
            return lambda d: (d >= lo) & (d <= hi)

        mirror = lambda d: 2 * SHIFT + COLS - 1 - d
        a1 = tile(a, 1)
        b1 = tile(b, 1)
        p1 = tile(p, 1)
        row = move(p1, [(mirror, inside(SHIFT, SHIFT + 255))])
        row = row + move(a1, [(lambda d: SHIFT + 1 - d, inside(0, 1))])
        row = row + move(b1, [(lambda d: SHIFT + 255 - (d - (SHIFT + 256)), inside(SHIFT + 256, SHIFT + 257))])
        in_ref[10] = row * signs
        corner_a = [(lambda d: SHIFT + 1 - (d - 264), inside(264, 266))]
        corner_b = [(lambda d: SHIFT + 256 - (d - 272), inside(272, 274))]
        whole = [(mirror, inside(SHIFT - 1, SHIFT + 256))]
        for k in range(2):
            in_ref[12 + k] = (
                move(p1 if k else tile(p, 0), whole)
                + move(a1 if k else tile(a, 0), corner_a)
                + move(b1 if k else tile(b, 0), corner_b)
            )
        own = in_ref[9].astype(BF)
        low = tile(fold_ref[wrap(p + 1)], 1)
        high = tile(fold_ref[wrap(p - 1)], 1)
        side_a = tile(fold_ref[wrap(a - 1)], 1)
        side_b = tile(fold_ref[wrap(b + 1)], 1)
        last = move(
            own,
            [
                (lambda d: d, inside(SHIFT, SHIFT + 255)),
                (lambda d: d - 264, inside(264, 265)),
                (lambda d: d - 273 + SHIFT + 256, inside(273, 274)),
            ],
        )
        last = last + move(low, [(lambda d: d - d + SHIFT + 255, inside(SHIFT - 1, SHIFT - 1))])
        last = last + move(high, [(lambda d: d - d + SHIFT, inside(SHIFT + 256, SHIFT + 256))])
        last = last + move(side_a, [(lambda d: d - d + SHIFT, inside(266, 266))])
        last = last + move(side_b, [(lambda d: d - d + SHIFT + 255, inside(272, 272))])
        in_ref[14] = last * signs

    def hidden(rows, flip):
        total = jnp.broadcast_to(b1_ref[...], (HID, PAD))
        for u in range(3):
            x = in_ref[rows + u]
            for v in range(3):
                shifted = pltpu.roll(x, (1 - v) % PAD, 1) if v != 1 else x
                total = total + jnp.dot(
                    w1_ref[u, 2 - v if flip else v], shifted.astype(BF), preferred_element_type=F32
                )
        return jnp.maximum(total, 0.0).astype(BF)

    virtual = hidden(12, True).astype(F32)
    lane = lanes((HID, PAD))
    virtual = jnp.where(
        lane == SHIFT - 1,
        pltpu.roll(virtual, (SHIFT - 1 - 265) % PAD, 1),
        jnp.where(lane == SHIFT + 256, pltpu.roll(virtual, (SHIFT + 256 - 273) % PAD, 1), virtual),
    )
    for half in range(2):
        hid = [hidden(6 * half + k, False).astype(F32) for k in range(4)]
        if half == 0:
            hid[0] = jnp.where(gy == 0, jnp.zeros_like(hid[0]), hid[0])
        else:
            hid[3] = jnp.where(gy == 7, virtual, hid[3])
        for r in range(2):
            total = jnp.broadcast_to(b2_ref[...], (OUT, PAD))
            for u in range(3):
                x = hid[r + u]
                for v in range(3):
                    shifted = pltpu.roll(x, (1 - v) % PAD, 1) if v != 1 else x
                    total = total + jnp.dot(w2_ref[u, v], shifted.astype(BF), preferred_element_type=F32)
            m = ocean_ref[6 * half + 2 + r][FLD : FLD + OUT].astype(F32)
            total = pltpu.roll(total * m, PAD - SHIFT, 1)
            res_ref[2 * half + r] = total[:, :COLS].astype(BF)
    copies = [
        pltpu.make_async_copy(res_ref.at[pl.ds(0, 2)], out_ref.at[pl.ds(0, 2)], sem.at[0]),
        pltpu.make_async_copy(res_ref.at[pl.ds(2, 2)], out_ref.at[pl.ds(ROWS - 2, 2)], sem.at[1]),
    ]
    for c in copies:
        c.start()
    for c in copies:
        c.wait()


def patch_rows(pos, fold_pair, ocean, coarse, tops, ctops, w1, b1, w2, b2, main):
    smem = pl.BlockSpec(memory_space=pltpu.SMEM)
    vmem = pl.BlockSpec(memory_space=pltpu.VMEM)
    hbm = pl.BlockSpec(memory_space=pl.ANY)
    return pl.pallas_call(
        patch_kernel,
        out_shape=jax.ShapeDtypeStruct((ROWS, OUT, COLS), BF),
        in_specs=[smem, smem] + [vmem] * 8 + [hbm],
        out_specs=hbm,
        scratch_shapes=[
            pltpu.VMEM((15, 2 * FLD, PAD), F32),
            pltpu.VMEM((4, OUT, COLS), BF),
            pltpu.SemaphoreType.DMA((2,)),
        ],
        input_output_aliases={10: 0},
        compiler_params=pltpu.CompilerParams(vmem_limit_bytes=VMEM_LIMIT),
        name="patch",
    )(pos, fold_pair, ocean, coarse, tops, ctops, w1, b1, w2, b2, main)


def shift_gx(x, step):
    n = lax.axis_size("gx")
    return lax.ppermute(x, "gx", [(i, (i + step) % n) for i in range(n)])


def shift_gy(x, step):
    n = lax.axis_size("gy")
    return lax.ppermute(x, "gy", [(i, i + step) for i in range(n) if 0 <= i + step < n])


def to_all_gx(x):
    n = lax.axis_size("gx")
    return lax.all_to_all(
        jnp.broadcast_to(x[None], (n,) + x.shape), "gx", split_axis=0, concat_axis=0, tiled=True
    )


def per_device(
    ocean, atm, dest_tile, dest_row, live, land_mask, fold_pair, w1, b1, w2, b2
):
    code = jnp.where(live == 1, dest_tile[:, 0] * 256 + dest_row, -1)
    outgoing, out_rows = pack(code, atm)
    incoming = lax.all_to_all(
        outgoing.reshape(DEV, CAP, FLD, 128), ("gy", "gx"), split_axis=0, concat_axis=0, tiled=True
    )
    in_rows = lax.all_to_all(out_rows, ("gy", "gx"), split_axis=0, concat_axis=0, tiled=True)

    w1b = jnp.zeros((3, HID, 5, 3, 2 * FLD), BF)
    for r in range(3):
        w1b = w1b.at[r, :, r : r + 3].set(w1.transpose(2, 0, 1, 3))
    w1b = w1b.reshape(192, 480)
    w1t = w1.transpose(2, 0, 1, 3).reshape(HID, 288)
    w2b = jnp.zeros((6, 3, OUT, 8, HID), BF)
    for r in range(6):
        w2b = w2b.at[r, :, :, r : r + 3].set(w2.transpose(1, 2, 0, 3))
    w2b = w2b.reshape(144, 512)
    w2l = w2[:, 0].transpose(1, 0, 2).reshape(OUT, 192)
    w2r = w2[:, 2].transpose(1, 0, 2).reshape(OUT, 192)
    b1c = jnp.tile(b1, 3)[:, None]
    b2c = b2[:, None]

    edges = edge_columns(ocean, land_mask)
    west = shift_gx(edges[2:4], 1)
    east = shift_gx(edges[0:2], -1)
    strip = jnp.concatenate([ocean[0:4], ocean[ROWS - 4 :]], axis=0)
    strip_mask = jnp.concatenate([land_mask[0:4], land_mask[ROWS - 4 :]], axis=0).astype(BF)
    strip_mask = jnp.broadcast_to(strip_mask[:, None, :], strip.shape)
    strip = jnp.concatenate([strip * strip_mask, strip_mask], axis=1)

    def beside(cols):
        picked = jnp.concatenate([cols[:, :, 0:4], cols[:, :, ROWS - 4 :]], axis=2)
        return picked.transpose(2, 1, 0)

    strip = jnp.concatenate([beside(west), strip, beside(east)], axis=2)
    strip = jnp.pad(strip, ((0, 0), (0, 0), (0, PAD - COLS - 4)))
    south = shift_gy(strip[6:8], 1)
    north = shift_gy(strip[0:2], -1)
    tops = to_all_gx(strip[6:8])
    ocean_strip = jnp.concatenate([south, strip, north], axis=0)

    coarse, ccols = coarse_sums(in_rows, incoming.reshape(DEV * CAP, FLD, 128))
    cwest = shift_gx(ccols[1], 1)
    ceast = shift_gx(ccols[0], -1)

    def pick(c):
        return jnp.concatenate([c[:, 0:2], c[:, HALF - 2 : HALF]], axis=1).T[:, :, None]

    cstrip = jnp.concatenate([coarse[0:2], coarse[HALF - 2 :]], axis=0)
    cstrip = jnp.concatenate([pick(cwest), cstrip, pick(ceast)], axis=2)
    cstrip = jnp.pad(cstrip, ((0, 0), (0, 0), (0, 126)))
    csouth = shift_gy(cstrip[3:4], 1)
    cnorth = shift_gy(cstrip[0:1], -1)
    ctops = to_all_gx(cstrip[3])
    coarse_strip = jnp.concatenate([csouth, cstrip, cnorth], axis=0)

    out = main_conv(
        ocean, land_mask, coarse, edges, west, east, ccols, cwest, ceast,
        w1b, w1t, b1c, w2b, w2l, w2r, b2c,
    )
    pos = jnp.stack([lax.axis_index("gy"), lax.axis_index("gx")]).astype(I32)
    return patch_rows(
        pos, fold_pair, ocean_strip, coarse_strip, tops, ctops, w1, b1[:, None], w2, b2c, out
    )


def solution(mesh):
    return jax.shard_map(
        per_device,
        mesh=mesh,
        in_specs=(
            P("gy", None, "gx"),
            P(("gy", "gx"), None, None),
            P(("gy", "gx"), None),
            P(("gy", "gx")),
            P(("gy", "gx")),
            P("gy", "gx"),
            P(),
            P(),
            P(),
            P(),
            P(),
        ),
        out_specs=P("gy", None, "gx"),
        check_vma=False,
    )
```

```python
import functools

import jax
import jax.numpy as jnp
from jax import lax
from jax.experimental import pallas as pl
from jax.experimental.pallas import tpu as pltpu
from jax.sharding import PartitionSpec as P

BF = jnp.bfloat16
F32 = jnp.float32
I32 = jnp.int32
VMEM_LIMIT = 56 << 20
ROWS = 384
COLS = 256
HALF = 192
DEV = 128
CAP = 3
FLD = 16
HID = 64
OUT = 8
PAD = 384
SHIFT = 2


def lanes(shape):
    return lax.broadcasted_iota(I32, shape, len(shape) - 1)


def subs(shape):
    return lax.broadcasted_iota(I32, shape, len(shape) - 2)


STEP = 2 * CAP + 1


def pack_kernel(info_ref, row_ref, atm_ref, out_ref, q_ref):
    lane = lanes((FLD, 128))
    first, last = [], []
    for chunk, count in ((0, 128), (128, 64)):

        def place(i, carry):
            c0, c1 = carry
            n = chunk + i
            code = info_ref[0, n]
            block = atm_ref[pl.ds(2 * n, 2)]
            out_ref[pl.ds(STEP * (code >> 2) + 2 * (code & 3), 2)] = block
            block = block.reshape(FLD, 128)
            here = lane == i
            c0 = jnp.where(here, pltpu.roll(block, i, 1), c0)
            c1 = jnp.where(here, pltpu.roll(block, i + 1, 1), c1)
            return c0, c1

        zero = jnp.zeros((FLD, 128), BF)
        c0, c1 = lax.fori_loop(0, count, place, (zero, zero), unroll=16)
        first.append(c0)
        last.append(c1)
    values = [jnp.concatenate(last, axis=1), jnp.concatenate(first, axis=1)]
    code = jnp.broadcast_to(row_ref[0:1, :], (DEV, 256))
    row = row_ref[1:2, :].astype(F32).astype(BF)
    total = jnp.zeros((DEV, 128), F32)
    tile = subs((DEV, 256))
    none = jnp.zeros((FLD, 256), BF)
    for k in range(CAP):
        hit = (code == 4 * tile + k).astype(BF)
        rows = jnp.where(subs((FLD, 256)) == k, jnp.broadcast_to(row, (FLD, 256)), none)
        parts = [rows] + [values[0] if i == k else none for i in range(3)]
        parts = parts + [values[1] if i == k else none for i in range(3)] + [none]
        total = total + lax.dot_general(
            hit, jnp.concatenate(parts, axis=0), (((1,), (1,)), ((), ())), preferred_element_type=F32
        )
    q_ref[...] = total
    sub = subs((8, 128))

    def head(t, carry):
        near = (t & -16) + ((t + 15) & 15)
        far = (t & -16) + ((t + 1) & 15)
        own, west, east = [
            jnp.broadcast_to(q_ref[pl.ds(i, 1), :], (8, 128)) for i in (t, near, far)
        ]
        out_ref[STEP * t + STEP - 1] = jnp.where(sub == 0, own, jnp.where(sub == 1, west, east)).astype(BF)
        return carry

    lax.fori_loop(0, DEV, head, 0, unroll=16)


def pack(info, atm):
    return pl.pallas_call(
        pack_kernel,
        out_shape=jax.ShapeDtypeStruct((DEV * STEP, 8, 128), BF),
        in_specs=[
            pl.BlockSpec(memory_space=pltpu.SMEM),
            pl.BlockSpec(memory_space=pltpu.VMEM),
            pl.BlockSpec(memory_space=pltpu.VMEM),
        ],
        out_specs=pl.BlockSpec(memory_space=pltpu.VMEM),
        scratch_shapes=[pltpu.VMEM((DEV, 128), F32)],
        name="pack",
    )(info, info, atm)


def coarse_kernel(
    inc_ref, strip_ref, out_ref, cols_ref, west_ref, east_ref, low_ref, mid_ref, top_ref, tops_ref,
    acc_ref, head_ref, idx_ref, where_ref, sem,
):
    few = lanes((8, 128)) < CAP
    for g in range(4):

        def gather(s, total):
            head = inc_ref[STEP * (32 * g + s) + STEP - 1].astype(F32)
            head_ref[32 * g + s] = head
            return total + pltpu.roll(jnp.where(few, head, 0.0), 4 * s, 1)

        idx_ref[g] = lax.fori_loop(0, 32, gather, jnp.zeros((8, 128), F32), unroll=32).astype(I32)
    copy = pltpu.make_async_copy(idx_ref, where_ref, sem)
    copy.start()
    acc_ref[...] = jnp.zeros_like(acc_ref)
    copy.wait()
    for g in range(4):

        def add(s, carry):
            for k in range(CAP):
                r = where_ref[g, 0, 4 * s + k]
                block = inc_ref[pl.ds(STEP * (32 * g + s) + 2 * k, 2)]
                acc_ref[k, r] = acc_ref[k, r] + block.astype(F32)
            return carry

        lax.fori_loop(0, 32, add, 0, unroll=8)
    lane = lanes((FLD, 128))

    def finish(r, carry):
        total = acc_ref[0, r + 1] + acc_ref[1, r + 1] + acc_ref[2, r + 1]
        out_ref[r] = total.reshape(FLD, 128).astype(BF)
        return carry

    lax.fori_loop(0, HALF, finish, 0, unroll=16)
    target = (lanes((DEV, 256)) + 1).astype(F32)
    for j, wanted in (
        (0, ((4 * FLD, cols_ref.at[0]), (FLD, cols_ref.at[1]))),
        (1, ((FLD, west_ref),)),
        (2, ((4 * FLD, east_ref),)),
    ):
        heads = head_ref[:, j, :]
        turned = heads.T.astype(BF)
        hits = [
            (jnp.broadcast_to(heads[:, k : k + 1], (DEV, 256)) == target).astype(BF) for k in range(CAP)
        ]
        for first, ref in wanted:
            total = jnp.zeros((FLD, 256), F32)
            for k in range(CAP):
                at = first + FLD * k
                total = total + jnp.dot(turned[at : at + FLD], hits[k], preferred_element_type=F32)
            ref[...] = total.astype(BF)
    spread = (subs((256, PAD)) == lanes((256, PAD)) // 2).astype(BF)
    for k, r in enumerate((0, 1, HALF - 2, HALF - 1)):
        chunk, i = (r // 128) * 128, r % 128
        west = pltpu.roll(west_ref[:, chunk : chunk + 128].astype(F32), (128 - i) % 128, 1)
        east = pltpu.roll(east_ref[:, chunk : chunk + 128].astype(F32), (129 - i) % 128, 1)
        row = pltpu.roll(out_ref[r].astype(F32), 1, 1)
        wide = jnp.concatenate(
            [
                jnp.where(lane == 0, west, row),
                jnp.where(lane == 0, row, jnp.where(lane == 1, east, 0.0)),
            ],
            axis=1,
        ).astype(BF)
        fine = jnp.dot(wide, spread, preferred_element_type=F32).astype(BF)
        for h in range(2):
            n = 2 * k + h
            ref, at = ((low_ref, n), (mid_ref, n - 2), (mid_ref, n - 2), (top_ref, n - 6))[k]
            ref[at, 0:FLD, :] = strip_ref[n, 0:FLD, :]
            ref[at, FLD : 2 * FLD, :] = fine * strip_ref[n, FLD : 2 * FLD, :]
    for h in range(2):
        row = pltpu.roll(top_ref[h].astype(F32), PAD - SHIFT, 1)[:, :COLS].astype(BF)
        for t in range(16):
            tops_ref[t, h] = row


def coarse_sums(incoming, strip):
    return pl.pallas_call(
        coarse_kernel,
        out_shape=(
            jax.ShapeDtypeStruct((HALF, FLD, 128), BF),
            jax.ShapeDtypeStruct((2, FLD, 256), BF),
            jax.ShapeDtypeStruct((FLD, 256), BF),
            jax.ShapeDtypeStruct((FLD, 256), BF),
            jax.ShapeDtypeStruct((2, 2 * FLD, PAD), BF),
            jax.ShapeDtypeStruct((4, 2 * FLD, PAD), BF),
            jax.ShapeDtypeStruct((2, 2 * FLD, PAD), BF),
            jax.ShapeDtypeStruct((16, 2, 2 * FLD, COLS), BF),
        ),
        scratch_shapes=[
            pltpu.VMEM((CAP, HALF + 1, 2, 8, 128), F32),
            pltpu.VMEM((DEV, 8, 128), F32),
            pltpu.VMEM((4, 8, 128), I32),
            pltpu.SMEM((4, 8, 128), I32),
            pltpu.SemaphoreType.DMA,
        ],
        compiler_params=pltpu.CompilerParams(vmem_limit_bytes=24 << 20),
        name="coarse",
    )(incoming, strip)


def edge_kernel(ocean_ref, mask_ref, out_ref):
    lane = lanes((FLD, 128))
    for chunk in range(3):
        block = mask_ref[chunk * 128 : chunk * 128 + 128, :].astype(F32)
        m_left = block[:, :128].T
        m_right = block[:, 128:].T

        def take(i, carry):
            x = ocean_ref[chunk * 128 + i]
            left, right = x[:, :128], x[:, 128:]
            here = lane == i
            c0, c1, c2, c3 = carry
            c0 = jnp.where(here, pltpu.roll(left, i, 1), c0)
            c1 = jnp.where(here, pltpu.roll(left, i + 127, 1), c1)
            c2 = jnp.where(here, pltpu.roll(right, i + 2, 1), c2)
            c3 = jnp.where(here, pltpu.roll(right, i + 1, 1), c3)
            return c0, c1, c2, c3

        zero = jnp.zeros((FLD, 128), BF)
        got = lax.fori_loop(0, 128, take, (zero,) * 4, unroll=16)
        rows = (m_left[0:1], m_left[1:2], m_right[126:127], m_right[127:128])
        for k in range(4):
            m = jnp.broadcast_to(rows[k], (FLD, 128)).astype(BF)
            out_ref[k, :, chunk * 128 : chunk * 128 + 128] = jnp.concatenate([got[k] * m, m], axis=0)


def edge_columns(ocean, mask):
    return pl.pallas_call(
        edge_kernel,
        out_shape=jax.ShapeDtypeStruct((4, 2 * FLD, ROWS), BF),
        compiler_params=pltpu.CompilerParams(vmem_limit_bytes=24 << 20),
        name="edges",
    )(ocean, mask)


BLOCKS = 16


def banded(w_ref, dst_ref, first):
    dst_ref[...] = jnp.zeros_like(dst_ref)
    for r in range(3):
        for u in range(3):
            for v in range(3):
                at = ((r + u) * 3 + v) * FLD
                dst_ref[r * HID : r * HID + HID, at : at + FLD] = w_ref[u, v, :, first : first + FLD]


def ocean_kernel(
    ocean_ref, mask_ref, west_ref, east_ref, w_ref, b_ref, part_ref, m3_ref, strip_ref,
    xs_ref, h_ref, band_ref, sem,
):
    banded(w_ref, band_ref, 0)
    bias = jnp.concatenate([b_ref[...]] * 3, axis=0)
    lane = lanes((128, 128))
    for chunk in range(3):
        at = slice(chunk * 128, chunk * 128 + 128)
        m = mask_ref[at, :].astype(F32)
        up, down = pltpu.roll(m, 1, 1), pltpu.roll(m, COLS - 1, 1)
        west = jnp.broadcast_to(west_ref[1, FLD : FLD + 1, at].astype(F32), (128, 128)).T
        east = jnp.broadcast_to(east_ref[0, FLD : FLD + 1, at].astype(F32), (128, 128)).T
        m3_ref[0, at, 0:128] = jnp.where(lane == 0, west, up[:, :128])
        m3_ref[0, at, 128:256] = up[:, 128:]
        m3_ref[1, at, :] = m
        m3_ref[2, at, 0:128] = down[:, :128]
        m3_ref[2, at, 128:256] = jnp.where(lane == 127, east, down[:, 128:])

    lane16 = lanes((FLD, 128))
    zero = jnp.zeros((48, COLS), BF)
    xs_ref[0] = zero
    xs_ref[ROWS + 1] = zero

    def build(y):
        base = pl.multiple_of((y // 128) * 128, 128)
        i = y % 128
        m = jnp.broadcast_to(m3_ref[1, pl.ds(y, 1), :], (FLD, COLS)).astype(BF)
        x = ocean_ref[y] * m
        west = pltpu.roll(west_ref[1, 0:FLD, pl.ds(base, 128)], 128 - i, 1)
        east = pltpu.roll(east_ref[0, 0:FLD, pl.ds(base, 128)], 127 - i, 1)
        up, down = pltpu.roll(x, 1, 1), pltpu.roll(x, COLS - 1, 1)
        xs_ref[y + 1, 0:16, 0:128] = jnp.where(lane16 == 0, west, up[:, :128])
        xs_ref[y + 1, 0:16, 128:256] = up[:, 128:]
        xs_ref[y + 1, 16:32, :] = x
        xs_ref[y + 1, 32:48, 0:128] = down[:, :128]
        xs_ref[y + 1, 32:48, 128:256] = jnp.where(lane16 == 127, east, down[:, 128:])

    wide_lane = lanes((2 * FLD, 128))
    for n, y in enumerate((0, 1, 2, 3, ROWS - 4, ROWS - 3, ROWS - 2, ROWS - 1)):
        base, i = (y // 128) * 128, y % 128
        m = jnp.broadcast_to(m3_ref[1, y : y + 1, :], (FLD, COLS))
        x = jnp.concatenate([ocean_ref[y].astype(F32) * m, m], axis=0)
        x = jnp.concatenate([x, jnp.zeros((2 * FLD, 128), F32)], axis=1)
        x = pltpu.roll(x, SHIFT, 1)

        def beside(ref, k, lane_at):
            return pltpu.roll(ref[k, :, base : base + 128].astype(F32), (128 + lane_at - i) % 128, 1)

        lo = jnp.where(wide_lane == 0, beside(west_ref, 0, 0), x[:, 0:128])
        lo = jnp.where(wide_lane == 1, beside(west_ref, 1, 1), lo)
        hi = jnp.where(wide_lane == 2, beside(east_ref, 0, 2), x[:, 256:])
        hi = jnp.where(wide_lane == 3, beside(east_ref, 1, 3), hi)
        strip_ref[n, :, 0:128] = lo.astype(BF)
        strip_ref[n, :, 128:256] = x[:, 128:256].astype(BF)
        strip_ref[n, :, 256:384] = hi.astype(BF)

    def first(i, carry):
        build(i)
        return carry

    lax.fori_loop(0, 24, first, 0, unroll=8)

    def conv(block, carry):
        for k in range(8):
            g = block * 8 + k
            for r in range(3):
                build(jnp.minimum(3 * g + 24 + r, ROWS - 1))
            x = xs_ref[pl.ds(3 * g, 5)].reshape(240, COLS)
            t = jnp.dot(band_ref[...], x, preferred_element_type=F32) + bias
            h_ref[pl.ds(3 * g, 3)] = t.astype(BF).reshape(3, HID, COLS)
        at = pl.ds(block * 24, 24)
        pltpu.make_async_copy(h_ref.at[at], part_ref.at[at], sem.at[block]).start()
        return carry

    lax.fori_loop(0, BLOCKS, conv, 0)
    for block in range(BLOCKS):
        at = pl.ds(block * 24, 24)
        pltpu.make_async_copy(h_ref.at[at], part_ref.at[at], sem.at[block]).wait()


def ocean_part(ocean, mask, west, east, w1, b1):
    return pl.pallas_call(
        ocean_kernel,
        out_shape=(
            jax.ShapeDtypeStruct((ROWS, HID, COLS), BF),
            jax.ShapeDtypeStruct((3, ROWS, COLS), F32),
            jax.ShapeDtypeStruct((8, 2 * FLD, PAD), BF),
        ),
        out_specs=(
            pl.BlockSpec(memory_space=pl.ANY),
            pl.BlockSpec(memory_space=pltpu.VMEM),
            pl.BlockSpec(memory_space=pltpu.VMEM),
        ),
        scratch_shapes=[
            pltpu.VMEM((ROWS + 2, 48, COLS), BF),
            pltpu.VMEM((ROWS, HID, COLS), BF),
            pltpu.VMEM((192, 240), BF),
            pltpu.SemaphoreType.DMA((BLOCKS,)),
        ],
        compiler_params=pltpu.CompilerParams(vmem_limit_bytes=44 << 20),
        name="ocean",
    )(ocean, mask, west, east, w1, b1)


def main_kernel(
    part_ref, m3_ref, coarse_ref, own_ref, west_ref, east_ref, cown_ref, cwest_ref, ceast_ref,
    w1_ref, b1_ref, w2_ref, b2_ref, out_ref,
    cx_ref, fine_ref, p_ref, h_ref, add_ref, band1_ref, band2_ref, side1_ref, side2_ref, sem,
):
    def fetch(block):
        return pltpu.make_async_copy(
            part_ref.at[pl.ds(block * 24, 24)], p_ref.at[pl.ds(block * 24, 24)], sem.at[block]
        )

    for block in range(BLOCKS):
        fetch(block).start()

    banded(w1_ref, band1_ref, FLD)
    band2_ref[...] = jnp.zeros_like(band2_ref)
    for u in range(3):
        for v in range(3):
            w = w2_ref[u, v]
            for r in range(6):
                at = (r * 3 + v) * OUT
                band2_ref[at : at + OUT, (r + u) * HID : (r + u) * HID + HID] = w
            w1 = w1_ref[u, v]
            at = (u * 3 + v) * 2 * FLD
            side1_ref[:, at : at + 2 * FLD] = w1
        side2_ref[0, :, u * HID : u * HID + HID] = w2_ref[u, 0]
        side2_ref[1, :, u * HID : u * HID + HID] = w2_ref[u, 2]

    rep = (subs((256, ROWS)) == lanes((256, ROWS)) // 2).astype(BF)

    def column(coarse_t, strip):
        fine = jnp.dot(coarse_t, rep, preferred_element_type=F32)
        return jnp.concatenate([strip[:FLD], (fine * strip[FLD:].astype(F32)).astype(BF)], axis=0)

    w2c = column(cwest_ref[...], west_ref[0])
    w1c = column(cwest_ref[...], west_ref[1])
    o0c = column(cown_ref[0], own_ref[0])
    o255c = column(cown_ref[1], own_ref[3])
    e1c = column(ceast_ref[...], east_ref[0])
    e2c = column(ceast_ref[...], east_ref[1])
    for side, cols in ((0, (w2c, w1c, o0c)), (1, (o255c, e1c, e2c))):
        x = jnp.concatenate(cols, axis=0)
        xt = jnp.concatenate([pltpu.roll(x, 1, 1), x, pltpu.roll(x, ROWS - 1, 1)], axis=0)
        hid = jnp.dot(side1_ref[...], xt, preferred_element_type=F32)
        hid = jnp.maximum(hid + b1_ref[...], 0.0).astype(BF)
        ht = jnp.concatenate([pltpu.roll(hid, 1, 1), hid, pltpu.roll(hid, ROWS - 1, 1)], axis=0)
        add_ref[side] = jnp.dot(side2_ref[side], ht, preferred_element_type=F32)

    lane = lanes((FLD, 128))
    for chunk, count in ((0, 128), (128, 64)):

        def extend(i, carry):
            r = chunk + i
            west = pltpu.roll(cwest_ref[:, chunk : chunk + 128], 128 - i, 1)
            east = pltpu.roll(ceast_ref[:, chunk : chunk + 128], 129 - i, 1)
            cx_ref[r, :, 0:128] = coarse_ref[r]
            both = jnp.where(lane == 0, west, jnp.where(lane == 1, east, jnp.zeros_like(east)))
            cx_ref[r, :, 128:256] = both
            return carry

        lax.fori_loop(0, count, extend, 0, unroll=16)

    src, dst = subs((256, COLS)), lanes((256, COLS))
    spread = [
        (src == jnp.where(dst == 0, 128, (dst - 1) // 2)).astype(BF),
        (src == dst // 2).astype(BF),
        (src == jnp.where(dst == COLS - 1, 129, (dst + 1) // 2)).astype(BF),
    ]
    fine_ref[0] = jnp.zeros((48, COLS), BF)
    fine_ref[HALF + 1] = jnp.zeros((48, COLS), BF)

    def widen(k, carry):
        part = cx_ref[pl.ds(k * 16, 16)].reshape(256, 256)
        for v in range(3):
            fine = jnp.dot(part, spread[v], preferred_element_type=F32).astype(BF)
            fine_ref[pl.ds(k * 16 + 1, 16), 16 * v : 16 * v + 16, :] = fine.reshape(16, FLD, COLS)
        return carry

    lax.fori_loop(0, 12, widen, 0, unroll=2)

    hzero = jnp.zeros((HID, COLS), BF)
    h_ref[0] = hzero
    h_ref[ROWS + 1] = hzero

    def conv1(block):
        fetch(block).wait()
        for j in range(4):
            y0 = block * 24 + j * 6
            rows = []
            for i in range(8):
                y = y0 - 1 + i
                half = (block * 12 + j * 3) + (i + 1) // 2
                ym = y if 0 < i < 7 else jnp.clip(y, 0, ROWS - 1)
                for v in range(3):
                    m = jnp.broadcast_to(m3_ref[v, pl.ds(ym, 1), :], (FLD, COLS)).astype(BF)
                    rows.append(fine_ref[half, 16 * v : 16 * v + 16, :] * m)
            for k in range(2):
                x = jnp.concatenate(rows[9 * k : 9 * k + 15], axis=0)
                t = jnp.dot(band1_ref[...], x, preferred_element_type=F32)
                t = t + p_ref[pl.ds(y0 + 3 * k, 3)].reshape(192, COLS).astype(F32)
                h_ref[pl.ds(y0 + 3 * k + 1, 3)] = jnp.maximum(t, 0.0).astype(BF).reshape(3, HID, COLS)

    b2 = b2_ref[...]
    lane8 = lanes((OUT, 128))

    def conv2(first, count):
        for k in range(count):
            j = jnp.maximum(first + k, 0)
            x = h_ref[pl.ds(6 * j, 8)].reshape(512, COLS)
            t = jnp.dot(band2_ref[...], x, preferred_element_type=F32).reshape(6, 3, OUT, COLS)
            for r in range(6):
                y = 6 * j + r
                base = pl.multiple_of((y // 128) * 128, 128)
                i = y % 128
                west = pltpu.roll(add_ref[0, :, pl.ds(base, 128)], 128 - i, 1)
                east = pltpu.roll(add_ref[1, :, pl.ds(base, 128)], 127 - i, 1)
                up = pltpu.roll(t[r, 0], 1, 1)
                down = pltpu.roll(t[r, 2], COLS - 1, 1)
                mid = t[r, 1] + b2
                m = m3_ref[1, pl.ds(y, 1), :]
                lo = mid[:, :128] + jnp.where(lane8 == 0, west, up[:, :128]) + down[:, :128]
                hi = mid[:, 128:] + up[:, 128:] + jnp.where(lane8 == 127, east, down[:, 128:])
                out_ref[y, :, 0:128] = (lo * m[:, :128]).astype(BF)
                out_ref[y, :, 128:256] = (hi * m[:, 128:]).astype(BF)

    def both(block, carry):
        conv2(4 * block - 5, 4)
        conv1(block)
        return carry

    lax.fori_loop(0, BLOCKS, both, 0)
    conv2(4 * BLOCKS - 5, 5)


def main_conv(*args):
    vmem = pl.BlockSpec(memory_space=pltpu.VMEM)
    return pl.pallas_call(
        main_kernel,
        out_shape=jax.ShapeDtypeStruct((ROWS, OUT, COLS), BF),
        in_specs=[pl.BlockSpec(memory_space=pl.ANY)] + [vmem] * 12,
        scratch_shapes=[
            pltpu.VMEM((HALF, FLD, COLS), BF),
            pltpu.VMEM((HALF + 2, 48, COLS), BF),
            pltpu.VMEM((ROWS, HID, COLS), BF),
            pltpu.VMEM((ROWS + 2, HID, COLS), BF),
            pltpu.VMEM((2, OUT, ROWS), F32),
            pltpu.VMEM((192, 240), BF),
            pltpu.VMEM((144, 512), BF),
            pltpu.VMEM((HID, 288), BF),
            pltpu.VMEM((2, OUT, 192), BF),
            pltpu.SemaphoreType.DMA((BLOCKS,)),
        ],
        compiler_params=pltpu.CompilerParams(vmem_limit_bytes=44 << 20),
        name="convs",
    )(*args)


def onehot(pairs, rows, cols):
    src = subs((rows, cols))
    dst = lanes((rows, cols))
    hit = jnp.zeros((rows, cols), jnp.bool_)
    for source, cond in pairs:
        hit = hit | ((src == source(dst)) & cond(dst))
    return hit.astype(BF)


def patch_kernel(
    pos_ref, fold_ref, south_ref, low_ref, mid_ref, top_ref, north_ref, tops_ref, strip_ref,
    w1_ref, b1_ref, w2_ref, b2_ref, main_ref, out_ref, in_ref, res_ref, sem,
):
    gy, gx = pos_ref[0], pos_ref[1]
    signs = jnp.where(
        (subs((2 * FLD, PAD)) < 8) | (subs((2 * FLD, PAD)) == 16) | (subs((2 * FLD, PAD)) == 17), -1.0, 1.0
    )
    at = 0
    for ref, count in ((south_ref, 2), (low_ref, 2), (mid_ref, 4), (top_ref, 2), (north_ref, 2)):
        for k in range(count):
            in_ref[at] = ref[k].astype(F32)
            at += 1
    for k in range(3):
        in_ref[12 + k] = jnp.zeros((2 * FLD, PAD), F32)

    wrap = lambda t: jnp.where(t < 0, t + 16, jnp.where(t > 15, t - 16, t))
    near = wrap(gx - 1)
    far = wrap(gx + 1)
    p = fold_ref[gx]
    a = fold_ref[near]
    b = fold_ref[far]

    @pl.when(gy == 7)
    def _():
        def move(x, pairs):
            return jnp.dot(x, onehot(pairs, x.shape[1], PAD), preferred_element_type=F32)

        def inside(lo, hi):
            return lambda d: (d >= lo) & (d <= hi)

        def put(column, lane_at, step=0):
            count = 2 if step else 1
            return [(lambda d: column + step * (d - lane_at), inside(lane_at, lane_at + count - 1))]

        mirror = lambda d: SHIFT + COLS - 1 - d
        row = move(tops_ref[p, 1], [(mirror, inside(SHIFT, SHIFT + 255))])
        row = row + move(tops_ref[a, 1], put(1, 0, -1))
        row = row + move(tops_ref[b, 1], put(COLS - 1, SHIFT + COLS, -1))
        in_ref[10] = row * signs
        for k in range(2):
            in_ref[12 + k] = (
                move(tops_ref[p, k], [(mirror, inside(SHIFT, SHIFT + 255))])
                + move(tops_ref[wrap(p + 1), k], put(0, SHIFT - 1))
                + move(tops_ref[wrap(p - 1), k], put(COLS - 1, SHIFT + COLS))
                + move(tops_ref[a, k], put(1, 264, -1))
                + move(tops_ref[wrap(a - 1), k], put(COLS - 1, 266))
                + move(tops_ref[b, k], put(COLS - 1, 273, -1))
                + move(tops_ref[wrap(b + 1), k], put(0, 272))
            )
        last = move(
            in_ref[9].astype(BF),
            [(lambda d: d, inside(SHIFT, SHIFT + 255))] + put(0, 264, 1) + put(SHIFT + COLS, 273, 1),
        )
        last = last + move(tops_ref[fold_ref[wrap(p + 1)], 1], put(COLS - 1, SHIFT - 1))
        last = last + move(tops_ref[fold_ref[wrap(p - 1)], 1], put(0, SHIFT + COLS))
        last = last + move(tops_ref[fold_ref[wrap(a - 1)], 1], put(0, 266))
        last = last + move(tops_ref[fold_ref[wrap(b + 1)], 1], put(COLS - 1, 272))
        in_ref[14] = last * signs

    def hidden(rows, flip):
        total = jnp.broadcast_to(b1_ref[...], (HID, PAD))
        for u in range(3):
            x = in_ref[rows + u]
            for v in range(3):
                shifted = pltpu.roll(x, (1 - v) % PAD, 1) if v != 1 else x
                total = total + jnp.dot(
                    w1_ref[u, 2 - v if flip else v], shifted.astype(BF), preferred_element_type=F32
                )
        return jnp.maximum(total, 0.0).astype(BF)

    virtual = hidden(12, True).astype(F32)
    lane = lanes((HID, PAD))
    virtual = jnp.where(
        lane == SHIFT - 1,
        pltpu.roll(virtual, (SHIFT - 1 - 265) % PAD, 1),
        jnp.where(lane == SHIFT + 256, pltpu.roll(virtual, (SHIFT + 256 - 273) % PAD, 1), virtual),
    )
    for half in range(2):
        hid = [hidden(6 * half + k, False).astype(F32) for k in range(4)]
        if half == 0:
            hid[0] = jnp.where(gy == 0, jnp.zeros_like(hid[0]), hid[0])
        else:
            hid[3] = jnp.where(gy == 7, virtual, hid[3])
        for r in range(2):
            total = jnp.broadcast_to(b2_ref[...], (OUT, PAD))
            for u in range(3):
                x = hid[r + u]
                for v in range(3):
                    shifted = pltpu.roll(x, (1 - v) % PAD, 1) if v != 1 else x
                    total = total + jnp.dot(w2_ref[u, v], shifted.astype(BF), preferred_element_type=F32)
            m = strip_ref[6 * half + r, FLD : 2 * FLD, :].astype(F32)[:OUT]
            total = pltpu.roll(total * m, PAD - SHIFT, 1)
            res_ref[2 * half + r] = total[:, :COLS].astype(BF)
    copies = [
        pltpu.make_async_copy(res_ref.at[pl.ds(0, 2)], out_ref.at[pl.ds(0, 2)], sem.at[0]),
        pltpu.make_async_copy(res_ref.at[pl.ds(2, 2)], out_ref.at[pl.ds(ROWS - 2, 2)], sem.at[1]),
    ]
    for c in copies:
        c.start()
    for c in copies:
        c.wait()


def patch_rows(*args):
    smem = pl.BlockSpec(memory_space=pltpu.SMEM)
    vmem = pl.BlockSpec(memory_space=pltpu.VMEM)
    hbm = pl.BlockSpec(memory_space=pl.ANY)
    return pl.pallas_call(
        patch_kernel,
        out_shape=jax.ShapeDtypeStruct((ROWS, OUT, COLS), BF),
        in_specs=[smem, smem] + [vmem] * 11 + [hbm],
        out_specs=hbm,
        scratch_shapes=[
            pltpu.VMEM((15, 2 * FLD, PAD), F32),
            pltpu.VMEM((4, OUT, COLS), BF),
            pltpu.SemaphoreType.DMA((2,)),
        ],
        input_output_aliases={13: 0},
        compiler_params=pltpu.CompilerParams(vmem_limit_bytes=24 << 20),
        name="patch",
    )(*args)


def shift_gx(x, step):
    n = lax.axis_size("gx")
    return lax.ppermute(x, "gx", [(i, (i + step) % n) for i in range(n)])


def shift_gy(x, step):
    n = lax.axis_size("gy")
    return lax.ppermute(x, "gy", [(i, i + step) for i in range(n) if 0 <= i + step < n])


def per_device(
    ocean, atm, dest_tile, dest_row, live, land_mask, fold_pair, w1, b1, w2, b2
):
    edges = edge_columns(ocean, land_mask)
    west = shift_gx(edges[2:4], 1)
    east = shift_gx(edges[0:2], -1)

    tile = dest_tile[:, 0]
    same = tile[:, None] == tile[None, :]
    before = jnp.arange(HALF)[:, None] > jnp.arange(HALF)[None, :]
    rank = jnp.sum((same & before).astype(I32), axis=1)
    info = jnp.stack([tile * 4 + rank, jnp.where(live == 1, dest_row + 1, 0)])
    info = jnp.pad(info, ((0, 0), (0, 64)), constant_values=-1)
    outgoing = pack(info, atm.reshape(2 * HALF, 8, 128))
    outgoing, west, east = lax.optimization_barrier((outgoing, west, east))
    incoming = lax.all_to_all(
        outgoing.reshape(DEV, STEP, 8, 128), ("gy", "gx"), split_axis=0, concat_axis=0, tiled=True
    )
    b1c = b1[:, None]
    b2c = b2[:, None]
    part, m3, strip = ocean_part(ocean, land_mask, west, east, w1, b1c)

    coarse, ccols, cwest, ceast, low, mid, top, tops = coarse_sums(
        incoming.reshape(DEV * STEP, 8, 128), strip
    )
    south = shift_gy(top, 1)
    north = shift_gy(low, -1)
    tops = lax.all_to_all(tops, "gx", split_axis=0, concat_axis=0, tiled=True)
    out = main_conv(
        part, m3, coarse, edges, west, east, ccols, cwest, ceast, w1, b1c, w2, b2c,
    )
    pos = jnp.stack([lax.axis_index("gy"), lax.axis_index("gx")]).astype(I32)
    return patch_rows(
        pos, fold_pair, south, low, mid, top, north, tops, strip, w1, b1c, w2, b2c, out
    )


def solution(mesh):
    return jax.shard_map(
        per_device,
        mesh=mesh,
        in_specs=(
            P("gy", None, "gx"),
            P(("gy", "gx"), None, None),
            P(("gy", "gx"), None),
            P(("gy", "gx")),
            P(("gy", "gx")),
            P("gy", "gx"),
            P(),
            P(),
            P(),
            P(),
            P(),
        ),
        out_specs=P("gy", None, "gx"),
        check_vma=False,
    )
```

```python
import functools

import jax
import jax.numpy as jnp
from jax import lax
from jax.experimental import pallas as pl
from jax.experimental.pallas import tpu as pltpu
from jax.sharding import PartitionSpec as P

BF = jnp.bfloat16
F32 = jnp.float32
I32 = jnp.int32
VMEM_LIMIT = 56 << 20
ROWS = 384
COLS = 256
HALF = 192
DEV = 128
CAP = 3
FLD = 16
HID = 64
OUT = 8
PAD = 384
SHIFT = 2


def lanes(shape):
    return lax.broadcasted_iota(I32, shape, len(shape) - 1)


def subs(shape):
    return lax.broadcasted_iota(I32, shape, len(shape) - 2)


STEP = 2 * CAP + 1


def pack_kernel(tile_ref, row_ref, live_ref, atm_ref, out_ref, q_ref, code_ref, info_ref, sem):
    across = jnp.concatenate([tile_ref[...].astype(F32), jnp.full((1, 64), -1.0, F32)], axis=1)
    column = jnp.broadcast_to(across, (128, 256))
    column = jnp.concatenate([column[:, :128].T, column[:, 128:].T[:64]], axis=0)
    earlier = (subs((HALF, 256)) < lanes((HALF, 256))) & (
        jnp.concatenate([column, column], axis=1) == jnp.broadcast_to(across, (HALF, 256))
    )
    code = 4.0 * across + jnp.sum(earlier.astype(F32), axis=0, keepdims=True)
    code_ref[...] = code.astype(I32)
    copy = pltpu.make_async_copy(code_ref, info_ref, sem)
    copy.start()
    copy.wait()
    lane = lanes((FLD, 128))
    first, last = [], []
    for chunk, count in ((0, 128), (128, 64)):

        def place(i, carry):
            c0, c1 = carry
            n = chunk + i
            code = info_ref[0, n]
            block = atm_ref[pl.ds(2 * n, 2)]
            out_ref[pl.ds(STEP * (code >> 2) + 2 * (code & 3), 2)] = block
            block = block.reshape(FLD, 128)
            here = lane == i
            c0 = jnp.where(here, pltpu.roll(block, i, 1), c0)
            c1 = jnp.where(here, pltpu.roll(block, i + 1, 1), c1)
            return c0, c1

        zero = jnp.zeros((FLD, 128), BF)
        c0, c1 = lax.fori_loop(0, count, place, (zero, zero), unroll=16)
        first.append(c0)
        last.append(c1)
    values = [jnp.concatenate(last, axis=1), jnp.concatenate(first, axis=1)]
    code = jnp.broadcast_to(code_ref[...], (DEV, 256))
    row = jnp.where(live_ref[...] == 1, row_ref[...] + 1, 0).astype(F32)
    row = jnp.concatenate([row, jnp.zeros((1, 64), F32)], axis=1).astype(BF)
    total = jnp.zeros((DEV, 128), F32)
    tile = subs((DEV, 256))
    none = jnp.zeros((FLD, 256), BF)
    for k in range(CAP):
        hit = (code == 4 * tile + k).astype(BF)
        rows = jnp.where(subs((FLD, 256)) == k, jnp.broadcast_to(row, (FLD, 256)), none)
        parts = [rows] + [values[0] if i == k else none for i in range(3)]
        parts = parts + [values[1] if i == k else none for i in range(3)] + [none]
        total = total + lax.dot_general(
            hit, jnp.concatenate(parts, axis=0), (((1,), (1,)), ((), ())), preferred_element_type=F32
        )
    q_ref[...] = total
    sub = subs((8, 128))

    def head(t, carry):
        near = (t & -16) + ((t + 15) & 15)
        far = (t & -16) + ((t + 1) & 15)
        own, west, east = [
            jnp.broadcast_to(q_ref[pl.ds(i, 1), :], (8, 128)) for i in (t, near, far)
        ]
        out_ref[STEP * t + STEP - 1] = jnp.where(sub == 0, own, jnp.where(sub == 1, west, east)).astype(BF)
        return carry

    lax.fori_loop(0, DEV, head, 0, unroll=16)


def pack(tile, row, live, atm):
    return pl.pallas_call(
        pack_kernel,
        out_shape=jax.ShapeDtypeStruct((DEV * STEP, 8, 128), BF),
        scratch_shapes=[
            pltpu.VMEM((DEV, 128), F32),
            pltpu.VMEM((1, 256), I32),
            pltpu.SMEM((1, 256), I32),
            pltpu.SemaphoreType.DMA,
        ],
        name="pack",
    )(tile, row, live, atm)


def coarse_kernel(
    inc_ref, strip_ref, out_ref, cols_ref, west_ref, east_ref, low_ref, mid_ref, top_ref, tops_ref,
    acc_ref, head_ref, idx_ref, where_ref, sem,
):
    few = lanes((8, 128)) < CAP
    for g in range(4):

        def gather(s, total):
            head = inc_ref[STEP * (32 * g + s) + STEP - 1].astype(F32)
            head_ref[32 * g + s] = head
            return total + pltpu.roll(jnp.where(few, head, 0.0), 4 * s, 1)

        idx_ref[g] = lax.fori_loop(0, 32, gather, jnp.zeros((8, 128), F32), unroll=32).astype(I32)
    copy = pltpu.make_async_copy(idx_ref, where_ref, sem)
    copy.start()
    acc_ref[...] = jnp.zeros_like(acc_ref)
    copy.wait()
    for g in range(4):

        def add(s, carry):
            for k in range(CAP):
                r = where_ref[g, 0, 4 * s + k]
                block = inc_ref[pl.ds(STEP * (32 * g + s) + 2 * k, 2)]
                acc_ref[k, r] = acc_ref[k, r] + block.astype(F32)
            return carry

        lax.fori_loop(0, 32, add, 0, unroll=8)
    lane = lanes((FLD, 128))

    def finish(r, carry):
        total = acc_ref[0, r + 1] + acc_ref[1, r + 1] + acc_ref[2, r + 1]
        out_ref[r] = total.reshape(FLD, 128).astype(BF)
        return carry

    lax.fori_loop(0, HALF, finish, 0, unroll=16)
    target = (lanes((DEV, 256)) + 1).astype(F32)
    for j, wanted in (
        (0, ((4 * FLD, cols_ref.at[0]), (FLD, cols_ref.at[1]))),
        (1, ((FLD, west_ref),)),
        (2, ((4 * FLD, east_ref),)),
    ):
        heads = head_ref[:, j, :]
        turned = heads.T.astype(BF)
        hits = [
            (jnp.broadcast_to(heads[:, k : k + 1], (DEV, 256)) == target).astype(BF) for k in range(CAP)
        ]
        for first, ref in wanted:
            total = jnp.zeros((FLD, 256), F32)
            for k in range(CAP):
                at = first + FLD * k
                total = total + jnp.dot(turned[at : at + FLD], hits[k], preferred_element_type=F32)
            ref[...] = total.astype(BF)
    spread = (subs((256, PAD)) == lanes((256, PAD)) // 2).astype(BF)
    for k, r in enumerate((0, 1, HALF - 2, HALF - 1)):
        chunk, i = (r // 128) * 128, r % 128
        west = pltpu.roll(west_ref[:, chunk : chunk + 128].astype(F32), (128 - i) % 128, 1)
        east = pltpu.roll(east_ref[:, chunk : chunk + 128].astype(F32), (129 - i) % 128, 1)
        row = pltpu.roll(out_ref[r].astype(F32), 1, 1)
        wide = jnp.concatenate(
            [
                jnp.where(lane == 0, west, row),
                jnp.where(lane == 0, row, jnp.where(lane == 1, east, 0.0)),
            ],
            axis=1,
        ).astype(BF)
        fine = jnp.dot(wide, spread, preferred_element_type=F32).astype(BF)
        for h in range(2):
            n = 2 * k + h
            ref, at = ((low_ref, n), (mid_ref, n - 2), (mid_ref, n - 2), (top_ref, n - 6))[k]
            ref[at, 0:FLD, :] = strip_ref[n, 0:FLD, :]
            ref[at, FLD : 2 * FLD, :] = fine * strip_ref[n, FLD : 2 * FLD, :]
    for h in range(2):
        row = pltpu.roll(top_ref[h].astype(F32), PAD - SHIFT, 1)[:, :COLS].astype(BF)
        for t in range(16):
            tops_ref[t, h] = row


def coarse_sums(incoming, strip):
    return pl.pallas_call(
        coarse_kernel,
        out_shape=(
            jax.ShapeDtypeStruct((HALF, FLD, 128), BF),
            jax.ShapeDtypeStruct((2, FLD, 256), BF),
            jax.ShapeDtypeStruct((FLD, 256), BF),
            jax.ShapeDtypeStruct((FLD, 256), BF),
            jax.ShapeDtypeStruct((2, 2 * FLD, PAD), BF),
            jax.ShapeDtypeStruct((4, 2 * FLD, PAD), BF),
            jax.ShapeDtypeStruct((2, 2 * FLD, PAD), BF),
            jax.ShapeDtypeStruct((16, 2, 2 * FLD, COLS), BF),
        ),
        scratch_shapes=[
            pltpu.VMEM((CAP, HALF + 1, 2, 8, 128), F32),
            pltpu.VMEM((DEV, 8, 128), F32),
            pltpu.VMEM((4, 8, 128), I32),
            pltpu.SMEM((4, 8, 128), I32),
            pltpu.SemaphoreType.DMA,
        ],
        compiler_params=pltpu.CompilerParams(vmem_limit_bytes=12 << 20),
        name="coarse",
    )(incoming, strip)


def edge_kernel(ocean_ref, mask_ref, first_ref, last_ref):
    lane = lanes((FLD, 128))
    for chunk in range(3):
        block = mask_ref[chunk * 128 : chunk * 128 + 128, :].astype(F32)
        m_left = block[:, :128].T
        m_right = block[:, 128:].T

        def take(i, carry):
            x = ocean_ref[chunk * 128 + i]
            left, right = x[:, :128], x[:, 128:]
            here = lane == i
            c0, c1, c2, c3 = carry
            c0 = jnp.where(here, pltpu.roll(left, i, 1), c0)
            c1 = jnp.where(here, pltpu.roll(left, i + 127, 1), c1)
            c2 = jnp.where(here, pltpu.roll(right, i + 2, 1), c2)
            c3 = jnp.where(here, pltpu.roll(right, i + 1, 1), c3)
            return c0, c1, c2, c3

        zero = jnp.zeros((FLD, 128), BF)
        got = lax.fori_loop(0, 128, take, (zero,) * 4, unroll=16)
        rows = (m_left[0:1], m_left[1:2], m_right[126:127], m_right[127:128])
        for k in range(4):
            m = jnp.broadcast_to(rows[k], (FLD, 128)).astype(BF)
            ref = last_ref if k >= 2 else first_ref
            ref[k % 2, :, chunk * 128 : chunk * 128 + 128] = jnp.concatenate([got[k] * m, m], axis=0)


def edge_columns(ocean, mask):
    return pl.pallas_call(
        edge_kernel,
        out_shape=(jax.ShapeDtypeStruct((2, 2 * FLD, ROWS), BF),) * 2,
        compiler_params=pltpu.CompilerParams(vmem_limit_bytes=24 << 20),
        name="edges",
    )(ocean, mask)


BLOCKS = 16


def banded(w_ref, dst_ref, first):
    dst_ref[...] = jnp.zeros_like(dst_ref)
    for r in range(3):
        for u in range(3):
            for v in range(3):
                at = ((r + u) * 3 + v) * FLD
                dst_ref[r * HID : r * HID + HID, at : at + FLD] = w_ref[u, v, :, first : first + FLD]


def ocean_kernel(
    ocean_ref, mask_ref, wt_ref, b1_ref, b2_ref, part_ref, strip_ref, w_ref, b1c_ref, b2c_ref, xs_ref, band_ref, h_ref, sem,
):
    for u in range(3):
        for v in range(3):
            w_ref[u, v] = wt_ref[u, v].astype(F32).T.astype(BF)
    b1c_ref[...] = jnp.broadcast_to(b1_ref[...], (128, HID)).T
    b2c_ref[...] = jnp.broadcast_to(b2_ref[...], (128, OUT)).T
    banded(w_ref, band_ref, 0)
    bias = jnp.concatenate([b1c_ref[:, 0:1]] * 3, axis=0)
    lane16 = lanes((FLD, 128))
    zero = jnp.zeros((48, COLS), BF)
    xs_ref[0] = zero
    xs_ref[ROWS + 1] = zero
    nothing = jnp.zeros((FLD, 128), BF)

    def build(y):
        m = jnp.broadcast_to(mask_ref[pl.ds(y, 1), :].astype(F32), (FLD, COLS)).astype(BF)
        x = ocean_ref[y] * m
        up, down = pltpu.roll(x, 1, 1), pltpu.roll(x, COLS - 1, 1)
        xs_ref[y + 1, 0:16, 0:128] = jnp.where(lane16 == 0, nothing, up[:, :128])
        xs_ref[y + 1, 0:16, 128:256] = up[:, 128:]
        xs_ref[y + 1, 16:32, :] = x
        xs_ref[y + 1, 32:48, 0:128] = down[:, :128]
        xs_ref[y + 1, 32:48, 128:256] = jnp.where(lane16 == 127, nothing, down[:, 128:])

    for n, y in enumerate((0, 1, 2, 3, ROWS - 4, ROWS - 3, ROWS - 2, ROWS - 1)):
        m = jnp.broadcast_to(mask_ref[y : y + 1, :].astype(F32), (FLD, COLS))
        x = jnp.concatenate([ocean_ref[y].astype(F32) * m, m], axis=0)
        x = jnp.concatenate([x, jnp.zeros((2 * FLD, 128), F32)], axis=1)
        strip_ref[n] = pltpu.roll(x, SHIFT, 1).astype(BF)

    def first(i, carry):
        build(i)
        return carry

    lax.fori_loop(0, 24, first, 0, unroll=8)

    def conv(block, carry):
        for k in range(8):
            g = block * 8 + k
            for r in range(3):
                build(jnp.minimum(3 * g + 24 + r, ROWS - 1))
            x = xs_ref[pl.ds(3 * g, 5)].reshape(240, COLS)
            t = jnp.dot(band_ref[...], x, preferred_element_type=F32) + bias
            h_ref[pl.ds(3 * g, 3)] = t.astype(BF).reshape(3, HID, COLS)
        at = pl.ds(block * 24, 24)
        pltpu.make_async_copy(h_ref.at[at], part_ref.at[at], sem.at[block]).start()
        return carry

    lax.fori_loop(0, BLOCKS, conv, 0)
    for block in range(BLOCKS):
        at = pl.ds(block * 24, 24)
        pltpu.make_async_copy(h_ref.at[at], part_ref.at[at], sem.at[block]).wait()


def ocean_part(*args):
    return pl.pallas_call(
        ocean_kernel,
        out_shape=(
            jax.ShapeDtypeStruct((ROWS, HID, COLS), BF),
            jax.ShapeDtypeStruct((8, 2 * FLD, PAD), BF),
            jax.ShapeDtypeStruct((3, 3, HID, 2 * FLD), BF),
            jax.ShapeDtypeStruct((HID, 128), F32),
            jax.ShapeDtypeStruct((OUT, 128), F32),
        ),
        out_specs=(pl.BlockSpec(memory_space=pl.ANY),) + (pl.BlockSpec(memory_space=pltpu.VMEM),) * 4,
        scratch_shapes=[
            pltpu.VMEM((ROWS + 2, 48, COLS), BF),
            pltpu.VMEM((192, 240), BF),
            pltpu.VMEM((ROWS, HID, COLS), BF),
            pltpu.SemaphoreType.DMA((BLOCKS,)),
        ],
        compiler_params=pltpu.CompilerParams(vmem_limit_bytes=40 << 20),
        name="ocean",
    )(*args)


def margin_kernel(mask_ref, west_ref, east_ref, rows_ref, m3_ref, strip_ref):
    lane = lanes((128, 128))
    for chunk in range(3):
        at = slice(chunk * 128, chunk * 128 + 128)
        m = mask_ref[at, :].astype(F32)
        up, down = pltpu.roll(m, 1, 1), pltpu.roll(m, COLS - 1, 1)
        west = jnp.broadcast_to(west_ref[1, FLD : FLD + 1, at].astype(F32), (128, 128)).T
        east = jnp.broadcast_to(east_ref[0, FLD : FLD + 1, at].astype(F32), (128, 128)).T
        m3_ref[0, at, 0:128] = jnp.where(lane == 0, west, up[:, :128])
        m3_ref[0, at, 128:256] = up[:, 128:]
        m3_ref[1, at, :] = m
        m3_ref[2, at, 0:128] = down[:, :128]
        m3_ref[2, at, 128:256] = jnp.where(lane == 127, east, down[:, 128:])
    wide_lane = lanes((2 * FLD, 128))
    for n, y in enumerate((0, 1, 2, 3, ROWS - 4, ROWS - 3, ROWS - 2, ROWS - 1)):
        base, i = (y // 128) * 128, y % 128
        x = rows_ref[n].astype(F32)

        def beside(ref, k, lane_at):
            return pltpu.roll(ref[k, :, base : base + 128].astype(F32), (128 + lane_at - i) % 128, 1)

        lo = jnp.where(wide_lane == 0, beside(west_ref, 0, 0), x[:, 0:128])
        lo = jnp.where(wide_lane == 1, beside(west_ref, 1, 1), lo)
        hi = jnp.where(wide_lane == 2, beside(east_ref, 0, 2), x[:, 256:])
        hi = jnp.where(wide_lane == 3, beside(east_ref, 1, 3), hi)
        strip_ref[n, :, 0:128] = lo.astype(BF)
        strip_ref[n, :, 128:256] = x[:, 128:256].astype(BF)
        strip_ref[n, :, 256:384] = hi.astype(BF)

def margins(*args):
    return pl.pallas_call(
        margin_kernel,
        out_shape=(
            jax.ShapeDtypeStruct((3, ROWS, COLS), F32),
            jax.ShapeDtypeStruct((8, 2 * FLD, PAD), BF),
        ),
        compiler_params=pltpu.CompilerParams(vmem_limit_bytes=24 << 20),
        name="margins",
    )(*args)


def main_kernel(
    part_ref, m3_ref, coarse_ref, first_ref, last_ref, west_ref, east_ref, cown_ref, cwest_ref, ceast_ref,
    w1_ref, b1_ref, w2_ref, b2_ref, out_ref,
    cx_ref, fine_ref, p_ref, h_ref, add_ref, band1_ref, band2_ref, side1_ref, side2_ref, pair_ref, sem,
):
    def fetch(block):
        at = pl.ds(block * 24, 24)
        return pltpu.make_async_copy(part_ref.at[at], p_ref.at[at], sem.at[block])

    for block in range(BLOCKS):
        fetch(block).start()

    banded(w1_ref, band1_ref, FLD)
    band2_ref[...] = jnp.zeros_like(band2_ref)
    for u in range(3):
        for v in range(3):
            w = w2_ref[u, v]
            for r in range(6):
                at = (r * 3 + v) * OUT
                band2_ref[at : at + OUT, (r + u) * HID : (r + u) * HID + HID] = w
            w1 = w1_ref[u, v]
            at = (u * 3 + v) * 2 * FLD
            side1_ref[:, at : at + 2 * FLD] = w1
        for side in range(2):
            at = u * HID
            side2_ref[side, 0:OUT, at : at + HID] = w2_ref[u, 2 * side]
            side2_ref[side, OUT : 2 * OUT, at : at + HID] = jnp.zeros((OUT, HID), BF)
            at = (3 + u) * HID
            side2_ref[side, 0:OUT, at : at + HID] = w2_ref[u, 1]
            side2_ref[side, OUT : 2 * OUT, at : at + HID] = w2_ref[u, 2 * side]

    rep = (subs((256, ROWS)) == lanes((256, ROWS)) // 2).astype(BF)

    def column(coarse_t, strip):
        fine = jnp.dot(coarse_t, rep, preferred_element_type=F32)
        return jnp.concatenate([strip[:FLD], (fine * strip[FLD:].astype(F32)).astype(BF)], axis=0)

    w2c = column(cwest_ref[...], west_ref[0])
    w1c = column(cwest_ref[...], west_ref[1])
    o0c = column(cown_ref[0], first_ref[0])
    o1c = column(cown_ref[0], first_ref[1])
    o254c = column(cown_ref[1], last_ref[0])
    o255c = column(cown_ref[1], last_ref[1])
    e1c = column(ceast_ref[...], east_ref[0])
    e2c = column(ceast_ref[...], east_ref[1])

    def around(x):
        return jnp.concatenate([pltpu.roll(x, 1, 1), x, pltpu.roll(x, ROWS - 1, 1)], axis=0)

    ends = []
    for side, outer, inner in (
        (0, (w2c, w1c, o0c), (w1c, o0c, o1c)),
        (1, (o255c, e1c, e2c), (o254c, o255c, e1c)),
    ):
        hidden = []
        for cols in (outer, inner):
            xt = around(jnp.concatenate(cols, axis=0))
            hid = jnp.dot(side1_ref[...], xt, preferred_element_type=F32)
            hidden.append(around(jnp.maximum(hid + b1_ref[:, 0:1], 0.0).astype(BF)))
        ends.append(jnp.dot(side2_ref[side], jnp.concatenate(hidden, axis=0), preferred_element_type=F32))
    phase = lanes((OUT, 128)) & 3
    for chunk in range(3):
        at = slice(chunk * 128, chunk * 128 + 128)
        c0 = ends[0][0:OUT, at]
        c1 = pltpu.roll(ends[0][OUT:, at], 1, 1)
        c254 = pltpu.roll(ends[1][OUT:, at], 126, 1)
        c255 = pltpu.roll(ends[1][0:OUT, at], 127, 1)
        for q in range(4):
            z = jnp.where(phase == q, c0, jnp.where(phase == (q + 1) % 4, c1, c255))
            add_ref[q, chunk] = jnp.where(phase == (q + 2) % 4, c254, z)

    lane = lanes((FLD, 128))
    for chunk, count in ((0, 128), (128, 64)):
        west = cwest_ref[:, chunk : chunk + 128]
        east = pltpu.roll(ceast_ref[:, chunk : chunk + 128], 1, 1)
        for q in range(2):
            pair_ref[q] = jnp.where((lane & 1) == q, west, east)

        def extend(i, carry):
            r = chunk + i
            cx_ref[r, :, 0:128] = coarse_ref[r]
            cx_ref[r, :, 128:256] = pltpu.roll(pair_ref[i & 1], 128 - i, 1)
            return carry

        lax.fori_loop(0, count, extend, 0, unroll=16)

    src, dst = subs((256, COLS)), lanes((256, COLS))
    spread = [
        (src == jnp.where(dst == 0, 128, (dst - 1) // 2)).astype(BF),
        (src == dst // 2).astype(BF),
        (src == jnp.where(dst == COLS - 1, 129, (dst + 1) // 2)).astype(BF),
    ]
    fine_ref[0] = jnp.zeros((48, COLS), BF)
    fine_ref[HALF + 1] = jnp.zeros((48, COLS), BF)

    def widen(k, carry):
        part = cx_ref[pl.ds(k * 16, 16)].reshape(256, 256)
        for v in range(3):
            fine = jnp.dot(part, spread[v], preferred_element_type=F32).astype(BF)
            fine_ref[pl.ds(k * 16 + 1, 16), 16 * v : 16 * v + 16, :] = fine.reshape(16, FLD, COLS)
        return carry

    lax.fori_loop(0, 12, widen, 0, unroll=2)

    hzero = jnp.zeros((HID, COLS), BF)
    h_ref[0] = hzero
    h_ref[ROWS + 1] = hzero

    def conv1(block, carry):
        fetch(block).wait()
        for j in range(4):
            y0 = block * 24 + j * 6
            rows = []
            for i in range(8):
                y = y0 - 1 + i
                half = (block * 12 + j * 3) + (i + 1) // 2
                ym = y if 0 < i < 7 else jnp.clip(y, 0, ROWS - 1)
                for v in range(3):
                    m = jnp.broadcast_to(m3_ref[v, pl.ds(ym, 1), :], (FLD, COLS)).astype(BF)
                    rows.append(fine_ref[half, 16 * v : 16 * v + 16, :] * m)
            for k in range(2):
                x = jnp.concatenate(rows[9 * k : 9 * k + 15], axis=0)
                t = jnp.dot(band1_ref[...], x, preferred_element_type=F32)
                t = t + p_ref[pl.ds(y0 + 3 * k, 3)].reshape(192, COLS).astype(F32)
                h_ref[pl.ds(y0 + 3 * k + 1, 3)] = jnp.maximum(t, 0.0).astype(BF).reshape(3, HID, COLS)
        return carry

    lax.fori_loop(0, BLOCKS, conv1, 0)

    b2 = b2_ref[:, 0:1]
    lane8 = lanes((OUT, 128))

    def conv2(block, carry):
        for k in range(8):
            j = block * 8 + k
            x = h_ref[pl.ds(6 * j, 8)].reshape(512, COLS)
            t = jnp.dot(band2_ref[...], x, preferred_element_type=F32).reshape(6, 3, OUT, COLS)
            for r in range(6):
                y = 6 * j + r
                ends = pltpu.roll(add_ref[y & 3, y >> 7], 128 - (y & 127), 1)
                up = pltpu.roll(t[r, 0], 1, 1)
                down = pltpu.roll(t[r, 2], COLS - 1, 1)
                m = m3_ref[1, pl.ds(y, 1), :]
                lo = jnp.where(lane8 == 0, 0.0, t[r, 1, :, :128]) + b2
                lo = lo + jnp.where(lane8 < 2, ends, up[:, :128]) + down[:, :128]
                hi = jnp.where(lane8 == 127, 0.0, t[r, 1, :, 128:]) + b2
                hi = hi + up[:, 128:] + jnp.where(lane8 > 125, ends, down[:, 128:])
                out_ref[y, :, 0:128] = (lo * m[:, :128]).astype(BF)
                out_ref[y, :, 128:256] = (hi * m[:, 128:]).astype(BF)

        return carry

    lax.fori_loop(0, 8, conv2, 0)


def main_conv(*args):
    vmem = pl.BlockSpec(memory_space=pltpu.VMEM)
    return pl.pallas_call(
        main_kernel,
        out_shape=jax.ShapeDtypeStruct((ROWS, OUT, COLS), BF),
        in_specs=[pl.BlockSpec(memory_space=pl.ANY)] + [vmem] * 13,
        scratch_shapes=[
            pltpu.VMEM((HALF, FLD, COLS), BF),
            pltpu.VMEM((HALF + 2, 48, COLS), BF),
            pltpu.VMEM((ROWS, HID, COLS), BF),
            pltpu.VMEM((ROWS + 2, HID, COLS), BF),
            pltpu.VMEM((4, 3, OUT, 128), F32),
            pltpu.VMEM((192, 240), BF),
            pltpu.VMEM((144, 512), BF),
            pltpu.VMEM((HID, 288), BF),
            pltpu.VMEM((2, 2 * OUT, 384), BF),
            pltpu.VMEM((2, FLD, 128), BF),
            pltpu.SemaphoreType.DMA((BLOCKS,)),
        ],
        compiler_params=pltpu.CompilerParams(vmem_limit_bytes=44 << 20),
        name="convs",
    )(*args)


def onehot(pairs, rows, cols):
    src = subs((rows, cols))
    dst = lanes((rows, cols))
    hit = jnp.zeros((rows, cols), jnp.bool_)
    for source, cond in pairs:
        hit = hit | ((src == source(dst)) & cond(dst))
    return hit.astype(BF)


def patch_kernel(
    fold_ref, south_ref, low_ref, mid_ref, top_ref, north_ref, tops_ref, strip_ref,
    w1_ref, b1_ref, w2_ref, b2_ref, main_ref, out_ref, in_ref, res_ref, sem,
):
    gy, gx = lax.axis_index("gy"), lax.axis_index("gx")
    signs = jnp.where(
        (subs((2 * FLD, PAD)) < 8) | (subs((2 * FLD, PAD)) == 16) | (subs((2 * FLD, PAD)) == 17), -1.0, 1.0
    )
    at = 0
    for ref, count in ((south_ref, 2), (low_ref, 2), (mid_ref, 4), (top_ref, 2), (north_ref, 2)):
        for k in range(count):
            in_ref[at] = ref[k].astype(F32)
            at += 1
    for k in range(3):
        in_ref[12 + k] = jnp.zeros((2 * FLD, PAD), F32)

    wrap = lambda t: jnp.where(t < 0, t + 16, jnp.where(t > 15, t - 16, t))
    near = wrap(gx - 1)
    far = wrap(gx + 1)
    p = fold_ref[gx]
    a = fold_ref[near]
    b = fold_ref[far]

    @pl.when(gy == 7)
    def _():
        def move(x, pairs):
            return jnp.dot(x, onehot(pairs, x.shape[1], PAD), preferred_element_type=F32)

        def inside(lo, hi):
            return lambda d: (d >= lo) & (d <= hi)

        def put(column, lane_at, step=0):
            count = 2 if step else 1
            return [(lambda d: column + step * (d - lane_at), inside(lane_at, lane_at + count - 1))]

        mirror = lambda d: SHIFT + COLS - 1 - d
        row = move(tops_ref[p, 1], [(mirror, inside(SHIFT, SHIFT + 255))])
        row = row + move(tops_ref[a, 1], put(1, 0, -1))
        row = row + move(tops_ref[b, 1], put(COLS - 1, SHIFT + COLS, -1))
        in_ref[10] = row * signs
        for k in range(2):
            in_ref[12 + k] = (
                move(tops_ref[p, k], [(mirror, inside(SHIFT, SHIFT + 255))])
                + move(tops_ref[wrap(p + 1), k], put(0, SHIFT - 1))
                + move(tops_ref[wrap(p - 1), k], put(COLS - 1, SHIFT + COLS))
                + move(tops_ref[a, k], put(1, 264, -1))
                + move(tops_ref[wrap(a - 1), k], put(COLS - 1, 266))
                + move(tops_ref[b, k], put(COLS - 1, 273, -1))
                + move(tops_ref[wrap(b + 1), k], put(0, 272))
            )
        last = move(
            in_ref[9].astype(BF),
            [(lambda d: d, inside(SHIFT, SHIFT + 255))] + put(0, 264, 1) + put(SHIFT + COLS, 273, 1),
        )
        last = last + move(tops_ref[fold_ref[wrap(p + 1)], 1], put(COLS - 1, SHIFT - 1))
        last = last + move(tops_ref[fold_ref[wrap(p - 1)], 1], put(0, SHIFT + COLS))
        last = last + move(tops_ref[fold_ref[wrap(a - 1)], 1], put(0, 266))
        last = last + move(tops_ref[fold_ref[wrap(b + 1)], 1], put(COLS - 1, 272))
        in_ref[14] = last * signs

    def hidden(rows, flip):
        total = jnp.broadcast_to(b1_ref[:, 0:1], (HID, PAD))
        for u in range(3):
            x = in_ref[rows + u]
            for v in range(3):
                shifted = pltpu.roll(x, (1 - v) % PAD, 1) if v != 1 else x
                total = total + jnp.dot(
                    w1_ref[u, 2 - v if flip else v], shifted.astype(BF), preferred_element_type=F32
                )
        return jnp.maximum(total, 0.0).astype(BF)

    virtual = hidden(12, True).astype(F32)
    lane = lanes((HID, PAD))
    virtual = jnp.where(
        lane == SHIFT - 1,
        pltpu.roll(virtual, (SHIFT - 1 - 265) % PAD, 1),
        jnp.where(lane == SHIFT + 256, pltpu.roll(virtual, (SHIFT + 256 - 273) % PAD, 1), virtual),
    )
    for half in range(2):
        hid = [hidden(6 * half + k, False).astype(F32) for k in range(4)]
        if half == 0:
            hid[0] = jnp.where(gy == 0, jnp.zeros_like(hid[0]), hid[0])
        else:
            hid[3] = jnp.where(gy == 7, virtual, hid[3])
        for r in range(2):
            total = jnp.broadcast_to(b2_ref[:, 0:1], (OUT, PAD))
            for u in range(3):
                x = hid[r + u]
                for v in range(3):
                    shifted = pltpu.roll(x, (1 - v) % PAD, 1) if v != 1 else x
                    total = total + jnp.dot(w2_ref[u, v], shifted.astype(BF), preferred_element_type=F32)
            m = strip_ref[6 * half + r, FLD : 2 * FLD, :].astype(F32)[:OUT]
            total = pltpu.roll(total * m, PAD - SHIFT, 1)
            res_ref[2 * half + r] = total[:, :COLS].astype(BF)
    copies = [
        pltpu.make_async_copy(res_ref.at[pl.ds(0, 2)], out_ref.at[pl.ds(0, 2)], sem.at[0]),
        pltpu.make_async_copy(res_ref.at[pl.ds(2, 2)], out_ref.at[pl.ds(ROWS - 2, 2)], sem.at[1]),
    ]
    for c in copies:
        c.start()
    for c in copies:
        c.wait()


def patch_rows(*args):
    smem = pl.BlockSpec(memory_space=pltpu.SMEM)
    vmem = pl.BlockSpec(memory_space=pltpu.VMEM)
    hbm = pl.BlockSpec(memory_space=pl.ANY)
    return pl.pallas_call(
        patch_kernel,
        out_shape=jax.ShapeDtypeStruct((ROWS, OUT, COLS), BF),
        in_specs=[smem] + [vmem] * 11 + [hbm],
        out_specs=hbm,
        scratch_shapes=[
            pltpu.VMEM((15, 2 * FLD, PAD), F32),
            pltpu.VMEM((4, OUT, COLS), BF),
            pltpu.SemaphoreType.DMA((2,)),
        ],
        input_output_aliases={12: 0},
        compiler_params=pltpu.CompilerParams(vmem_limit_bytes=24 << 20),
        name="patch",
    )(*args)


def shift_gx(x, step):
    n = lax.axis_size("gx")
    return lax.ppermute(x, "gx", [(i, (i + step) % n) for i in range(n)])


def shift_gy(x, step):
    n = lax.axis_size("gy")
    return lax.ppermute(x, "gy", [(i, i + step) for i in range(n) if 0 <= i + step < n])


def per_device(
    ocean, atm, dest_tile, dest_row, live, land_mask, fold_pair, w1, b1, w2, b2
):
    outgoing = pack(
        dest_tile.reshape(1, HALF), dest_row.reshape(1, HALF), live.reshape(1, HALF), atm.reshape(2 * HALF, 8, 128)
    )
    incoming = lax.all_to_all(
        outgoing.reshape(DEV, STEP, 8, 128), ("gy", "gx"), split_axis=0, concat_axis=0, tiled=True
    )
    ocean, land_mask, _ = lax.optimization_barrier((ocean, land_mask, outgoing))
    first, last = edge_columns(ocean, land_mask)
    west = shift_gx(last, 1)
    east = shift_gx(first, -1)
    part, rows, w1, b1c, b2c = ocean_part(
        ocean, land_mask, w1.swapaxes(2, 3), b1.reshape(1, HID), b2.reshape(1, OUT)
    )
    m3, strip = margins(land_mask, west, east, rows)

    coarse, ccols, cwest, ceast, low, mid, top, tops = coarse_sums(
        incoming.reshape(DEV * STEP, 8, 128), strip
    )
    south = shift_gy(top, 1)
    north = shift_gy(low, -1)
    tops = lax.all_to_all(tops, "gx", split_axis=0, concat_axis=0, tiled=True)
    out = main_conv(
        part, m3, coarse, first, last, west, east, ccols, cwest, ceast, w1, b1c, w2, b2c,
    )
    return patch_rows(
        fold_pair, south, low, mid, top, north, tops, strip, w1, b1c, w2, b2c, out
    )


def solution(mesh):
    return jax.shard_map(
        per_device,
        mesh=mesh,
        in_specs=(
            P("gy", None, "gx"),
            P(("gy", "gx"), None, None),
            P(("gy", "gx"), None),
            P(("gy", "gx")),
            P(("gy", "gx")),
            P("gy", "gx"),
            P(),
            P(),
            P(),
            P(),
            P(),
        ),
        out_specs=P("gy", None, "gx"),
        check_vma=False,
    )
```

```python
import functools

import jax
import jax.numpy as jnp
from jax import lax
from jax.experimental import pallas as pl
from jax.experimental.pallas import tpu as pltpu
from jax.sharding import PartitionSpec as P

BF = jnp.bfloat16
F32 = jnp.float32
I32 = jnp.int32
VMEM_LIMIT = 56 << 20
ROWS = 384
COLS = 256
HALF = 192
DEV = 128
CAP = 3
FLD = 16
HID = 64
OUT = 8
PAD = 384
SHIFT = 2


def lanes(shape):
    return lax.broadcasted_iota(I32, shape, len(shape) - 1)


def subs(shape):
    return lax.broadcasted_iota(I32, shape, len(shape) - 2)


STEP = 2 * CAP + 1


PIECES = 8


def pack_kernel(
    tile_ref, row_ref, live_ref, atm_hbm, out_hbm, atm_ref, out_ref, q_ref, code_ref, info_ref,
    sem, in_sem, out_sem,
):
    loads, stores = [], []
    for c in range(PIECES):
        at = pl.ds(c * (2 * HALF // PIECES), 2 * HALF // PIECES)
        loads.append(pltpu.make_async_copy(atm_hbm.at[at], atm_ref.at[at], in_sem.at[c]))
        at = pl.ds(c * (DEV * STEP // PIECES), DEV * STEP // PIECES)
        stores.append(pltpu.make_async_copy(out_ref.at[at], out_hbm.at[at], out_sem.at[c]))
        loads[c].start()
    across = jnp.concatenate([tile_ref[...].astype(F32), jnp.full((1, 64), -1.0, F32)], axis=1)
    column = jnp.broadcast_to(across, (128, 256))
    column = jnp.concatenate([column[:, :128].T, column[:, 128:].T[:64]], axis=0)
    earlier = (subs((HALF, 256)) < lanes((HALF, 256))) & (
        jnp.concatenate([column, column], axis=1) == jnp.broadcast_to(across, (HALF, 256))
    )
    code = 4.0 * across + jnp.sum(earlier.astype(F32), axis=0, keepdims=True)
    code_ref[...] = code.astype(I32)
    copy = pltpu.make_async_copy(code_ref, info_ref, sem)
    copy.start()
    for load in loads:
        load.wait()
    lane = lanes((FLD, 128))
    first, last = [], []
    for chunk, count in ((0, 128), (128, 64)):

        def ends(i, carry):
            c0, c1 = carry
            block = atm_ref[pl.ds(2 * (chunk + i), 2)].reshape(FLD, 128)
            here = lane == i
            c0 = jnp.where(here, pltpu.roll(block, i, 1), c0)
            c1 = jnp.where(here, pltpu.roll(block, i + 1, 1), c1)
            return c0, c1

        zero = jnp.zeros((FLD, 128), BF)
        c0, c1 = lax.fori_loop(0, count, ends, (zero, zero), unroll=32)
        first.append(c0)
        last.append(c1)
    values = [jnp.concatenate(last, axis=1), jnp.concatenate(first, axis=1)]
    code = jnp.broadcast_to(code_ref[...], (DEV, 256))
    row = jnp.where(live_ref[...] == 1, row_ref[...] + 1, 0).astype(F32)
    row = jnp.concatenate([row, jnp.zeros((1, 64), F32)], axis=1).astype(BF)
    total = jnp.zeros((DEV, 128), F32)
    tile = subs((DEV, 256))
    none = jnp.zeros((FLD, 256), BF)
    for k in range(CAP):
        hit = (code == 4 * tile + k).astype(BF)
        rows = jnp.where(subs((FLD, 256)) == k, jnp.broadcast_to(row, (FLD, 256)), none)
        parts = [rows] + [values[0] if i == k else none for i in range(3)]
        parts = parts + [values[1] if i == k else none for i in range(3)] + [none]
        total = total + lax.dot_general(
            hit, jnp.concatenate(parts, axis=0), (((1,), (1,)), ((), ())), preferred_element_type=F32
        )
    q_ref[...] = total
    copy.wait()

    def place(n, carry):
        code = info_ref[0, n]
        out_ref[pl.ds(STEP * (code >> 2) + 2 * (code & 3), 2)] = atm_ref[pl.ds(2 * n, 2)]
        return carry

    lax.fori_loop(0, HALF, place, 0, unroll=32)
    sub = subs((8, 128))
    for c in range(PIECES):
        for t in range(c * DEV // PIECES, (c + 1) * DEV // PIECES):
            near = (t & -16) + ((t + 15) & 15)
            far = (t & -16) + ((t + 1) & 15)
            own, west, east = [
                jnp.broadcast_to(q_ref[i : i + 1, :], (8, 128)) for i in (t, near, far)
            ]
            head = jnp.where(sub == 0, own, jnp.where(sub == 1, west, east))
            out_ref[STEP * t + STEP - 1] = head.astype(BF)
        stores[c].start()
    for store in stores:
        store.wait()


def pack(tile, row, live, atm):
    vmem = pl.BlockSpec(memory_space=pltpu.VMEM)
    hbm = pl.BlockSpec(memory_space=pl.ANY)
    return pl.pallas_call(
        pack_kernel,
        out_shape=jax.ShapeDtypeStruct((DEV * STEP, 8, 128), BF),
        in_specs=[vmem, vmem, vmem, hbm],
        out_specs=hbm,
        scratch_shapes=[
            pltpu.VMEM((2 * HALF, 8, 128), BF),
            pltpu.VMEM((DEV * STEP, 8, 128), BF),
            pltpu.VMEM((DEV, 128), F32),
            pltpu.VMEM((1, 256), I32),
            pltpu.SMEM((1, 256), I32),
            pltpu.SemaphoreType.DMA,
            pltpu.SemaphoreType.DMA((PIECES,)),
            pltpu.SemaphoreType.DMA((PIECES,)),
        ],
        compiler_params=pltpu.CompilerParams(vmem_limit_bytes=56 << 20),
        name="pack",
    )(tile, row, live, atm)


def coarse_kernel(
    inc_hbm, strip_ref, out_ref, cols_ref, west_ref, east_ref, low_ref, mid_ref, top_ref, tops_ref,
    inc_ref, raw_ref, acc_ref, head_ref, idx_ref, where_ref, sem, raw_sem, in_sem,
):
    raw = pltpu.make_async_copy(inc_hbm.at[:, STEP - 1], raw_ref, raw_sem)
    raw.start()
    loads = []
    for c in range(PIECES):
        at = pl.ds(c * DEV // PIECES, DEV // PIECES)
        loads.append(pltpu.make_async_copy(inc_hbm.at[at], inc_ref.at[at], in_sem.at[c]))
        loads[c].start()
    acc_ref[...] = jnp.zeros_like(acc_ref)
    raw.wait()
    few = lanes((8, 128)) < CAP
    for g in range(4):

        def gather(s, total):
            head = raw_ref[32 * g + s].astype(F32)
            head_ref[32 * g + s] = head
            return total + pltpu.roll(jnp.where(few, head, 0.0), 4 * s, 1)

        idx_ref[g] = lax.fori_loop(0, 32, gather, jnp.zeros((8, 128), F32), unroll=32).astype(I32)
    copy = pltpu.make_async_copy(idx_ref, where_ref, sem)
    copy.start()
    target = (subs((256, DEV)) + 1).astype(F32)
    for j, wanted in (
        (0, ((4 * FLD, cols_ref.at[0]), (FLD, cols_ref.at[1]))),
        (1, ((FLD, west_ref),)),
        (2, ((4 * FLD, east_ref),)),
    ):
        turned = head_ref[:, j, :].T
        values = turned.astype(BF)
        hits = jnp.concatenate(
            [
                (jnp.broadcast_to(turned[k : k + 1], (256, DEV)) == target).astype(BF)
                for k in range(CAP)
            ],
            axis=1,
        )
        blocks = jnp.concatenate(
            [
                jnp.concatenate([values[at + FLD * k : at + FLD * k + FLD] for k in range(CAP)], axis=1)
                for at, _ in wanted
            ],
            axis=0,
        )
        total = lax.dot_general(blocks, hits, (((1,), (1,)), ((), ())), preferred_element_type=F32)
        for n, (_, ref) in enumerate(wanted):
            ref[...] = total[n * FLD : n * FLD + FLD].astype(BF)
    copy.wait()
    for c in range(PIECES):
        loads[c].wait()
        count = DEV // PIECES

        def add(i, carry):
            for k in range(CAP):
                r = where_ref[c * count // 32, 0, 4 * (c * count % 32 + i) + k]
                block = inc_ref[c * count + i, 2 * k : 2 * k + 2]
                acc_ref[k, r] = acc_ref[k, r] + block.astype(F32)
            return carry

        lax.fori_loop(0, count, add, 0, unroll=16)
    lane = lanes((FLD, 128))

    def finish(r, carry):
        total = acc_ref[0, r + 1] + acc_ref[1, r + 1] + acc_ref[2, r + 1]
        out_ref[r] = total.reshape(FLD, 128).astype(BF)
        return carry

    lax.fori_loop(0, HALF, finish, 0, unroll=16)
    spread = (subs((256, PAD)) == lanes((256, PAD)) // 2).astype(BF)
    for k, r in enumerate((0, 1, HALF - 2, HALF - 1)):
        chunk, i = (r // 128) * 128, r % 128
        west = pltpu.roll(west_ref[:, chunk : chunk + 128].astype(F32), (128 - i) % 128, 1)
        east = pltpu.roll(east_ref[:, chunk : chunk + 128].astype(F32), (129 - i) % 128, 1)
        row = pltpu.roll(out_ref[r].astype(F32), 1, 1)
        wide = jnp.concatenate(
            [
                jnp.where(lane == 0, west, row),
                jnp.where(lane == 0, row, jnp.where(lane == 1, east, 0.0)),
            ],
            axis=1,
        ).astype(BF)
        fine = jnp.dot(wide, spread, preferred_element_type=F32).astype(BF)
        for h in range(2):
            n = 2 * k + h
            ref, at = ((low_ref, n), (mid_ref, n - 2), (mid_ref, n - 2), (top_ref, n - 6))[k]
            ref[at, 0:FLD, :] = strip_ref[n, 0:FLD, :]
            ref[at, FLD : 2 * FLD, :] = fine * strip_ref[n, FLD : 2 * FLD, :]
    for h in range(2):
        row = pltpu.roll(top_ref[h].astype(F32), PAD - SHIFT, 1)[:, :COLS].astype(BF)
        for t in range(16):
            tops_ref[t, h] = row


def coarse_sums(incoming, strip):
    return pl.pallas_call(
        coarse_kernel,
        out_shape=(
            jax.ShapeDtypeStruct((HALF, FLD, 128), BF),
            jax.ShapeDtypeStruct((2, FLD, 256), BF),
            jax.ShapeDtypeStruct((FLD, 256), BF),
            jax.ShapeDtypeStruct((FLD, 256), BF),
            jax.ShapeDtypeStruct((2, 2 * FLD, PAD), BF),
            jax.ShapeDtypeStruct((4, 2 * FLD, PAD), BF),
            jax.ShapeDtypeStruct((2, 2 * FLD, PAD), BF),
            jax.ShapeDtypeStruct((16, 2, 2 * FLD, COLS), BF),
        ),
        in_specs=[pl.BlockSpec(memory_space=pl.ANY), pl.BlockSpec(memory_space=pltpu.VMEM)],
        scratch_shapes=[
            pltpu.VMEM((DEV, STEP, 8, 128), BF),
            pltpu.VMEM((DEV, 8, 128), BF),
            pltpu.VMEM((CAP, HALF + 1, 2, 8, 128), F32),
            pltpu.VMEM((DEV, 8, 128), F32),
            pltpu.VMEM((4, 8, 128), I32),
            pltpu.SMEM((4, 8, 128), I32),
            pltpu.SemaphoreType.DMA,
            pltpu.SemaphoreType.DMA,
            pltpu.SemaphoreType.DMA((PIECES,)),
        ],
        compiler_params=pltpu.CompilerParams(vmem_limit_bytes=20 << 20),
        name="coarse",
    )(incoming, strip)


def edge_kernel(ocean_ref, mask_ref, first_ref, last_ref):
    lane = lanes((FLD, 128))
    for chunk in range(3):
        block = mask_ref[chunk * 128 : chunk * 128 + 128, :].astype(F32)
        m_left = block[:, :128].T
        m_right = block[:, 128:].T

        def take(i, carry):
            x = ocean_ref[chunk * 128 + i]
            left, right = x[:, :128], x[:, 128:]
            here = lane == i
            c0, c1, c2, c3 = carry
            c0 = jnp.where(here, pltpu.roll(left, i, 1), c0)
            c1 = jnp.where(here, pltpu.roll(left, i + 127, 1), c1)
            c2 = jnp.where(here, pltpu.roll(right, i + 2, 1), c2)
            c3 = jnp.where(here, pltpu.roll(right, i + 1, 1), c3)
            return c0, c1, c2, c3

        zero = jnp.zeros((FLD, 128), BF)
        got = lax.fori_loop(0, 128, take, (zero,) * 4, unroll=16)
        rows = (m_left[0:1], m_left[1:2], m_right[126:127], m_right[127:128])
        for k in range(4):
            m = jnp.broadcast_to(rows[k], (FLD, 128)).astype(BF)
            ref = last_ref if k >= 2 else first_ref
            ref[k % 2, :, chunk * 128 : chunk * 128 + 128] = jnp.concatenate([got[k] * m, m], axis=0)


def edge_columns(ocean, mask):
    return pl.pallas_call(
        edge_kernel,
        out_shape=(jax.ShapeDtypeStruct((2, 2 * FLD, ROWS), BF),) * 2,
        compiler_params=pltpu.CompilerParams(vmem_limit_bytes=24 << 20),
        name="edges",
    )(ocean, mask)


BLOCKS = 16


def banded(w_ref, dst_ref, first):
    dst_ref[...] = jnp.zeros_like(dst_ref)
    for r in range(3):
        for u in range(3):
            for v in range(3):
                at = ((r + u) * 3 + v) * FLD
                dst_ref[r * HID : r * HID + HID, at : at + FLD] = w_ref[u, v, :, first : first + FLD]


def ocean_kernel(
    ocean_ref, mask_ref, wt_ref, b1_ref, b2_ref, part_ref, strip_ref, w_ref, b1c_ref, b2c_ref, xs_ref, band_ref, h_ref, sem,
):
    for u in range(3):
        for v in range(3):
            w_ref[u, v] = wt_ref[u, v].astype(F32).T.astype(BF)
    b1c_ref[...] = jnp.broadcast_to(b1_ref[...], (128, HID)).T
    b2c_ref[...] = jnp.broadcast_to(b2_ref[...], (128, OUT)).T
    banded(w_ref, band_ref, 0)
    bias = jnp.concatenate([b1c_ref[:, 0:1]] * 3, axis=0)
    lane16 = lanes((FLD, 128))
    zero = jnp.zeros((48, COLS), BF)
    xs_ref[0] = zero
    xs_ref[ROWS + 1] = zero
    nothing = jnp.zeros((FLD, 128), BF)

    def build(y):
        m = jnp.broadcast_to(mask_ref[pl.ds(y, 1), :].astype(F32), (FLD, COLS)).astype(BF)
        x = ocean_ref[y] * m
        up, down = pltpu.roll(x, 1, 1), pltpu.roll(x, COLS - 1, 1)
        xs_ref[y + 1, 0:16, 0:128] = jnp.where(lane16 == 0, nothing, up[:, :128])
        xs_ref[y + 1, 0:16, 128:256] = up[:, 128:]
        xs_ref[y + 1, 16:32, :] = x
        xs_ref[y + 1, 32:48, 0:128] = down[:, :128]
        xs_ref[y + 1, 32:48, 128:256] = jnp.where(lane16 == 127, nothing, down[:, 128:])

    for n, y in enumerate((0, 1, 2, 3, ROWS - 4, ROWS - 3, ROWS - 2, ROWS - 1)):
        m = jnp.broadcast_to(mask_ref[y : y + 1, :].astype(F32), (FLD, COLS))
        x = jnp.concatenate([ocean_ref[y].astype(F32) * m, m], axis=0)
        x = jnp.concatenate([x, jnp.zeros((2 * FLD, 128), F32)], axis=1)
        strip_ref[n] = pltpu.roll(x, SHIFT, 1).astype(BF)

    def first(i, carry):
        build(i)
        return carry

    lax.fori_loop(0, 24, first, 0, unroll=8)

    def conv(block, carry):
        for k in range(8):
            g = block * 8 + k
            for r in range(3):
                build(jnp.minimum(3 * g + 24 + r, ROWS - 1))
            x = xs_ref[pl.ds(3 * g, 5)].reshape(240, COLS)
            t = jnp.dot(band_ref[...], x, preferred_element_type=F32) + bias
            h_ref[pl.ds(3 * g, 3)] = t.astype(BF).reshape(3, HID, COLS)
        at = pl.ds(block * 24, 24)
        pltpu.make_async_copy(h_ref.at[at], part_ref.at[at], sem.at[block]).start()
        return carry

    lax.fori_loop(0, BLOCKS, conv, 0)
    for block in range(BLOCKS):
        at = pl.ds(block * 24, 24)
        pltpu.make_async_copy(h_ref.at[at], part_ref.at[at], sem.at[block]).wait()


def ocean_part(*args):
    return pl.pallas_call(
        ocean_kernel,
        out_shape=(
            jax.ShapeDtypeStruct((ROWS, HID, COLS), BF),
            jax.ShapeDtypeStruct((8, 2 * FLD, PAD), BF),
            jax.ShapeDtypeStruct((3, 3, HID, 2 * FLD), BF),
            jax.ShapeDtypeStruct((HID, 128), F32),
            jax.ShapeDtypeStruct((OUT, 128), F32),
        ),
        out_specs=(pl.BlockSpec(memory_space=pl.ANY),) + (pl.BlockSpec(memory_space=pltpu.VMEM),) * 4,
        scratch_shapes=[
            pltpu.VMEM((ROWS + 2, 48, COLS), BF),
            pltpu.VMEM((192, 240), BF),
            pltpu.VMEM((ROWS, HID, COLS), BF),
            pltpu.SemaphoreType.DMA((BLOCKS,)),
        ],
        compiler_params=pltpu.CompilerParams(vmem_limit_bytes=40 << 20),
        name="ocean",
    )(*args)


def margin_kernel(mask_ref, west_ref, east_ref, rows_ref, m3_ref, strip_ref):
    lane = lanes((128, 128))
    for chunk in range(3):
        at = slice(chunk * 128, chunk * 128 + 128)
        m = mask_ref[at, :].astype(F32)
        up, down = pltpu.roll(m, 1, 1), pltpu.roll(m, COLS - 1, 1)
        west = jnp.broadcast_to(west_ref[1, FLD : FLD + 1, at].astype(F32), (128, 128)).T
        east = jnp.broadcast_to(east_ref[0, FLD : FLD + 1, at].astype(F32), (128, 128)).T
        m3_ref[0, at, 0:128] = jnp.where(lane == 0, west, up[:, :128])
        m3_ref[0, at, 128:256] = up[:, 128:]
        m3_ref[1, at, :] = m
        m3_ref[2, at, 0:128] = down[:, :128]
        m3_ref[2, at, 128:256] = jnp.where(lane == 127, east, down[:, 128:])
    wide_lane = lanes((2 * FLD, 128))
    for n, y in enumerate((0, 1, 2, 3, ROWS - 4, ROWS - 3, ROWS - 2, ROWS - 1)):
        base, i = (y // 128) * 128, y % 128
        x = rows_ref[n].astype(F32)

        def beside(ref, k, lane_at):
            return pltpu.roll(ref[k, :, base : base + 128].astype(F32), (128 + lane_at - i) % 128, 1)

        lo = jnp.where(wide_lane == 0, beside(west_ref, 0, 0), x[:, 0:128])
        lo = jnp.where(wide_lane == 1, beside(west_ref, 1, 1), lo)
        hi = jnp.where(wide_lane == 2, beside(east_ref, 0, 2), x[:, 256:])
        hi = jnp.where(wide_lane == 3, beside(east_ref, 1, 3), hi)
        strip_ref[n, :, 0:128] = lo.astype(BF)
        strip_ref[n, :, 128:256] = x[:, 128:256].astype(BF)
        strip_ref[n, :, 256:384] = hi.astype(BF)

def margins(*args):
    return pl.pallas_call(
        margin_kernel,
        out_shape=(
            jax.ShapeDtypeStruct((3, ROWS, COLS), F32),
            jax.ShapeDtypeStruct((8, 2 * FLD, PAD), BF),
        ),
        compiler_params=pltpu.CompilerParams(vmem_limit_bytes=24 << 20),
        name="margins",
    )(*args)


def main_kernel(
    part_ref, m3_ref, coarse_ref, first_ref, last_ref, west_ref, east_ref, cown_ref, cwest_ref, ceast_ref,
    w1_ref, b1_ref, w2_ref, b2_ref, out_ref,
    fine_ref, p_ref, h_ref, add_ref, band1_ref, band2_ref, side1_ref, side2_ref, pair_ref, sem,
):
    def fetch(block):
        at = pl.ds(block * 24, 24)
        return pltpu.make_async_copy(part_ref.at[at], p_ref.at[at], sem.at[block])

    for block in range(BLOCKS):
        fetch(block).start()

    banded(w1_ref, band1_ref, FLD)
    band2_ref[...] = jnp.zeros_like(band2_ref)
    for u in range(3):
        for v in range(3):
            w = w2_ref[u, v]
            for r in range(6):
                at = (r * 3 + v) * OUT
                band2_ref[at : at + OUT, (r + u) * HID : (r + u) * HID + HID] = w
            w1 = w1_ref[u, v]
            at = (u * 3 + v) * 2 * FLD
            side1_ref[:, at : at + 2 * FLD] = w1
        for side in range(2):
            at = u * HID
            side2_ref[side, 0:OUT, at : at + HID] = w2_ref[u, 2 * side]
            side2_ref[side, OUT : 2 * OUT, at : at + HID] = jnp.zeros((OUT, HID), BF)
            at = (3 + u) * HID
            side2_ref[side, 0:OUT, at : at + HID] = w2_ref[u, 1]
            side2_ref[side, OUT : 2 * OUT, at : at + HID] = w2_ref[u, 2 * side]

    rep = (subs((256, ROWS)) == lanes((256, ROWS)) // 2).astype(BF)

    def column(coarse_t, strip):
        fine = jnp.dot(coarse_t, rep, preferred_element_type=F32)
        return jnp.concatenate([strip[:FLD], (fine * strip[FLD:].astype(F32)).astype(BF)], axis=0)

    w2c = column(cwest_ref[...], west_ref[0])
    w1c = column(cwest_ref[...], west_ref[1])
    o0c = column(cown_ref[0], first_ref[0])
    o1c = column(cown_ref[0], first_ref[1])
    o254c = column(cown_ref[1], last_ref[0])
    o255c = column(cown_ref[1], last_ref[1])
    e1c = column(ceast_ref[...], east_ref[0])
    e2c = column(ceast_ref[...], east_ref[1])

    def around(x):
        return jnp.concatenate([pltpu.roll(x, 1, 1), x, pltpu.roll(x, ROWS - 1, 1)], axis=0)

    ends = []
    for side, outer, inner in (
        (0, (w2c, w1c, o0c), (w1c, o0c, o1c)),
        (1, (o255c, e1c, e2c), (o254c, o255c, e1c)),
    ):
        hidden = []
        for cols in (outer, inner):
            xt = around(jnp.concatenate(cols, axis=0))
            hid = jnp.dot(side1_ref[...], xt, preferred_element_type=F32)
            hidden.append(around(jnp.maximum(hid + b1_ref[:, 0:1], 0.0).astype(BF)))
        ends.append(jnp.dot(side2_ref[side], jnp.concatenate(hidden, axis=0), preferred_element_type=F32))
    phase = lanes((OUT, 128)) & 3
    for chunk in range(3):
        at = slice(chunk * 128, chunk * 128 + 128)
        c0 = ends[0][0:OUT, at]
        c1 = pltpu.roll(ends[0][OUT:, at], 1, 1)
        c254 = pltpu.roll(ends[1][OUT:, at], 126, 1)
        c255 = pltpu.roll(ends[1][0:OUT, at], 127, 1)
        for q in range(4):
            z = jnp.where(phase == q, c0, jnp.where(phase == (q + 1) % 4, c1, c255))
            add_ref[q, chunk] = jnp.where(phase == (q + 2) % 4, c254, z)

    lane = lanes((FLD, 128))
    spread = (subs((128, COLS)) == lanes((128, COLS)) // 2).astype(BF)
    fine_ref[0] = jnp.zeros((48, COLS), BF)
    fine_ref[HALF + 1] = jnp.zeros((48, COLS), BF)
    for chunk, count in ((0, 8), (128, 4)):
        west = cwest_ref[:, chunk : chunk + 128]
        east = pltpu.roll(ceast_ref[:, chunk : chunk + 128], 127, 1)
        for q in range(2):
            pair_ref[q] = jnp.where((lane & 1) == q, west, east)

        def widen(k, carry):
            r0 = chunk + 16 * k
            part = coarse_ref[pl.ds(r0, 16)].reshape(256, 128)
            fine = jnp.dot(part, spread, preferred_element_type=F32).astype(BF).reshape(16, FLD, COLS)
            for i in range(16):
                x = fine[i]
                beside = pltpu.roll(pair_ref[i & 1], 128 - (16 * k + i), 1)
                up, down = pltpu.roll(x, 1, 1), pltpu.roll(x, COLS - 1, 1)
                fine_ref[r0 + i + 1, 0:16, 0:128] = jnp.where(lane == 0, beside, up[:, :128])
                fine_ref[r0 + i + 1, 0:16, 128:256] = up[:, 128:]
                fine_ref[r0 + i + 1, 16:32, :] = x
                fine_ref[r0 + i + 1, 32:48, 0:128] = down[:, :128]
                fine_ref[r0 + i + 1, 32:48, 128:256] = jnp.where(lane == 127, beside, down[:, 128:])
            return carry

        lax.fori_loop(0, count, widen, 0, unroll=2)

    hzero = jnp.zeros((HID, COLS), BF)
    h_ref[0] = hzero
    h_ref[ROWS + 1] = hzero

    def conv1(block, carry):
        fetch(block).wait()
        for j in range(4):
            y0 = block * 24 + j * 6
            rows = []
            for i in range(8):
                y = y0 - 1 + i
                half = (block * 12 + j * 3) + (i + 1) // 2
                ym = y if 0 < i < 7 else jnp.clip(y, 0, ROWS - 1)
                for v in range(3):
                    m = jnp.broadcast_to(m3_ref[v, pl.ds(ym, 1), :], (FLD, COLS)).astype(BF)
                    rows.append(fine_ref[half, 16 * v : 16 * v + 16, :] * m)
            for k in range(2):
                x = jnp.concatenate(rows[9 * k : 9 * k + 15], axis=0)
                t = jnp.dot(band1_ref[...], x, preferred_element_type=F32)
                t = t + p_ref[pl.ds(y0 + 3 * k, 3)].reshape(192, COLS).astype(F32)
                h_ref[pl.ds(y0 + 3 * k + 1, 3)] = jnp.maximum(t, 0.0).astype(BF).reshape(3, HID, COLS)
        return carry

    lax.fori_loop(0, BLOCKS, conv1, 0)

    b2 = b2_ref[:, 0:1]
    lane8 = lanes((OUT, 128))

    def conv2(block, carry):
        for k in range(8):
            j = block * 8 + k
            x = h_ref[pl.ds(6 * j, 8)].reshape(512, COLS)
            t = jnp.dot(band2_ref[...], x, preferred_element_type=F32).reshape(6, 3, OUT, COLS)
            for r in range(6):
                y = 6 * j + r
                ends = pltpu.roll(add_ref[y & 3, y >> 7], 128 - (y & 127), 1)
                up = pltpu.roll(t[r, 0], 1, 1)
                down = pltpu.roll(t[r, 2], COLS - 1, 1)
                m = m3_ref[1, pl.ds(y, 1), :]
                lo = jnp.where(lane8 == 0, 0.0, t[r, 1, :, :128]) + b2
                lo = lo + jnp.where(lane8 < 2, ends, up[:, :128]) + down[:, :128]
                hi = jnp.where(lane8 == 127, 0.0, t[r, 1, :, 128:]) + b2
                hi = hi + up[:, 128:] + jnp.where(lane8 > 125, ends, down[:, 128:])
                out_ref[y, :, 0:128] = (lo * m[:, :128]).astype(BF)
                out_ref[y, :, 128:256] = (hi * m[:, 128:]).astype(BF)

        return carry

    lax.fori_loop(0, 8, conv2, 0)


def main_conv(*args):
    vmem = pl.BlockSpec(memory_space=pltpu.VMEM)
    return pl.pallas_call(
        main_kernel,
        out_shape=jax.ShapeDtypeStruct((ROWS, OUT, COLS), BF),
        in_specs=[pl.BlockSpec(memory_space=pl.ANY)] + [vmem] * 13,
        scratch_shapes=[
            pltpu.VMEM((HALF + 2, 48, COLS), BF),
            pltpu.VMEM((ROWS, HID, COLS), BF),
            pltpu.VMEM((ROWS + 2, HID, COLS), BF),
            pltpu.VMEM((4, 3, OUT, 128), F32),
            pltpu.VMEM((192, 240), BF),
            pltpu.VMEM((144, 512), BF),
            pltpu.VMEM((HID, 288), BF),
            pltpu.VMEM((2, 2 * OUT, 384), BF),
            pltpu.VMEM((2, FLD, 128), BF),
            pltpu.SemaphoreType.DMA((BLOCKS,)),
        ],
        compiler_params=pltpu.CompilerParams(vmem_limit_bytes=44 << 20),
        name="convs",
    )(*args)


def onehot(pairs, rows, cols):
    src = subs((rows, cols))
    dst = lanes((rows, cols))
    hit = jnp.zeros((rows, cols), jnp.bool_)
    for source, cond in pairs:
        hit = hit | ((src == source(dst)) & cond(dst))
    return hit.astype(BF)


def patch_kernel(
    fold_ref, south_ref, low_ref, mid_ref, top_ref, north_ref, tops_ref, strip_ref,
    w1_ref, b1_ref, w2_ref, b2_ref, main_ref, out_ref, in_ref, res_ref, sem,
):
    gy, gx = lax.axis_index("gy"), lax.axis_index("gx")
    signs = jnp.where(
        (subs((2 * FLD, PAD)) < 8) | (subs((2 * FLD, PAD)) == 16) | (subs((2 * FLD, PAD)) == 17), -1.0, 1.0
    )
    at = 0
    for ref, count in ((south_ref, 2), (low_ref, 2), (mid_ref, 4), (top_ref, 2), (north_ref, 2)):
        for k in range(count):
            in_ref[at] = ref[k].astype(F32)
            at += 1
    for k in range(3):
        in_ref[12 + k] = jnp.zeros((2 * FLD, PAD), F32)

    wrap = lambda t: jnp.where(t < 0, t + 16, jnp.where(t > 15, t - 16, t))
    near = wrap(gx - 1)
    far = wrap(gx + 1)
    p = fold_ref[gx]
    a = fold_ref[near]
    b = fold_ref[far]

    @pl.when(gy == 7)
    def _():
        def move(x, pairs):
            return jnp.dot(x, onehot(pairs, x.shape[1], PAD), preferred_element_type=F32)

        def inside(lo, hi):
            return lambda d: (d >= lo) & (d <= hi)

        def put(column, lane_at, step=0):
            count = 2 if step else 1
            return [(lambda d: column + step * (d - lane_at), inside(lane_at, lane_at + count - 1))]

        mirror = lambda d: SHIFT + COLS - 1 - d
        row = move(tops_ref[p, 1], [(mirror, inside(SHIFT, SHIFT + 255))])
        row = row + move(tops_ref[a, 1], put(1, 0, -1))
        row = row + move(tops_ref[b, 1], put(COLS - 1, SHIFT + COLS, -1))
        in_ref[10] = row * signs
        for k in range(2):
            in_ref[12 + k] = (
                move(tops_ref[p, k], [(mirror, inside(SHIFT, SHIFT + 255))])
                + move(tops_ref[wrap(p + 1), k], put(0, SHIFT - 1))
                + move(tops_ref[wrap(p - 1), k], put(COLS - 1, SHIFT + COLS))
                + move(tops_ref[a, k], put(1, 264, -1))
                + move(tops_ref[wrap(a - 1), k], put(COLS - 1, 266))
                + move(tops_ref[b, k], put(COLS - 1, 273, -1))
                + move(tops_ref[wrap(b + 1), k], put(0, 272))
            )
        last = move(
            in_ref[9].astype(BF),
            [(lambda d: d, inside(SHIFT, SHIFT + 255))] + put(0, 264, 1) + put(SHIFT + COLS, 273, 1),
        )
        last = last + move(tops_ref[fold_ref[wrap(p + 1)], 1], put(COLS - 1, SHIFT - 1))
        last = last + move(tops_ref[fold_ref[wrap(p - 1)], 1], put(0, SHIFT + COLS))
        last = last + move(tops_ref[fold_ref[wrap(a - 1)], 1], put(0, 266))
        last = last + move(tops_ref[fold_ref[wrap(b + 1)], 1], put(COLS - 1, 272))
        in_ref[14] = last * signs

    def shifted(x):
        return [pltpu.roll(x, 1, 1).astype(BF), x.astype(BF), pltpu.roll(x, PAD - 1, 1).astype(BF)]

    inputs = [shifted(in_ref[k]) for k in range(15)]
    weights = [
        jnp.concatenate([w1_ref[u, 2 - v if flip else v] for u in range(3) for v in range(3)], axis=1)
        for flip in (False, True)
    ]

    def hidden(rows, flip):
        x = jnp.concatenate(inputs[rows] + inputs[rows + 1] + inputs[rows + 2], axis=0)
        total = jnp.dot(weights[flip], x, preferred_element_type=F32)
        return jnp.maximum(total + b1_ref[:, 0:1], 0.0).astype(BF)

    virtual = hidden(12, True).astype(F32)
    lane = lanes((HID, PAD))
    virtual = jnp.where(
        lane == SHIFT - 1,
        pltpu.roll(virtual, (SHIFT - 1 - 265) % PAD, 1),
        jnp.where(lane == SHIFT + 256, pltpu.roll(virtual, (SHIFT + 256 - 273) % PAD, 1), virtual),
    )
    second = jnp.concatenate([w2_ref[u, v] for u in range(3) for v in range(3)], axis=1)
    for half in range(2):
        hid = [hidden(6 * half + k, False).astype(F32) for k in range(4)]
        if half == 0:
            hid[0] = jnp.where(gy == 0, jnp.zeros_like(hid[0]), hid[0])
        else:
            hid[3] = jnp.where(gy == 7, virtual, hid[3])
        around = [shifted(x) for x in hid]
        for r in range(2):
            x = jnp.concatenate(around[r] + around[r + 1] + around[r + 2], axis=0)
            total = jnp.dot(second, x, preferred_element_type=F32) + b2_ref[:, 0:1]
            m = strip_ref[6 * half + r, FLD : 2 * FLD, :].astype(F32)[:OUT]
            total = pltpu.roll(total * m, PAD - SHIFT, 1)
            res_ref[2 * half + r] = total[:, :COLS].astype(BF)
    copies = [
        pltpu.make_async_copy(res_ref.at[pl.ds(0, 2)], out_ref.at[pl.ds(0, 2)], sem.at[0]),
        pltpu.make_async_copy(res_ref.at[pl.ds(2, 2)], out_ref.at[pl.ds(ROWS - 2, 2)], sem.at[1]),
    ]
    for c in copies:
        c.start()
    for c in copies:
        c.wait()


def patch_rows(*args):
    smem = pl.BlockSpec(memory_space=pltpu.SMEM)
    vmem = pl.BlockSpec(memory_space=pltpu.VMEM)
    hbm = pl.BlockSpec(memory_space=pl.ANY)
    return pl.pallas_call(
        patch_kernel,
        out_shape=jax.ShapeDtypeStruct((ROWS, OUT, COLS), BF),
        in_specs=[smem] + [vmem] * 11 + [hbm],
        out_specs=hbm,
        scratch_shapes=[
            pltpu.VMEM((15, 2 * FLD, PAD), F32),
            pltpu.VMEM((4, OUT, COLS), BF),
            pltpu.SemaphoreType.DMA((2,)),
        ],
        input_output_aliases={12: 0},
        compiler_params=pltpu.CompilerParams(vmem_limit_bytes=24 << 20),
        name="patch",
    )(*args)


def shift_gx(x, step):
    n = lax.axis_size("gx")
    return lax.ppermute(x, "gx", [(i, (i + step) % n) for i in range(n)])


def shift_gy(x, step):
    n = lax.axis_size("gy")
    return lax.ppermute(x, "gy", [(i, i + step) for i in range(n) if 0 <= i + step < n])


def per_device(
    ocean, atm, dest_tile, dest_row, live, land_mask, fold_pair, w1, b1, w2, b2
):
    outgoing = pack(
        dest_tile.reshape(1, HALF), dest_row.reshape(1, HALF), live.reshape(1, HALF), atm.reshape(2 * HALF, 8, 128)
    )
    incoming = lax.all_to_all(
        outgoing.reshape(DEV, STEP, 8, 128), ("gy", "gx"), split_axis=0, concat_axis=0, tiled=True
    )
    ocean, land_mask, _ = lax.optimization_barrier((ocean, land_mask, outgoing))
    first, last = edge_columns(ocean, land_mask)
    west = shift_gx(last, 1)
    east = shift_gx(first, -1)
    part, rows, w1, b1c, b2c = ocean_part(
        ocean, land_mask, w1.swapaxes(2, 3), b1.reshape(1, HID), b2.reshape(1, OUT)
    )
    m3, strip = margins(land_mask, west, east, rows)

    coarse, ccols, cwest, ceast, low, mid, top, tops = coarse_sums(
        incoming, strip
    )
    south = shift_gy(top, 1)
    north = shift_gy(low, -1)
    tops = lax.all_to_all(tops, "gx", split_axis=0, concat_axis=0, tiled=True)
    out = main_conv(
        part, m3, coarse, first, last, west, east, ccols, cwest, ceast, w1, b1c, w2, b2c,
    )
    return patch_rows(
        fold_pair, south, low, mid, top, north, tops, strip, w1, b1c, w2, b2c, out
    )


def solution(mesh):
    return jax.shard_map(
        per_device,
        mesh=mesh,
        in_specs=(
            P("gy", None, "gx"),
            P(("gy", "gx"), None, None),
            P(("gy", "gx"), None),
            P(("gy", "gx")),
            P(("gy", "gx")),
            P("gy", "gx"),
            P(),
            P(),
            P(),
            P(),
            P(),
        ),
        out_specs=P("gy", None, "gx"),
        check_vma=False,
    )
```

```python
import functools

import jax
import jax.numpy as jnp
from jax import lax
from jax.experimental import pallas as pl
from jax.experimental.pallas import tpu as pltpu
from jax.sharding import PartitionSpec as P

BF = jnp.bfloat16
F32 = jnp.float32
I32 = jnp.int32
VMEM_LIMIT = 56 << 20
ROWS = 384
COLS = 256
HALF = 192
DEV = 128
CAP = 3
FLD = 16
HID = 64
OUT = 8
PAD = 384
SHIFT = 2


def lanes(shape):
    return lax.broadcasted_iota(I32, shape, len(shape) - 1)


def subs(shape):
    return lax.broadcasted_iota(I32, shape, len(shape) - 2)


STEP = 2 * CAP + 1


PIECES = 8


def pack_kernel(
    tile_ref, row_ref, live_ref, atm_hbm, out_hbm, atm_ref, out_ref, q_ref, code_ref, info_ref,
    sem, in_sem, out_sem,
):
    loads, stores = [], []
    for c in range(PIECES):
        at = pl.ds(c * (2 * HALF // PIECES), 2 * HALF // PIECES)
        loads.append(pltpu.make_async_copy(atm_hbm.at[at], atm_ref.at[at], in_sem.at[c]))
        at = pl.ds(c * (DEV * STEP // PIECES), DEV * STEP // PIECES)
        stores.append(pltpu.make_async_copy(out_ref.at[at], out_hbm.at[at], out_sem.at[c]))
        loads[c].start()
    across = jnp.concatenate([tile_ref[...].astype(F32), jnp.full((1, 64), -1.0, F32)], axis=1)
    column = jnp.broadcast_to(across, (128, 256))
    column = jnp.concatenate([column[:, :128].T, column[:, 128:].T[:64]], axis=0)
    earlier = (subs((HALF, 256)) < lanes((HALF, 256))) & (
        jnp.concatenate([column, column], axis=1) == jnp.broadcast_to(across, (HALF, 256))
    )
    code = 4.0 * across + jnp.sum(earlier.astype(F32), axis=0, keepdims=True)
    code_ref[...] = code.astype(I32)
    copy = pltpu.make_async_copy(code_ref, info_ref, sem)
    copy.start()
    lane = lanes((FLD, 128))
    first, last = [], []
    for chunk, count, need in ((0, 128, loads[:6]), (128, 64, loads[6:])):
        for load in need:
            load.wait()

        def ends(i, carry):
            c0, c1 = carry
            block = atm_ref[pl.ds(2 * (chunk + i), 2)].reshape(FLD, 128)
            here = lane == i
            c0 = jnp.where(here, pltpu.roll(block, i, 1), c0)
            c1 = jnp.where(here, pltpu.roll(block, i + 1, 1), c1)
            return c0, c1

        zero = jnp.zeros((FLD, 128), BF)
        c0, c1 = lax.fori_loop(0, count, ends, (zero, zero), unroll=32)
        first.append(c0)
        last.append(c1)
    values = [jnp.concatenate(last, axis=1), jnp.concatenate(first, axis=1)]
    code = jnp.broadcast_to(code_ref[...], (DEV, 256))
    row = jnp.where(live_ref[...] == 1, row_ref[...] + 1, 0).astype(F32)
    row = jnp.concatenate([row, jnp.zeros((1, 64), F32)], axis=1).astype(BF)
    hits, columns = [], []
    tile = subs((DEV, 256))
    none = jnp.zeros((FLD, 256), BF)
    for k in range(CAP):
        hits.append((code == 4 * tile + k).astype(BF))
        rows = jnp.where(subs((FLD, 256)) == k, jnp.broadcast_to(row, (FLD, 256)), none)
        parts = [rows] + [values[0] if i == k else none for i in range(3)]
        parts = parts + [values[1] if i == k else none for i in range(3)] + [none]
        columns.append(jnp.concatenate(parts, axis=0))
    total = lax.dot_general(
        jnp.concatenate(hits, axis=1),
        jnp.concatenate(columns, axis=1),
        (((1,), (1,)), ((), ())),
        preferred_element_type=F32,
    )
    q_ref[...] = total
    copy.wait()

    def place(n, carry):
        code = info_ref[0, n]
        out_ref[pl.ds(STEP * (code >> 2) + 2 * (code & 3), 2)] = atm_ref[pl.ds(2 * n, 2)]
        return carry

    lax.fori_loop(0, HALF, place, 0, unroll=32)
    sub = subs((8, 128))
    for c in range(PIECES):
        for t in range(c * DEV // PIECES, (c + 1) * DEV // PIECES):
            near = (t & -16) + ((t + 15) & 15)
            far = (t & -16) + ((t + 1) & 15)
            own, west, east = [
                jnp.broadcast_to(q_ref[i : i + 1, :], (8, 128)) for i in (t, near, far)
            ]
            head = jnp.where(sub == 0, own, jnp.where(sub == 1, west, east))
            out_ref[STEP * t + STEP - 1] = head.astype(BF)
        stores[c].start()
    for store in stores:
        store.wait()


def pack(tile, row, live, atm):
    vmem = pl.BlockSpec(memory_space=pltpu.VMEM)
    hbm = pl.BlockSpec(memory_space=pl.ANY)
    return pl.pallas_call(
        pack_kernel,
        out_shape=jax.ShapeDtypeStruct((DEV * STEP, 8, 128), BF),
        in_specs=[vmem, vmem, vmem, hbm],
        out_specs=hbm,
        scratch_shapes=[
            pltpu.VMEM((2 * HALF, 8, 128), BF),
            pltpu.VMEM((DEV * STEP, 8, 128), BF),
            pltpu.VMEM((DEV, 128), F32),
            pltpu.VMEM((1, 256), I32),
            pltpu.SMEM((1, 256), I32),
            pltpu.SemaphoreType.DMA,
            pltpu.SemaphoreType.DMA((PIECES,)),
            pltpu.SemaphoreType.DMA((PIECES,)),
        ],
        compiler_params=pltpu.CompilerParams(vmem_limit_bytes=56 << 20),
        name="pack",
    )(tile, row, live, atm)


def coarse_kernel(
    inc_hbm, strip_ref, out_ref, cols_ref, west_ref, east_ref, low_ref, mid_ref, top_ref, tops_ref,
    inc_ref, raw_ref, acc_ref, head_ref, idx_ref, where_ref, sem, raw_sem, in_sem,
):
    raw = pltpu.make_async_copy(inc_hbm.at[:, STEP - 1], raw_ref, raw_sem)
    raw.start()
    loads = []
    for c in range(PIECES):
        at = pl.ds(c * DEV // PIECES, DEV // PIECES)
        loads.append(pltpu.make_async_copy(inc_hbm.at[at], inc_ref.at[at], in_sem.at[c]))
        loads[c].start()
    acc_ref[...] = jnp.zeros_like(acc_ref)
    raw.wait()
    few = lanes((8, 128)) < CAP
    for g in range(4):

        def gather(s, total):
            head = raw_ref[32 * g + s].astype(F32)
            head_ref[32 * g + s] = head
            return total + pltpu.roll(jnp.where(few, head, 0.0), 4 * s, 1)

        idx_ref[g] = lax.fori_loop(0, 32, gather, jnp.zeros((8, 128), F32), unroll=32).astype(I32)
    copy = pltpu.make_async_copy(idx_ref, where_ref, sem)
    copy.start()
    target = (subs((256, DEV)) + 1).astype(F32)
    for j, wanted in (
        (0, ((4 * FLD, cols_ref.at[0]), (FLD, cols_ref.at[1]))),
        (1, ((FLD, west_ref),)),
        (2, ((4 * FLD, east_ref),)),
    ):
        turned = head_ref[:, j, :].T
        values = turned.astype(BF)
        hits = jnp.concatenate(
            [
                (jnp.broadcast_to(turned[k : k + 1], (256, DEV)) == target).astype(BF)
                for k in range(CAP)
            ],
            axis=1,
        )
        blocks = jnp.concatenate(
            [
                jnp.concatenate([values[at + FLD * k : at + FLD * k + FLD] for k in range(CAP)], axis=1)
                for at, _ in wanted
            ],
            axis=0,
        )
        total = lax.dot_general(blocks, hits, (((1,), (1,)), ((), ())), preferred_element_type=F32)
        for n, (_, ref) in enumerate(wanted):
            ref[...] = total[n * FLD : n * FLD + FLD].astype(BF)
    copy.wait()
    for c in range(PIECES):
        loads[c].wait()
        count = DEV // PIECES

        def add(i, carry):
            for k in range(CAP):
                r = where_ref[c * count // 32, 0, 4 * (c * count % 32 + i) + k]
                block = inc_ref[c * count + i, 2 * k : 2 * k + 2]
                acc_ref[k, r] = acc_ref[k, r] + block.astype(F32)
            return carry

        lax.fori_loop(0, count, add, 0, unroll=16)
    lane = lanes((FLD, 128))

    def summed(r):
        total = acc_ref[0, r + 1] + acc_ref[1, r + 1] + acc_ref[2, r + 1]
        return total.reshape(FLD, 128).astype(BF)

    def finish(r, carry):
        out_ref[r] = summed(r)
        return carry

    spread = (subs((256, PAD)) == lanes((256, PAD)) // 2).astype(BF)
    wides = []
    for r in (0, 1, HALF - 2, HALF - 1):
        chunk, i = (r // 128) * 128, r % 128
        west = pltpu.roll(west_ref[:, chunk : chunk + 128].astype(F32), (128 - i) % 128, 1)
        east = pltpu.roll(east_ref[:, chunk : chunk + 128].astype(F32), (129 - i) % 128, 1)
        row = pltpu.roll(summed(r).astype(F32), 1, 1)
        wides.append(jnp.concatenate(
            [
                jnp.where(lane == 0, west, row),
                jnp.where(lane == 0, row, jnp.where(lane == 1, east, 0.0)),
            ],
            axis=1,
        ).astype(BF))
    fines = jnp.dot(jnp.concatenate(wides, axis=0), spread, preferred_element_type=F32).astype(BF)
    for k in range(4):
        fine = fines[k * FLD : k * FLD + FLD]
        for h in range(2):
            n = 2 * k + h
            ref, at = ((low_ref, n), (mid_ref, n - 2), (mid_ref, n - 2), (top_ref, n - 6))[k]
            ref[at, 0:FLD, :] = strip_ref[n, 0:FLD, :]
            ref[at, FLD : 2 * FLD, :] = fine * strip_ref[n, FLD : 2 * FLD, :]
    for h in range(2):
        row = pltpu.roll(top_ref[h].astype(F32), PAD - SHIFT, 1)[:, :COLS].astype(BF)
        for t in range(16):
            tops_ref[t, h] = row
    lax.fori_loop(0, HALF, finish, 0, unroll=16)


def coarse_sums(incoming, strip):
    return pl.pallas_call(
        coarse_kernel,
        out_shape=(
            jax.ShapeDtypeStruct((HALF, FLD, 128), BF),
            jax.ShapeDtypeStruct((2, FLD, 256), BF),
            jax.ShapeDtypeStruct((FLD, 256), BF),
            jax.ShapeDtypeStruct((FLD, 256), BF),
            jax.ShapeDtypeStruct((2, 2 * FLD, PAD), BF),
            jax.ShapeDtypeStruct((4, 2 * FLD, PAD), BF),
            jax.ShapeDtypeStruct((2, 2 * FLD, PAD), BF),
            jax.ShapeDtypeStruct((16, 2, 2 * FLD, COLS), BF),
        ),
        in_specs=[pl.BlockSpec(memory_space=pl.ANY), pl.BlockSpec(memory_space=pltpu.VMEM)],
        scratch_shapes=[
            pltpu.VMEM((DEV, STEP, 8, 128), BF),
            pltpu.VMEM((DEV, 8, 128), BF),
            pltpu.VMEM((CAP, HALF + 1, 2, 8, 128), F32),
            pltpu.VMEM((DEV, 8, 128), F32),
            pltpu.VMEM((4, 8, 128), I32),
            pltpu.SMEM((4, 8, 128), I32),
            pltpu.SemaphoreType.DMA,
            pltpu.SemaphoreType.DMA,
            pltpu.SemaphoreType.DMA((PIECES,)),
        ],
        compiler_params=pltpu.CompilerParams(vmem_limit_bytes=20 << 20),
        name="coarse",
    )(incoming, strip)


def edge_kernel(ocean_ref, mask_ref, first_ref, last_ref):
    lane = lanes((FLD, 128))
    for chunk in range(3):
        block = mask_ref[chunk * 128 : chunk * 128 + 128, :].astype(F32)
        m_left = block[:, :128].T
        m_right = block[:, 128:].T

        def take(i, carry):
            x = ocean_ref[chunk * 128 + i]
            left, right = x[:, :128], x[:, 128:]
            here = lane == i
            c0, c1, c2, c3 = carry
            c0 = jnp.where(here, pltpu.roll(left, i, 1), c0)
            c1 = jnp.where(here, pltpu.roll(left, i + 127, 1), c1)
            c2 = jnp.where(here, pltpu.roll(right, i + 2, 1), c2)
            c3 = jnp.where(here, pltpu.roll(right, i + 1, 1), c3)
            return c0, c1, c2, c3

        zero = jnp.zeros((FLD, 128), BF)
        got = lax.fori_loop(0, 128, take, (zero,) * 4, unroll=16)
        rows = (m_left[0:1], m_left[1:2], m_right[126:127], m_right[127:128])
        for k in range(4):
            m = jnp.broadcast_to(rows[k], (FLD, 128)).astype(BF)
            ref = last_ref if k >= 2 else first_ref
            ref[k % 2, :, chunk * 128 : chunk * 128 + 128] = jnp.concatenate([got[k] * m, m], axis=0)


def edge_columns(ocean, mask):
    return pl.pallas_call(
        edge_kernel,
        out_shape=(jax.ShapeDtypeStruct((2, 2 * FLD, ROWS), BF),) * 2,
        compiler_params=pltpu.CompilerParams(vmem_limit_bytes=24 << 20),
        name="edges",
    )(ocean, mask)


BLOCKS = 16


def banded(w_ref, dst_ref, first):
    dst_ref[...] = jnp.zeros_like(dst_ref)
    for r in range(3):
        for u in range(3):
            for v in range(3):
                at = ((r + u) * 3 + v) * FLD
                dst_ref[r * HID : r * HID + HID, at : at + FLD] = w_ref[u, v, :, first : first + FLD]


def ocean_kernel(
    ocean_ref, mask_ref, wt_ref, b1_ref, b2_ref, part_ref, strip_ref, w_ref, b1c_ref, b2c_ref, xs_ref, band_ref, h_ref, sem,
):
    for u in range(3):
        for v in range(3):
            w_ref[u, v] = wt_ref[u, v].astype(F32).T.astype(BF)
    b1c_ref[...] = jnp.broadcast_to(b1_ref[...], (128, HID)).T
    b2c_ref[...] = jnp.broadcast_to(b2_ref[...], (128, OUT)).T
    banded(w_ref, band_ref, 0)
    bias = jnp.concatenate([b1c_ref[:, 0:1]] * 3, axis=0)
    lane16 = lanes((FLD, 128))
    zero = jnp.zeros((48, COLS), BF)
    xs_ref[0] = zero
    xs_ref[ROWS + 1] = zero
    nothing = jnp.zeros((FLD, 128), BF)

    def build(y):
        m = jnp.broadcast_to(mask_ref[pl.ds(y, 1), :].astype(F32), (FLD, COLS)).astype(BF)
        x = ocean_ref[y] * m
        up, down = pltpu.roll(x, 1, 1), pltpu.roll(x, COLS - 1, 1)
        xs_ref[y + 1, 0:16, 0:128] = jnp.where(lane16 == 0, nothing, up[:, :128])
        xs_ref[y + 1, 0:16, 128:256] = up[:, 128:]
        xs_ref[y + 1, 16:32, :] = x
        xs_ref[y + 1, 32:48, 0:128] = down[:, :128]
        xs_ref[y + 1, 32:48, 128:256] = jnp.where(lane16 == 127, nothing, down[:, 128:])

    for n, y in enumerate((0, 1, 2, 3, ROWS - 4, ROWS - 3, ROWS - 2, ROWS - 1)):
        m = jnp.broadcast_to(mask_ref[y : y + 1, :].astype(F32), (FLD, COLS))
        x = jnp.concatenate([ocean_ref[y].astype(F32) * m, m], axis=0)
        x = jnp.concatenate([x, jnp.zeros((2 * FLD, 128), F32)], axis=1)
        strip_ref[n] = pltpu.roll(x, SHIFT, 1).astype(BF)

    def first(i, carry):
        build(i)
        return carry

    lax.fori_loop(0, 24, first, 0, unroll=8)

    def conv(block, carry):
        for k in range(8):
            g = block * 8 + k
            for r in range(3):
                build(jnp.minimum(3 * g + 24 + r, ROWS - 1))
            x = xs_ref[pl.ds(3 * g, 5)].reshape(240, COLS)
            t = jnp.dot(band_ref[...], x, preferred_element_type=F32) + bias
            h_ref[pl.ds(3 * g, 3)] = t.astype(BF).reshape(3, HID, COLS)
        at = pl.ds(block * 24, 24)
        pltpu.make_async_copy(h_ref.at[at], part_ref.at[at], sem.at[block]).start()
        return carry

    lax.fori_loop(0, BLOCKS, conv, 0)
    for block in range(BLOCKS):
        at = pl.ds(block * 24, 24)
        pltpu.make_async_copy(h_ref.at[at], part_ref.at[at], sem.at[block]).wait()


def ocean_part(*args):
    return pl.pallas_call(
        ocean_kernel,
        out_shape=(
            jax.ShapeDtypeStruct((ROWS, HID, COLS), BF),
            jax.ShapeDtypeStruct((8, 2 * FLD, PAD), BF),
            jax.ShapeDtypeStruct((3, 3, HID, 2 * FLD), BF),
            jax.ShapeDtypeStruct((HID, 128), F32),
            jax.ShapeDtypeStruct((OUT, 128), F32),
        ),
        out_specs=(pl.BlockSpec(memory_space=pl.ANY),) + (pl.BlockSpec(memory_space=pltpu.VMEM),) * 4,
        scratch_shapes=[
            pltpu.VMEM((ROWS + 2, 48, COLS), BF),
            pltpu.VMEM((192, 240), BF),
            pltpu.VMEM((ROWS, HID, COLS), BF),
            pltpu.SemaphoreType.DMA((BLOCKS,)),
        ],
        compiler_params=pltpu.CompilerParams(vmem_limit_bytes=40 << 20),
        name="ocean",
    )(*args)


def margin_kernel(mask_ref, west_ref, east_ref, rows_ref, m3_ref, strip_ref):
    lane = lanes((128, 128))
    for chunk in range(3):
        at = slice(chunk * 128, chunk * 128 + 128)
        m = mask_ref[at, :].astype(F32)
        up, down = pltpu.roll(m, 1, 1), pltpu.roll(m, COLS - 1, 1)
        west = jnp.broadcast_to(west_ref[1, FLD : FLD + 1, at].astype(F32), (128, 128)).T
        east = jnp.broadcast_to(east_ref[0, FLD : FLD + 1, at].astype(F32), (128, 128)).T
        m3_ref[0, at, 0:128] = jnp.where(lane == 0, west, up[:, :128])
        m3_ref[0, at, 128:256] = up[:, 128:]
        m3_ref[1, at, :] = m
        m3_ref[2, at, 0:128] = down[:, :128]
        m3_ref[2, at, 128:256] = jnp.where(lane == 127, east, down[:, 128:])
    wide_lane = lanes((2 * FLD, 128))
    for n, y in enumerate((0, 1, 2, 3, ROWS - 4, ROWS - 3, ROWS - 2, ROWS - 1)):
        base, i = (y // 128) * 128, y % 128
        x = rows_ref[n].astype(F32)

        def beside(ref, k, lane_at):
            return pltpu.roll(ref[k, :, base : base + 128].astype(F32), (128 + lane_at - i) % 128, 1)

        lo = jnp.where(wide_lane == 0, beside(west_ref, 0, 0), x[:, 0:128])
        lo = jnp.where(wide_lane == 1, beside(west_ref, 1, 1), lo)
        hi = jnp.where(wide_lane == 2, beside(east_ref, 0, 2), x[:, 256:])
        hi = jnp.where(wide_lane == 3, beside(east_ref, 1, 3), hi)
        strip_ref[n, :, 0:128] = lo.astype(BF)
        strip_ref[n, :, 128:256] = x[:, 128:256].astype(BF)
        strip_ref[n, :, 256:384] = hi.astype(BF)

def margins(*args):
    return pl.pallas_call(
        margin_kernel,
        out_shape=(
            jax.ShapeDtypeStruct((3, ROWS, COLS), F32),
            jax.ShapeDtypeStruct((8, 2 * FLD, PAD), BF),
        ),
        compiler_params=pltpu.CompilerParams(vmem_limit_bytes=24 << 20),
        name="margins",
    )(*args)


def main_kernel(
    part_ref, m3_ref, coarse_ref, first_ref, last_ref, west_ref, east_ref, cown_ref, cwest_ref, ceast_ref,
    w1_ref, b1_ref, w2_ref, b2_ref, out_ref,
    fine_ref, p_ref, h_ref, add_ref, band1_ref, band2_ref, side1_ref, side2_ref, pair_ref, res_ref, sem, out_sem,
):
    def fetch(block):
        at = pl.ds(block * 24, 24)
        return pltpu.make_async_copy(part_ref.at[at], p_ref.at[at], sem.at[block])

    for block in range(BLOCKS):
        fetch(block).start()

    banded(w1_ref, band1_ref, FLD)
    band2_ref[...] = jnp.zeros_like(band2_ref)
    for u in range(3):
        for v in range(3):
            w = w2_ref[u, v]
            for i in range(4):
                at = ((i + 2 - u) * 3 + v) * OUT
                band2_ref[at : at + OUT, i * HID : i * HID + HID] = w
            w1 = w1_ref[u, v]
            at = (u * 3 + v) * 2 * FLD
            side1_ref[:, at : at + 2 * FLD] = w1
        for side in range(2):
            at = u * HID
            side2_ref[side, 0:OUT, at : at + HID] = w2_ref[u, 2 * side]
            side2_ref[side, OUT : 2 * OUT, at : at + HID] = jnp.zeros((OUT, HID), BF)
            at = (3 + u) * HID
            side2_ref[side, 0:OUT, at : at + HID] = w2_ref[u, 1]
            side2_ref[side, OUT : 2 * OUT, at : at + HID] = w2_ref[u, 2 * side]

    rep = (subs((256, ROWS)) == lanes((256, ROWS)) // 2).astype(BF)

    def column(coarse_t, strip):
        fine = jnp.dot(coarse_t, rep, preferred_element_type=F32)
        return jnp.concatenate([strip[:FLD], (fine * strip[FLD:].astype(F32)).astype(BF)], axis=0)

    w2c = column(cwest_ref[...], west_ref[0])
    w1c = column(cwest_ref[...], west_ref[1])
    o0c = column(cown_ref[0], first_ref[0])
    o1c = column(cown_ref[0], first_ref[1])
    o254c = column(cown_ref[1], last_ref[0])
    o255c = column(cown_ref[1], last_ref[1])
    e1c = column(ceast_ref[...], east_ref[0])
    e2c = column(ceast_ref[...], east_ref[1])

    def around(x):
        return jnp.concatenate([pltpu.roll(x, 1, 1), x, pltpu.roll(x, ROWS - 1, 1)], axis=0)

    groups = ((w2c, w1c, o0c), (w1c, o0c, o1c), (o255c, e1c, e2c), (o254c, o255c, e1c))
    xt = jnp.concatenate([around(jnp.concatenate(cols, axis=0)) for cols in groups], axis=1)
    hid = jnp.dot(side1_ref[...], xt, preferred_element_type=F32)
    hid = jnp.maximum(hid + b1_ref[:, 0:1], 0.0).astype(BF)
    hid = [around(hid[:, k * ROWS : k * ROWS + ROWS]) for k in range(4)]
    ends = [
        jnp.dot(
            side2_ref[side],
            jnp.concatenate(hid[2 * side : 2 * side + 2], axis=0),
            preferred_element_type=F32,
        )
        for side in range(2)
    ]
    phase = lanes((OUT, 128)) & 3
    for chunk in range(3):
        at = slice(chunk * 128, chunk * 128 + 128)
        c0 = ends[0][0:OUT, at]
        c1 = pltpu.roll(ends[0][OUT:, at], 1, 1)
        c254 = pltpu.roll(ends[1][OUT:, at], 126, 1)
        c255 = pltpu.roll(ends[1][0:OUT, at], 127, 1)
        for q in range(4):
            z = jnp.where(phase == q, c0, jnp.where(phase == (q + 1) % 4, c1, c255))
            add_ref[q, chunk] = jnp.where(phase == (q + 2) % 4, c254, z)

    lane = lanes((FLD, 128))
    spread = (subs((128, COLS)) == lanes((128, COLS)) // 2).astype(BF)
    fine_ref[0] = jnp.zeros((48, COLS), BF)
    fine_ref[HALF + 1] = jnp.zeros((48, COLS), BF)
    for chunk, count in ((0, 8), (128, 4)):
        west = cwest_ref[:, chunk : chunk + 128]
        east = pltpu.roll(ceast_ref[:, chunk : chunk + 128], 127, 1)
        for q in range(2):
            pair_ref[q] = jnp.where((lane & 1) == q, west, east)

        def widen(k, carry):
            r0 = chunk + 16 * k
            part = coarse_ref[pl.ds(r0, 16)].reshape(256, 128)
            fine = jnp.dot(part, spread, preferred_element_type=F32).astype(BF).reshape(16, FLD, COLS)
            for i in range(16):
                x = fine[i]
                beside = pltpu.roll(pair_ref[i & 1], 128 - (16 * k + i), 1)
                up, down = pltpu.roll(x, 1, 1), pltpu.roll(x, COLS - 1, 1)
                fine_ref[r0 + i + 1, 0:16, 0:128] = jnp.where(lane == 0, beside, up[:, :128])
                fine_ref[r0 + i + 1, 0:16, 128:256] = up[:, 128:]
                fine_ref[r0 + i + 1, 16:32, :] = x
                fine_ref[r0 + i + 1, 32:48, 0:128] = down[:, :128]
                fine_ref[r0 + i + 1, 32:48, 128:256] = jnp.where(lane == 127, beside, down[:, 128:])
            return carry

        lax.fori_loop(0, count, widen, 0, unroll=2)

    hzero = jnp.zeros((HID, COLS), BF)
    h_ref[0] = hzero
    h_ref[ROWS + 1] = hzero

    def conv1(block, carry):
        fetch(block).wait()
        for j in range(4):
            y0 = block * 24 + j * 6
            rows = []
            for i in range(8):
                y = y0 - 1 + i
                half = (block * 12 + j * 3) + (i + 1) // 2
                ym = y if 0 < i < 7 else jnp.clip(y, 0, ROWS - 1)
                for v in range(3):
                    m = jnp.broadcast_to(m3_ref[v, pl.ds(ym, 1), :], (FLD, COLS)).astype(BF)
                    rows.append(fine_ref[half, 16 * v : 16 * v + 16, :] * m)
            for k in range(2):
                x = jnp.concatenate(rows[9 * k : 9 * k + 15], axis=0)
                t = jnp.dot(band1_ref[...], x, preferred_element_type=F32)
                t = t + p_ref[pl.ds(y0 + 3 * k, 3)].reshape(192, COLS).astype(F32)
                h_ref[pl.ds(y0 + 3 * k + 1, 3)] = jnp.maximum(t, 0.0).astype(BF).reshape(3, HID, COLS)
        return carry

    lax.fori_loop(0, BLOCKS, conv1, 0)

    b2 = b2_ref[:, 0:1]
    lane8 = lanes((OUT, 128))

    def emit(y, t):
        ends = pltpu.roll(add_ref[y & 3, y >> 7], 128 - (y & 127), 1)
        up = pltpu.roll(t[0], 1, 1)
        down = pltpu.roll(t[2], COLS - 1, 1)
        m = m3_ref[1, pl.ds(y, 1), :]
        lo = jnp.where(lane8 == 0, 0.0, t[1, :, :128]) + b2
        lo = lo + jnp.where(lane8 < 2, ends, up[:, :128]) + down[:, :128]
        hi = jnp.where(lane8 == 127, 0.0, t[1, :, 128:]) + b2
        hi = hi + up[:, 128:] + jnp.where(lane8 > 125, ends, down[:, 128:])
        res_ref[y, :, 0:128] = (lo * m[:, :128]).astype(BF)
        res_ref[y, :, 128:256] = (hi * m[:, 128:]).astype(BF)

    def store(block):
        at = pl.ds(block * 48, 48)
        return pltpu.make_async_copy(res_ref.at[at], out_ref.at[at], out_sem.at[block])

    def conv2(block, carry):
        for k in range(12):
            g = block * 12 + k
            x = h_ref[pl.ds(4 * g + 1, 4)].reshape(256, COLS)
            t = jnp.dot(band2_ref[...], x, preferred_element_type=F32).reshape(6, 3, OUT, COLS)
            emit(jnp.maximum(4 * g - 1, 0), t[0] + carry[0])
            emit(4 * g, t[1] + carry[1])
            emit(4 * g + 1, t[2])
            emit(4 * g + 2, t[3])
            carry = (t[4], t[5])

        @pl.when(block > 0)
        def _():
            store(block - 1).start()

        return carry

    none = jnp.zeros((3, OUT, COLS), F32)
    lax.fori_loop(0, 8, conv2, (none, none))
    store(7).start()
    for block in range(8):
        store(block).wait()


def main_conv(*args):
    vmem = pl.BlockSpec(memory_space=pltpu.VMEM)
    return pl.pallas_call(
        main_kernel,
        out_shape=jax.ShapeDtypeStruct((ROWS, OUT, COLS), BF),
        in_specs=[pl.BlockSpec(memory_space=pl.ANY)] + [vmem] * 13,
        out_specs=pl.BlockSpec(memory_space=pl.ANY),
        scratch_shapes=[
            pltpu.VMEM((HALF + 2, 48, COLS), BF),
            pltpu.VMEM((ROWS, HID, COLS), BF),
            pltpu.VMEM((ROWS + 2, HID, COLS), BF),
            pltpu.VMEM((4, 3, OUT, 128), F32),
            pltpu.VMEM((192, 240), BF),
            pltpu.VMEM((144, 256), BF),
            pltpu.VMEM((HID, 288), BF),
            pltpu.VMEM((2, 2 * OUT, 384), BF),
            pltpu.VMEM((2, FLD, 128), BF),
            pltpu.VMEM((ROWS, OUT, COLS), BF),
            pltpu.SemaphoreType.DMA((BLOCKS,)),
            pltpu.SemaphoreType.DMA((8,)),
        ],
        compiler_params=pltpu.CompilerParams(vmem_limit_bytes=44 << 20),
        name="convs",
    )(*args)


def onehot(pairs, rows, cols):
    src = subs((rows, cols))
    dst = lanes((rows, cols))
    hit = jnp.zeros((rows, cols), jnp.bool_)
    for source, cond in pairs:
        hit = hit | ((src == source(dst)) & cond(dst))
    return hit.astype(BF)


def patch_kernel(
    fold_ref, south_ref, low_ref, mid_ref, top_ref, north_ref, tops_ref, strip_ref,
    w1_ref, b1_ref, w2_ref, b2_ref, main_ref, out_ref, in_ref, res_ref, sem,
):
    gy, gx = lax.axis_index("gy"), lax.axis_index("gx")
    signs = jnp.where(
        (subs((2 * FLD, PAD)) < 8) | (subs((2 * FLD, PAD)) == 16) | (subs((2 * FLD, PAD)) == 17), -1.0, 1.0
    )
    at = 0
    for ref, count in ((south_ref, 2), (low_ref, 2), (mid_ref, 4), (top_ref, 2), (north_ref, 2)):
        for k in range(count):
            in_ref[at] = ref[k].astype(F32)
            at += 1
    for k in range(3):
        in_ref[12 + k] = jnp.zeros((2 * FLD, PAD), F32)

    wrap = lambda t: jnp.where(t < 0, t + 16, jnp.where(t > 15, t - 16, t))
    near = wrap(gx - 1)
    far = wrap(gx + 1)
    p = fold_ref[gx]
    a = fold_ref[near]
    b = fold_ref[far]

    @pl.when(gy == 7)
    def _():
        def move(x, pairs):
            return jnp.dot(x, onehot(pairs, x.shape[1], PAD), preferred_element_type=F32)

        def inside(lo, hi):
            return lambda d: (d >= lo) & (d <= hi)

        def put(column, lane_at, step=0):
            count = 2 if step else 1
            return [(lambda d: column + step * (d - lane_at), inside(lane_at, lane_at + count - 1))]

        mirror = lambda d: SHIFT + COLS - 1 - d
        row = move(tops_ref[p, 1], [(mirror, inside(SHIFT, SHIFT + 255))])
        row = row + move(tops_ref[a, 1], put(1, 0, -1))
        row = row + move(tops_ref[b, 1], put(COLS - 1, SHIFT + COLS, -1))
        in_ref[10] = row * signs
        for k in range(2):
            in_ref[12 + k] = (
                move(tops_ref[p, k], [(mirror, inside(SHIFT, SHIFT + 255))])
                + move(tops_ref[wrap(p + 1), k], put(0, SHIFT - 1))
                + move(tops_ref[wrap(p - 1), k], put(COLS - 1, SHIFT + COLS))
                + move(tops_ref[a, k], put(1, 264, -1))
                + move(tops_ref[wrap(a - 1), k], put(COLS - 1, 266))
                + move(tops_ref[b, k], put(COLS - 1, 273, -1))
                + move(tops_ref[wrap(b + 1), k], put(0, 272))
            )
        last = move(
            in_ref[9].astype(BF),
            [(lambda d: d, inside(SHIFT, SHIFT + 255))] + put(0, 264, 1) + put(SHIFT + COLS, 273, 1),
        )
        last = last + move(tops_ref[fold_ref[wrap(p + 1)], 1], put(COLS - 1, SHIFT - 1))
        last = last + move(tops_ref[fold_ref[wrap(p - 1)], 1], put(0, SHIFT + COLS))
        last = last + move(tops_ref[fold_ref[wrap(a - 1)], 1], put(0, 266))
        last = last + move(tops_ref[fold_ref[wrap(b + 1)], 1], put(COLS - 1, 272))
        in_ref[14] = last * signs

    def shifted(x):
        return [pltpu.roll(x, 1, 1).astype(BF), x.astype(BF), pltpu.roll(x, PAD - 1, 1).astype(BF)]

    inputs = [shifted(in_ref[k]) for k in range(15)]
    weights = [
        jnp.concatenate([w1_ref[u, 2 - v if flip else v] for u in range(3) for v in range(3)], axis=1)
        for flip in (False, True)
    ]

    def hidden(rows, flip):
        x = jnp.concatenate(inputs[rows] + inputs[rows + 1] + inputs[rows + 2], axis=0)
        total = jnp.dot(weights[flip], x, preferred_element_type=F32)
        return jnp.maximum(total + b1_ref[:, 0:1], 0.0).astype(BF)

    virtual = hidden(12, True).astype(F32)
    lane = lanes((HID, PAD))
    virtual = jnp.where(
        lane == SHIFT - 1,
        pltpu.roll(virtual, (SHIFT - 1 - 265) % PAD, 1),
        jnp.where(lane == SHIFT + 256, pltpu.roll(virtual, (SHIFT + 256 - 273) % PAD, 1), virtual),
    )
    second = jnp.concatenate([w2_ref[u, v] for u in range(3) for v in range(3)], axis=1)
    for half in range(2):
        hid = [hidden(6 * half + k, False).astype(F32) for k in range(4)]
        if half == 0:
            hid[0] = jnp.where(gy == 0, jnp.zeros_like(hid[0]), hid[0])
        else:
            hid[3] = jnp.where(gy == 7, virtual, hid[3])
        around = [shifted(x) for x in hid]
        for r in range(2):
            x = jnp.concatenate(around[r] + around[r + 1] + around[r + 2], axis=0)
            total = jnp.dot(second, x, preferred_element_type=F32) + b2_ref[:, 0:1]
            m = strip_ref[6 * half + r, FLD : 2 * FLD, :].astype(F32)[:OUT]
            total = pltpu.roll(total * m, PAD - SHIFT, 1)
            res_ref[2 * half + r] = total[:, :COLS].astype(BF)
    copies = [
        pltpu.make_async_copy(res_ref.at[pl.ds(0, 2)], out_ref.at[pl.ds(0, 2)], sem.at[0]),
        pltpu.make_async_copy(res_ref.at[pl.ds(2, 2)], out_ref.at[pl.ds(ROWS - 2, 2)], sem.at[1]),
    ]
    for c in copies:
        c.start()
    for c in copies:
        c.wait()


def patch_rows(*args):
    smem = pl.BlockSpec(memory_space=pltpu.SMEM)
    vmem = pl.BlockSpec(memory_space=pltpu.VMEM)
    hbm = pl.BlockSpec(memory_space=pl.ANY)
    return pl.pallas_call(
        patch_kernel,
        out_shape=jax.ShapeDtypeStruct((ROWS, OUT, COLS), BF),
        in_specs=[smem] + [vmem] * 11 + [hbm],
        out_specs=hbm,
        scratch_shapes=[
            pltpu.VMEM((15, 2 * FLD, PAD), F32),
            pltpu.VMEM((4, OUT, COLS), BF),
            pltpu.SemaphoreType.DMA((2,)),
        ],
        input_output_aliases={12: 0},
        compiler_params=pltpu.CompilerParams(vmem_limit_bytes=24 << 20),
        name="patch",
    )(*args)


def shift_gx(x, step):
    n = lax.axis_size("gx")
    return lax.ppermute(x, "gx", [(i, (i + step) % n) for i in range(n)])


def shift_gy(x, step):
    n = lax.axis_size("gy")
    return lax.ppermute(x, "gy", [(i, i + step) for i in range(n) if 0 <= i + step < n])


def per_device(
    ocean, atm, dest_tile, dest_row, live, land_mask, fold_pair, w1, b1, w2, b2
):
    outgoing = pack(
        dest_tile.reshape(1, HALF), dest_row.reshape(1, HALF), live.reshape(1, HALF), atm.reshape(2 * HALF, 8, 128)
    )
    incoming = lax.all_to_all(
        outgoing.reshape(DEV, STEP, 8, 128), ("gy", "gx"), split_axis=0, concat_axis=0, tiled=True
    )
    ocean, land_mask, _ = lax.optimization_barrier((ocean, land_mask, outgoing))
    first, last = edge_columns(ocean, land_mask)
    west = shift_gx(last, 1)
    east = shift_gx(first, -1)
    part, rows, w1, b1c, b2c = ocean_part(
        ocean, land_mask, w1.swapaxes(2, 3), b1.reshape(1, HID), b2.reshape(1, OUT)
    )
    m3, strip = margins(land_mask, west, east, rows)

    coarse, ccols, cwest, ceast, low, mid, top, tops = coarse_sums(
        incoming, strip
    )
    south = shift_gy(top, 1)
    north = shift_gy(low, -1)
    tops = lax.all_to_all(tops, "gx", split_axis=0, concat_axis=0, tiled=True)
    out = main_conv(
        part, m3, coarse, first, last, west, east, ccols, cwest, ceast, w1, b1c, w2, b2c,
    )
    return patch_rows(
        fold_pair, south, low, mid, top, north, tops, strip, w1, b1c, w2, b2c, out
    )


def solution(mesh):
    return jax.shard_map(
        per_device,
        mesh=mesh,
        in_specs=(
            P("gy", None, "gx"),
            P(("gy", "gx"), None, None),
            P(("gy", "gx"), None),
            P(("gy", "gx")),
            P(("gy", "gx")),
            P("gy", "gx"),
            P(),
            P(),
            P(),
            P(),
            P(),
        ),
        out_specs=P("gy", None, "gx"),
        check_vma=False,
    )
```

```python
import functools

import jax
import jax.numpy as jnp
from jax import lax
from jax.experimental import pallas as pl
from jax.experimental.pallas import tpu as pltpu
from jax.sharding import PartitionSpec as P

BF = jnp.bfloat16
F32 = jnp.float32
I32 = jnp.int32
VMEM_LIMIT = 56 << 20
ROWS = 384
COLS = 256
HALF = 192
DEV = 128
CAP = 3
FLD = 16
HID = 64
OUT = 8
PAD = 384
SHIFT = 2


def lanes(shape):
    return lax.broadcasted_iota(I32, shape, len(shape) - 1)


def subs(shape):
    return lax.broadcasted_iota(I32, shape, len(shape) - 2)


STEP = 2 * CAP + 1


PIECES = 8


def pack_kernel(
    tile_ref, row_ref, live_ref, atm_hbm, out_hbm, atm_ref, out_ref, head_ref, q_ref, code_ref,
    info_ref, sem, in_sem, out_sem, head_sem,
):
    loads, stores = [], []
    for c in range(PIECES):
        at = pl.ds(c * (2 * HALF // PIECES), 2 * HALF // PIECES)
        loads.append(pltpu.make_async_copy(atm_hbm.at[at], atm_ref.at[at], in_sem.at[c]))
        at = pl.ds(c * (DEV // PIECES), DEV // PIECES)
        stores.append(
            pltpu.make_async_copy(out_ref.at[at], out_hbm.at[at, pl.ds(0, STEP - 1)], out_sem.at[c])
        )
        loads[c].start()
    across = jnp.concatenate([tile_ref[...].astype(F32), jnp.full((1, 64), -1.0, F32)], axis=1)
    column = jnp.broadcast_to(across, (128, 256))
    column = jnp.concatenate([column[:, :128].T, column[:, 128:].T[:64]], axis=0)
    earlier = (subs((HALF, 256)) < lanes((HALF, 256))) & (
        jnp.concatenate([column, column], axis=1) == jnp.broadcast_to(across, (HALF, 256))
    )
    code = 4.0 * across + jnp.sum(earlier.astype(F32), axis=0, keepdims=True)
    code_ref[...] = code.astype(I32)
    copy = pltpu.make_async_copy(code_ref, info_ref, sem)
    copy.start()
    lane = lanes((FLD, 128))
    first, last = [], []
    for chunk, count, need in ((0, 128, loads[:6]), (128, 64, loads[6:])):
        for load in need:
            load.wait()

        def ends(i, carry):
            c0, c1 = carry
            block = atm_ref[pl.ds(2 * (chunk + i), 2)].reshape(FLD, 128)
            here = lane == i
            c0 = jnp.where(here, pltpu.roll(block, i, 1), c0)
            c1 = jnp.where(here, pltpu.roll(block, i + 1, 1), c1)
            return c0, c1

        zero = jnp.zeros((FLD, 128), BF)
        c0, c1 = lax.fori_loop(0, count, ends, (zero, zero), unroll=32)
        first.append(c0)
        last.append(c1)
    copy.wait()

    def place(n, carry):
        code = info_ref[0, n]
        out_ref[code >> 2, pl.ds(2 * (code & 3), 2)] = atm_ref[pl.ds(2 * n, 2)]
        return carry

    lax.fori_loop(0, HALF, place, 0, unroll=32)
    for store in stores:
        store.start()
    values = [jnp.concatenate(last, axis=1), jnp.concatenate(first, axis=1)]
    code = jnp.broadcast_to(code_ref[...], (DEV, 256))
    row = jnp.where(live_ref[...] == 1, row_ref[...] + 1, 0).astype(F32)
    row = jnp.concatenate([row, jnp.zeros((1, 64), F32)], axis=1).astype(BF)
    hits, columns = [], []
    tile = subs((DEV, 256))
    none = jnp.zeros((FLD, 256), BF)
    for k in range(CAP):
        hits.append((code == 4 * tile + k).astype(BF))
        rows = jnp.where(subs((FLD, 256)) == k, jnp.broadcast_to(row, (FLD, 256)), none)
        parts = [rows] + [values[0] if i == k else none for i in range(3)]
        parts = parts + [values[1] if i == k else none for i in range(3)] + [none]
        columns.append(jnp.concatenate(parts, axis=0))
    total = lax.dot_general(
        jnp.concatenate(hits, axis=1),
        jnp.concatenate(columns, axis=1),
        (((1,), (1,)), ((), ())),
        preferred_element_type=F32,
    )
    q_ref[...] = total
    sub = subs((8, 128))
    for t in range(DEV):
        near = (t & -16) + ((t + 15) & 15)
        far = (t & -16) + ((t + 1) & 15)
        own, west, east = [jnp.broadcast_to(q_ref[i : i + 1, :], (8, 128)) for i in (t, near, far)]
        head_ref[t] = jnp.where(sub == 0, own, jnp.where(sub == 1, west, east)).astype(BF)
    heads = pltpu.make_async_copy(head_ref, out_hbm.at[:, STEP - 1], head_sem)
    heads.start()
    for store in stores:
        store.wait()
    heads.wait()


def pack(tile, row, live, atm):
    vmem = pl.BlockSpec(memory_space=pltpu.VMEM)
    hbm = pl.BlockSpec(memory_space=pl.ANY)
    return pl.pallas_call(
        pack_kernel,
        out_shape=jax.ShapeDtypeStruct((DEV, STEP, 8, 128), BF),
        in_specs=[vmem, vmem, vmem, hbm],
        out_specs=hbm,
        scratch_shapes=[
            pltpu.VMEM((2 * HALF, 8, 128), BF),
            pltpu.VMEM((DEV, STEP - 1, 8, 128), BF),
            pltpu.VMEM((DEV, 8, 128), BF),
            pltpu.VMEM((DEV, 128), F32),
            pltpu.VMEM((1, 256), I32),
            pltpu.SMEM((1, 256), I32),
            pltpu.SemaphoreType.DMA,
            pltpu.SemaphoreType.DMA((PIECES,)),
            pltpu.SemaphoreType.DMA((PIECES,)),
            pltpu.SemaphoreType.DMA,
        ],
        compiler_params=pltpu.CompilerParams(vmem_limit_bytes=56 << 20),
        name="pack",
    )(tile, row, live, atm)


def coarse_kernel(
    inc_hbm, strip_ref, out_ref, cols_ref, west_ref, east_ref, low_ref, mid_ref, top_ref, tops_ref,
    inc_ref, raw_ref, acc_ref, head_ref, idx_ref, where_ref, sem, raw_sem, in_sem,
):
    raw = pltpu.make_async_copy(inc_hbm.at[:, STEP - 1], raw_ref, raw_sem)
    raw.start()
    loads = []
    for c in range(PIECES):
        at = pl.ds(c * DEV // PIECES, DEV // PIECES)
        loads.append(pltpu.make_async_copy(inc_hbm.at[at], inc_ref.at[at], in_sem.at[c]))
        loads[c].start()
    acc_ref[...] = jnp.zeros_like(acc_ref)
    raw.wait()
    few = lanes((8, 128)) < CAP
    for g in range(4):

        def gather(s, total):
            head = raw_ref[32 * g + s].astype(F32)
            head_ref[32 * g + s] = head
            return total + pltpu.roll(jnp.where(few, head, 0.0), 4 * s, 1)

        idx_ref[g] = lax.fori_loop(0, 32, gather, jnp.zeros((8, 128), F32), unroll=32).astype(I32)
    copy = pltpu.make_async_copy(idx_ref, where_ref, sem)
    copy.start()
    target = (subs((256, DEV)) + 1).astype(F32)
    for j, wanted in (
        (0, ((4 * FLD, cols_ref.at[0]), (FLD, cols_ref.at[1]))),
        (1, ((FLD, west_ref),)),
        (2, ((4 * FLD, east_ref),)),
    ):
        turned = head_ref[:, j, :].T
        values = turned.astype(BF)
        hits = jnp.concatenate(
            [
                (jnp.broadcast_to(turned[k : k + 1], (256, DEV)) == target).astype(BF)
                for k in range(CAP)
            ],
            axis=1,
        )
        blocks = jnp.concatenate(
            [
                jnp.concatenate([values[at + FLD * k : at + FLD * k + FLD] for k in range(CAP)], axis=1)
                for at, _ in wanted
            ],
            axis=0,
        )
        total = lax.dot_general(blocks, hits, (((1,), (1,)), ((), ())), preferred_element_type=F32)
        for n, (_, ref) in enumerate(wanted):
            ref[...] = total[n * FLD : n * FLD + FLD].astype(BF)
    copy.wait()
    for c in range(PIECES):
        loads[c].wait()
        count = DEV // PIECES

        def add(i, carry):
            for k in range(CAP):
                r = where_ref[c * count // 32, 0, 4 * (c * count % 32 + i) + k]
                block = inc_ref[c * count + i, 2 * k : 2 * k + 2]
                acc_ref[k, r] = acc_ref[k, r] + block.astype(F32)
            return carry

        lax.fori_loop(0, count, add, 0, unroll=16)
    lane = lanes((FLD, 128))

    def summed(r):
        total = acc_ref[0, r + 1] + acc_ref[1, r + 1] + acc_ref[2, r + 1]
        return total.reshape(FLD, 128).astype(BF)

    def finish(r, carry):
        out_ref[r] = summed(r)
        return carry

    spread = (subs((256, PAD)) == lanes((256, PAD)) // 2).astype(BF)
    wides = []
    for r in (0, 1, HALF - 2, HALF - 1):
        chunk, i = (r // 128) * 128, r % 128
        west = pltpu.roll(west_ref[:, chunk : chunk + 128].astype(F32), (128 - i) % 128, 1)
        east = pltpu.roll(east_ref[:, chunk : chunk + 128].astype(F32), (129 - i) % 128, 1)
        row = pltpu.roll(summed(r).astype(F32), 1, 1)
        wides.append(jnp.concatenate(
            [
                jnp.where(lane == 0, west, row),
                jnp.where(lane == 0, row, jnp.where(lane == 1, east, 0.0)),
            ],
            axis=1,
        ).astype(BF))
    fines = jnp.dot(jnp.concatenate(wides, axis=0), spread, preferred_element_type=F32).astype(BF)
    for k in range(4):
        fine = fines[k * FLD : k * FLD + FLD]
        for h in range(2):
            n = 2 * k + h
            ref, at = ((low_ref, n), (mid_ref, n - 2), (mid_ref, n - 2), (top_ref, n - 6))[k]
            ref[at, 0:FLD, :] = strip_ref[n, 0:FLD, :]
            ref[at, FLD : 2 * FLD, :] = fine * strip_ref[n, FLD : 2 * FLD, :]
    for h in range(2):
        row = pltpu.roll(top_ref[h].astype(F32), PAD - SHIFT, 1)[:, :COLS].astype(BF)
        for t in range(16):
            tops_ref[t, h] = row
    lax.fori_loop(0, HALF, finish, 0, unroll=16)


def coarse_sums(incoming, strip):
    return pl.pallas_call(
        coarse_kernel,
        out_shape=(
            jax.ShapeDtypeStruct((HALF, FLD, 128), BF),
            jax.ShapeDtypeStruct((2, FLD, 256), BF),
            jax.ShapeDtypeStruct((FLD, 256), BF),
            jax.ShapeDtypeStruct((FLD, 256), BF),
            jax.ShapeDtypeStruct((2, 2 * FLD, PAD), BF),
            jax.ShapeDtypeStruct((4, 2 * FLD, PAD), BF),
            jax.ShapeDtypeStruct((2, 2 * FLD, PAD), BF),
            jax.ShapeDtypeStruct((16, 2, 2 * FLD, COLS), BF),
        ),
        in_specs=[pl.BlockSpec(memory_space=pl.ANY), pl.BlockSpec(memory_space=pltpu.VMEM)],
        scratch_shapes=[
            pltpu.VMEM((DEV, STEP, 8, 128), BF),
            pltpu.VMEM((DEV, 8, 128), BF),
            pltpu.VMEM((CAP, HALF + 1, 2, 8, 128), F32),
            pltpu.VMEM((DEV, 8, 128), F32),
            pltpu.VMEM((4, 8, 128), I32),
            pltpu.SMEM((4, 8, 128), I32),
            pltpu.SemaphoreType.DMA,
            pltpu.SemaphoreType.DMA,
            pltpu.SemaphoreType.DMA((PIECES,)),
        ],
        compiler_params=pltpu.CompilerParams(vmem_limit_bytes=20 << 20),
        name="coarse",
    )(incoming, strip)


def edge_kernel(ocean_ref, mask_ref, first_ref, last_ref):
    lane = lanes((FLD, 128))
    for chunk in range(3):
        block = mask_ref[chunk * 128 : chunk * 128 + 128, :].astype(F32)
        m_left = block[:, :128].T
        m_right = block[:, 128:].T

        def take(i, carry):
            x = ocean_ref[chunk * 128 + i]
            left, right = x[:, :128], x[:, 128:]
            here = lane == i
            c0, c1, c2, c3 = carry
            c0 = jnp.where(here, pltpu.roll(left, i, 1), c0)
            c1 = jnp.where(here, pltpu.roll(left, i + 127, 1), c1)
            c2 = jnp.where(here, pltpu.roll(right, i + 2, 1), c2)
            c3 = jnp.where(here, pltpu.roll(right, i + 1, 1), c3)
            return c0, c1, c2, c3

        zero = jnp.zeros((FLD, 128), BF)
        got = lax.fori_loop(0, 128, take, (zero,) * 4, unroll=16)
        rows = (m_left[0:1], m_left[1:2], m_right[126:127], m_right[127:128])
        for k in range(4):
            m = jnp.broadcast_to(rows[k], (FLD, 128)).astype(BF)
            ref = last_ref if k >= 2 else first_ref
            ref[k % 2, :, chunk * 128 : chunk * 128 + 128] = jnp.concatenate([got[k] * m, m], axis=0)


def edge_columns(ocean, mask):
    return pl.pallas_call(
        edge_kernel,
        out_shape=(jax.ShapeDtypeStruct((2, 2 * FLD, ROWS), BF),) * 2,
        compiler_params=pltpu.CompilerParams(vmem_limit_bytes=24 << 20),
        name="edges",
    )(ocean, mask)


BLOCKS = 16


def banded(w_ref, dst_ref, first):
    dst_ref[...] = jnp.zeros_like(dst_ref)
    for r in range(3):
        for u in range(3):
            for v in range(3):
                at = ((r + u) * 3 + v) * FLD
                dst_ref[r * HID : r * HID + HID, at : at + FLD] = w_ref[u, v, :, first : first + FLD]


def ocean_kernel(
    ocean_ref, mask_ref, wt_ref, b1_ref, b2_ref, part_ref, strip_ref, w_ref, b1c_ref, b2c_ref, xs_ref, band_ref, h_ref, sem,
):
    for u in range(3):
        for v in range(3):
            w_ref[u, v] = wt_ref[u, v].astype(F32).T.astype(BF)
    b1c_ref[...] = jnp.broadcast_to(b1_ref[...], (128, HID)).T
    b2c_ref[...] = jnp.broadcast_to(b2_ref[...], (128, OUT)).T
    banded(w_ref, band_ref, 0)
    bias = jnp.concatenate([b1c_ref[:, 0:1]] * 3, axis=0)
    lane16 = lanes((FLD, 128))
    zero = jnp.zeros((48, COLS), BF)
    xs_ref[0] = zero
    xs_ref[ROWS + 1] = zero
    nothing = jnp.zeros((FLD, 128), BF)

    def build(y):
        m = jnp.broadcast_to(mask_ref[pl.ds(y, 1), :].astype(F32), (FLD, COLS)).astype(BF)
        x = ocean_ref[y] * m
        up, down = pltpu.roll(x, 1, 1), pltpu.roll(x, COLS - 1, 1)
        xs_ref[y + 1, 0:16, 0:128] = jnp.where(lane16 == 0, nothing, up[:, :128])
        xs_ref[y + 1, 0:16, 128:256] = up[:, 128:]
        xs_ref[y + 1, 16:32, :] = x
        xs_ref[y + 1, 32:48, 0:128] = down[:, :128]
        xs_ref[y + 1, 32:48, 128:256] = jnp.where(lane16 == 127, nothing, down[:, 128:])

    for n, y in enumerate((0, 1, 2, 3, ROWS - 4, ROWS - 3, ROWS - 2, ROWS - 1)):
        m = jnp.broadcast_to(mask_ref[y : y + 1, :].astype(F32), (FLD, COLS))
        x = jnp.concatenate([ocean_ref[y].astype(F32) * m, m], axis=0)
        x = jnp.concatenate([x, jnp.zeros((2 * FLD, 128), F32)], axis=1)
        strip_ref[n] = pltpu.roll(x, SHIFT, 1).astype(BF)

    def first(i, carry):
        build(i)
        return carry

    lax.fori_loop(0, 24, first, 0, unroll=8)

    def conv(block, carry):
        for k in range(8):
            g = block * 8 + k
            for r in range(3):
                build(jnp.minimum(3 * g + 24 + r, ROWS - 1))
            x = xs_ref[pl.ds(3 * g, 5)].reshape(240, COLS)
            t = jnp.dot(band_ref[...], x, preferred_element_type=F32) + bias
            h_ref[pl.ds(3 * g, 3)] = t.astype(BF).reshape(3, HID, COLS)
        at = pl.ds(block * 24, 24)
        pltpu.make_async_copy(h_ref.at[at], part_ref.at[at], sem.at[block]).start()
        return carry

    lax.fori_loop(0, BLOCKS, conv, 0)
    for block in range(BLOCKS):
        at = pl.ds(block * 24, 24)
        pltpu.make_async_copy(h_ref.at[at], part_ref.at[at], sem.at[block]).wait()


def ocean_part(*args):
    return pl.pallas_call(
        ocean_kernel,
        out_shape=(
            jax.ShapeDtypeStruct((ROWS, HID, COLS), BF),
            jax.ShapeDtypeStruct((8, 2 * FLD, PAD), BF),
            jax.ShapeDtypeStruct((3, 3, HID, 2 * FLD), BF),
            jax.ShapeDtypeStruct((HID, 128), F32),
            jax.ShapeDtypeStruct((OUT, 128), F32),
        ),
        out_specs=(pl.BlockSpec(memory_space=pl.ANY),) + (pl.BlockSpec(memory_space=pltpu.VMEM),) * 4,
        scratch_shapes=[
            pltpu.VMEM((ROWS + 2, 48, COLS), BF),
            pltpu.VMEM((192, 240), BF),
            pltpu.VMEM((ROWS, HID, COLS), BF),
            pltpu.SemaphoreType.DMA((BLOCKS,)),
        ],
        compiler_params=pltpu.CompilerParams(vmem_limit_bytes=40 << 20),
        name="ocean",
    )(*args)


def margin_kernel(mask_ref, west_ref, east_ref, rows_ref, m3_ref, strip_ref):
    lane = lanes((128, 128))
    for chunk in range(3):
        at = slice(chunk * 128, chunk * 128 + 128)
        m = mask_ref[at, :].astype(F32)
        up, down = pltpu.roll(m, 1, 1), pltpu.roll(m, COLS - 1, 1)
        west = jnp.broadcast_to(west_ref[1, FLD : FLD + 1, at].astype(F32), (128, 128)).T
        east = jnp.broadcast_to(east_ref[0, FLD : FLD + 1, at].astype(F32), (128, 128)).T
        m3_ref[0, at, 0:128] = jnp.where(lane == 0, west, up[:, :128])
        m3_ref[0, at, 128:256] = up[:, 128:]
        m3_ref[1, at, :] = m
        m3_ref[2, at, 0:128] = down[:, :128]
        m3_ref[2, at, 128:256] = jnp.where(lane == 127, east, down[:, 128:])
    wide_lane = lanes((2 * FLD, 128))
    for n, y in enumerate((0, 1, 2, 3, ROWS - 4, ROWS - 3, ROWS - 2, ROWS - 1)):
        base, i = (y // 128) * 128, y % 128
        x = rows_ref[n].astype(F32)

        def beside(ref, k, lane_at):
            return pltpu.roll(ref[k, :, base : base + 128].astype(F32), (128 + lane_at - i) % 128, 1)

        lo = jnp.where(wide_lane == 0, beside(west_ref, 0, 0), x[:, 0:128])
        lo = jnp.where(wide_lane == 1, beside(west_ref, 1, 1), lo)
        hi = jnp.where(wide_lane == 2, beside(east_ref, 0, 2), x[:, 256:])
        hi = jnp.where(wide_lane == 3, beside(east_ref, 1, 3), hi)
        strip_ref[n, :, 0:128] = lo.astype(BF)
        strip_ref[n, :, 128:256] = x[:, 128:256].astype(BF)
        strip_ref[n, :, 256:384] = hi.astype(BF)

def margins(*args):
    return pl.pallas_call(
        margin_kernel,
        out_shape=(
            jax.ShapeDtypeStruct((3, ROWS, COLS), F32),
            jax.ShapeDtypeStruct((8, 2 * FLD, PAD), BF),
        ),
        compiler_params=pltpu.CompilerParams(vmem_limit_bytes=24 << 20),
        name="margins",
    )(*args)


def main_kernel(
    part_ref, m3_ref, coarse_ref, first_ref, last_ref, west_ref, east_ref, cown_ref, cwest_ref, ceast_ref,
    w1_ref, b1_ref, w2_ref, b2_ref, out_ref,
    fine_ref, p_ref, h_ref, add_ref, band1_ref, band2_ref, side1_ref, side2_ref, pair_ref, res_ref, sem, out_sem,
):
    def fetch(block):
        at = pl.ds(block * 24, 24)
        return pltpu.make_async_copy(part_ref.at[at], p_ref.at[at], sem.at[block])

    for block in range(BLOCKS):
        fetch(block).start()

    banded(w1_ref, band1_ref, FLD)
    band2_ref[...] = jnp.zeros_like(band2_ref)
    for u in range(3):
        for v in range(3):
            w = w2_ref[u, v]
            for i in range(4):
                at = ((i + 2 - u) * 3 + v) * OUT
                band2_ref[at : at + OUT, i * HID : i * HID + HID] = w
            w1 = w1_ref[u, v]
            at = (u * 3 + v) * 2 * FLD
            side1_ref[:, at : at + 2 * FLD] = w1
        for side in range(2):
            at = u * HID
            side2_ref[side, 0:OUT, at : at + HID] = w2_ref[u, 2 * side]
            side2_ref[side, OUT : 2 * OUT, at : at + HID] = jnp.zeros((OUT, HID), BF)
            at = (3 + u) * HID
            side2_ref[side, 0:OUT, at : at + HID] = w2_ref[u, 1]
            side2_ref[side, OUT : 2 * OUT, at : at + HID] = w2_ref[u, 2 * side]

    rep = (subs((256, ROWS)) == lanes((256, ROWS)) // 2).astype(BF)

    def column(coarse_t, strip):
        fine = jnp.dot(coarse_t, rep, preferred_element_type=F32)
        return jnp.concatenate([strip[:FLD], (fine * strip[FLD:].astype(F32)).astype(BF)], axis=0)

    w2c = column(cwest_ref[...], west_ref[0])
    w1c = column(cwest_ref[...], west_ref[1])
    o0c = column(cown_ref[0], first_ref[0])
    o1c = column(cown_ref[0], first_ref[1])
    o254c = column(cown_ref[1], last_ref[0])
    o255c = column(cown_ref[1], last_ref[1])
    e1c = column(ceast_ref[...], east_ref[0])
    e2c = column(ceast_ref[...], east_ref[1])

    def around(x):
        return jnp.concatenate([pltpu.roll(x, 1, 1), x, pltpu.roll(x, ROWS - 1, 1)], axis=0)

    groups = ((w2c, w1c, o0c), (w1c, o0c, o1c), (o255c, e1c, e2c), (o254c, o255c, e1c))
    xt = jnp.concatenate([around(jnp.concatenate(cols, axis=0)) for cols in groups], axis=1)
    hid = jnp.dot(side1_ref[...], xt, preferred_element_type=F32)
    hid = jnp.maximum(hid + b1_ref[:, 0:1], 0.0).astype(BF)
    hid = [around(hid[:, k * ROWS : k * ROWS + ROWS]) for k in range(4)]
    ends = [
        jnp.dot(
            side2_ref[side],
            jnp.concatenate(hid[2 * side : 2 * side + 2], axis=0),
            preferred_element_type=F32,
        )
        for side in range(2)
    ]
    phase = lanes((OUT, 128)) & 3
    for chunk in range(3):
        at = slice(chunk * 128, chunk * 128 + 128)
        c0 = ends[0][0:OUT, at]
        c1 = pltpu.roll(ends[0][OUT:, at], 1, 1)
        c254 = pltpu.roll(ends[1][OUT:, at], 126, 1)
        c255 = pltpu.roll(ends[1][0:OUT, at], 127, 1)
        for q in range(4):
            z = jnp.where(phase == q, c0, jnp.where(phase == (q + 1) % 4, c1, c255))
            add_ref[q, chunk] = jnp.where(phase == (q + 2) % 4, c254, z)

    lane = lanes((FLD, 128))
    spread = (subs((128, COLS)) == lanes((128, COLS)) // 2).astype(BF)
    fine_ref[0] = jnp.zeros((48, COLS), BF)
    fine_ref[HALF + 1] = jnp.zeros((48, COLS), BF)
    for chunk, count in ((0, 8), (128, 4)):
        west = cwest_ref[:, chunk : chunk + 128]
        east = pltpu.roll(ceast_ref[:, chunk : chunk + 128], 127, 1)
        for q in range(2):
            pair_ref[q] = jnp.where((lane & 1) == q, west, east)

        def widen(k, carry):
            r0 = chunk + 16 * k
            part = coarse_ref[pl.ds(r0, 16)].reshape(256, 128)
            fine = jnp.dot(part, spread, preferred_element_type=F32).astype(BF).reshape(16, FLD, COLS)
            for i in range(16):
                x = fine[i]
                beside = pltpu.roll(pair_ref[i & 1], 128 - (16 * k + i), 1)
                up, down = pltpu.roll(x, 1, 1), pltpu.roll(x, COLS - 1, 1)
                fine_ref[r0 + i + 1, 0:16, 0:128] = jnp.where(lane == 0, beside, up[:, :128])
                fine_ref[r0 + i + 1, 0:16, 128:256] = up[:, 128:]
                fine_ref[r0 + i + 1, 16:32, :] = x
                fine_ref[r0 + i + 1, 32:48, 0:128] = down[:, :128]
                fine_ref[r0 + i + 1, 32:48, 128:256] = jnp.where(lane == 127, beside, down[:, 128:])
            return carry

        lax.fori_loop(0, count, widen, 0, unroll=2)

    hzero = jnp.zeros((HID, COLS), BF)
    h_ref[0] = hzero
    h_ref[ROWS + 1] = hzero

    def conv1(block, carry):
        fetch(block).wait()
        for j in range(4):
            y0 = block * 24 + j * 6
            rows = []
            for i in range(8):
                y = y0 - 1 + i
                half = (block * 12 + j * 3) + (i + 1) // 2
                ym = y if 0 < i < 7 else jnp.clip(y, 0, ROWS - 1)
                for v in range(3):
                    m = jnp.broadcast_to(m3_ref[v, pl.ds(ym, 1), :], (FLD, COLS)).astype(BF)
                    rows.append(fine_ref[half, 16 * v : 16 * v + 16, :] * m)
            for k in range(2):
                x = jnp.concatenate(rows[9 * k : 9 * k + 15], axis=0)
                t = jnp.dot(band1_ref[...], x, preferred_element_type=F32)
                t = t + p_ref[pl.ds(y0 + 3 * k, 3)].reshape(192, COLS).astype(F32)
                h_ref[pl.ds(y0 + 3 * k + 1, 3)] = jnp.maximum(t, 0.0).astype(BF).reshape(3, HID, COLS)
        return carry

    lax.fori_loop(0, BLOCKS, conv1, 0)

    b2 = b2_ref[:, 0:1]
    lane8 = lanes((OUT, 128))

    def emit(y, t):
        ends = pltpu.roll(add_ref[y & 3, y >> 7], 128 - (y & 127), 1)
        up = pltpu.roll(t[0], 1, 1)
        down = pltpu.roll(t[2], COLS - 1, 1)
        m = m3_ref[1, pl.ds(y, 1), :]
        lo = jnp.where(lane8 == 0, 0.0, t[1, :, :128]) + b2
        lo = lo + jnp.where(lane8 < 2, ends, up[:, :128]) + down[:, :128]
        hi = jnp.where(lane8 == 127, 0.0, t[1, :, 128:]) + b2
        hi = hi + up[:, 128:] + jnp.where(lane8 > 125, ends, down[:, 128:])
        res_ref[y, :, 0:128] = (lo * m[:, :128]).astype(BF)
        res_ref[y, :, 128:256] = (hi * m[:, 128:]).astype(BF)

    def store(block):
        at = pl.ds(block * 48, 48)
        return pltpu.make_async_copy(res_ref.at[at], out_ref.at[at], out_sem.at[block])

    def conv2(block, carry):
        for k in range(12):
            g = block * 12 + k
            x = h_ref[pl.ds(4 * g + 1, 4)].reshape(256, COLS)
            t = jnp.dot(band2_ref[...], x, preferred_element_type=F32).reshape(6, 3, OUT, COLS)
            emit(jnp.maximum(4 * g - 1, 0), t[0] + carry[0])
            emit(4 * g, t[1] + carry[1])
            emit(4 * g + 1, t[2])
            emit(4 * g + 2, t[3])
            carry = (t[4], t[5])

        @pl.when(block > 0)
        def _():
            store(block - 1).start()

        return carry

    none = jnp.zeros((3, OUT, COLS), F32)
    lax.fori_loop(0, 8, conv2, (none, none))
    store(7).start()
    for block in range(8):
        store(block).wait()


def main_conv(*args):
    vmem = pl.BlockSpec(memory_space=pltpu.VMEM)
    return pl.pallas_call(
        main_kernel,
        out_shape=jax.ShapeDtypeStruct((ROWS, OUT, COLS), BF),
        in_specs=[pl.BlockSpec(memory_space=pl.ANY)] + [vmem] * 13,
        out_specs=pl.BlockSpec(memory_space=pl.ANY),
        scratch_shapes=[
            pltpu.VMEM((HALF + 2, 48, COLS), BF),
            pltpu.VMEM((ROWS, HID, COLS), BF),
            pltpu.VMEM((ROWS + 2, HID, COLS), BF),
            pltpu.VMEM((4, 3, OUT, 128), F32),
            pltpu.VMEM((192, 240), BF),
            pltpu.VMEM((144, 256), BF),
            pltpu.VMEM((HID, 288), BF),
            pltpu.VMEM((2, 2 * OUT, 384), BF),
            pltpu.VMEM((2, FLD, 128), BF),
            pltpu.VMEM((ROWS, OUT, COLS), BF),
            pltpu.SemaphoreType.DMA((BLOCKS,)),
            pltpu.SemaphoreType.DMA((8,)),
        ],
        compiler_params=pltpu.CompilerParams(vmem_limit_bytes=44 << 20),
        name="convs",
    )(*args)


def onehot(pairs, rows, cols):
    src = subs((rows, cols))
    dst = lanes((rows, cols))
    hit = jnp.zeros((rows, cols), jnp.bool_)
    for source, cond in pairs:
        hit = hit | ((src == source(dst)) & cond(dst))
    return hit.astype(BF)


def patch_kernel(
    fold_ref, south_ref, low_ref, mid_ref, top_ref, north_ref, tops_ref, strip_ref,
    w1_ref, b1_ref, w2_ref, b2_ref, main_ref, out_ref, in_ref, res_ref, sem,
):
    gy, gx = lax.axis_index("gy"), lax.axis_index("gx")
    signs = jnp.where(
        (subs((2 * FLD, PAD)) < 8) | (subs((2 * FLD, PAD)) == 16) | (subs((2 * FLD, PAD)) == 17), -1.0, 1.0
    )
    at = 0
    for ref, count in ((south_ref, 2), (low_ref, 2), (mid_ref, 4), (top_ref, 2), (north_ref, 2)):
        for k in range(count):
            in_ref[at] = ref[k].astype(F32)
            at += 1
    for k in range(3):
        in_ref[12 + k] = jnp.zeros((2 * FLD, PAD), F32)

    wrap = lambda t: jnp.where(t < 0, t + 16, jnp.where(t > 15, t - 16, t))
    near = wrap(gx - 1)
    far = wrap(gx + 1)
    p = fold_ref[gx]
    a = fold_ref[near]
    b = fold_ref[far]

    @pl.when(gy == 7)
    def _():
        def move(x, pairs):
            return jnp.dot(x, onehot(pairs, x.shape[1], PAD), preferred_element_type=F32)

        def inside(lo, hi):
            return lambda d: (d >= lo) & (d <= hi)

        def put(column, lane_at, step=0):
            count = 2 if step else 1
            return [(lambda d: column + step * (d - lane_at), inside(lane_at, lane_at + count - 1))]

        mirror = lambda d: SHIFT + COLS - 1 - d
        row = move(tops_ref[p, 1], [(mirror, inside(SHIFT, SHIFT + 255))])
        row = row + move(tops_ref[a, 1], put(1, 0, -1))
        row = row + move(tops_ref[b, 1], put(COLS - 1, SHIFT + COLS, -1))
        in_ref[10] = row * signs
        for k in range(2):
            in_ref[12 + k] = (
                move(tops_ref[p, k], [(mirror, inside(SHIFT, SHIFT + 255))])
                + move(tops_ref[wrap(p + 1), k], put(0, SHIFT - 1))
                + move(tops_ref[wrap(p - 1), k], put(COLS - 1, SHIFT + COLS))
                + move(tops_ref[a, k], put(1, 264, -1))
                + move(tops_ref[wrap(a - 1), k], put(COLS - 1, 266))
                + move(tops_ref[b, k], put(COLS - 1, 273, -1))
                + move(tops_ref[wrap(b + 1), k], put(0, 272))
            )
        last = move(
            in_ref[9].astype(BF),
            [(lambda d: d, inside(SHIFT, SHIFT + 255))] + put(0, 264, 1) + put(SHIFT + COLS, 273, 1),
        )
        last = last + move(tops_ref[fold_ref[wrap(p + 1)], 1], put(COLS - 1, SHIFT - 1))
        last = last + move(tops_ref[fold_ref[wrap(p - 1)], 1], put(0, SHIFT + COLS))
        last = last + move(tops_ref[fold_ref[wrap(a - 1)], 1], put(0, 266))
        last = last + move(tops_ref[fold_ref[wrap(b + 1)], 1], put(COLS - 1, 272))
        in_ref[14] = last * signs

    def shifted(x):
        return [pltpu.roll(x, 1, 1).astype(BF), x.astype(BF), pltpu.roll(x, PAD - 1, 1).astype(BF)]

    inputs = [shifted(in_ref[k]) for k in range(15)]
    weights = [
        jnp.concatenate([w1_ref[u, 2 - v if flip else v] for u in range(3) for v in range(3)], axis=1)
        for flip in (False, True)
    ]

    def hidden(rows, flip):
        x = jnp.concatenate(inputs[rows] + inputs[rows + 1] + inputs[rows + 2], axis=0)
        total = jnp.dot(weights[flip], x, preferred_element_type=F32)
        return jnp.maximum(total + b1_ref[:, 0:1], 0.0).astype(BF)

    virtual = hidden(12, True).astype(F32)
    lane = lanes((HID, PAD))
    virtual = jnp.where(
        lane == SHIFT - 1,
        pltpu.roll(virtual, (SHIFT - 1 - 265) % PAD, 1),
        jnp.where(lane == SHIFT + 256, pltpu.roll(virtual, (SHIFT + 256 - 273) % PAD, 1), virtual),
    )
    second = jnp.concatenate([w2_ref[u, v] for u in range(3) for v in range(3)], axis=1)
    for half in range(2):
        hid = [hidden(6 * half + k, False).astype(F32) for k in range(4)]
        if half == 0:
            hid[0] = jnp.where(gy == 0, jnp.zeros_like(hid[0]), hid[0])
        else:
            hid[3] = jnp.where(gy == 7, virtual, hid[3])
        around = [shifted(x) for x in hid]
        for r in range(2):
            x = jnp.concatenate(around[r] + around[r + 1] + around[r + 2], axis=0)
            total = jnp.dot(second, x, preferred_element_type=F32) + b2_ref[:, 0:1]
            m = strip_ref[6 * half + r, FLD : 2 * FLD, :].astype(F32)[:OUT]
            total = pltpu.roll(total * m, PAD - SHIFT, 1)
            res_ref[2 * half + r] = total[:, :COLS].astype(BF)
    copies = [
        pltpu.make_async_copy(res_ref.at[pl.ds(0, 2)], out_ref.at[pl.ds(0, 2)], sem.at[0]),
        pltpu.make_async_copy(res_ref.at[pl.ds(2, 2)], out_ref.at[pl.ds(ROWS - 2, 2)], sem.at[1]),
    ]
    for c in copies:
        c.start()
    for c in copies:
        c.wait()


def patch_rows(*args):
    smem = pl.BlockSpec(memory_space=pltpu.SMEM)
    vmem = pl.BlockSpec(memory_space=pltpu.VMEM)
    hbm = pl.BlockSpec(memory_space=pl.ANY)
    return pl.pallas_call(
        patch_kernel,
        out_shape=jax.ShapeDtypeStruct((ROWS, OUT, COLS), BF),
        in_specs=[smem] + [vmem] * 11 + [hbm],
        out_specs=hbm,
        scratch_shapes=[
            pltpu.VMEM((15, 2 * FLD, PAD), F32),
            pltpu.VMEM((4, OUT, COLS), BF),
            pltpu.SemaphoreType.DMA((2,)),
        ],
        input_output_aliases={12: 0},
        compiler_params=pltpu.CompilerParams(vmem_limit_bytes=24 << 20),
        name="patch",
    )(*args)


def shift_gx(x, step):
    n = lax.axis_size("gx")
    return lax.ppermute(x, "gx", [(i, (i + step) % n) for i in range(n)])


def shift_gy(x, step):
    n = lax.axis_size("gy")
    return lax.ppermute(x, "gy", [(i, i + step) for i in range(n) if 0 <= i + step < n])


def per_device(
    ocean, atm, dest_tile, dest_row, live, land_mask, fold_pair, w1, b1, w2, b2
):
    outgoing = pack(
        dest_tile.reshape(1, HALF), dest_row.reshape(1, HALF), live.reshape(1, HALF), atm.reshape(2 * HALF, 8, 128)
    )
    incoming = lax.all_to_all(
        outgoing, ("gy", "gx"), split_axis=0, concat_axis=0, tiled=True
    )
    ocean, land_mask, _ = lax.optimization_barrier((ocean, land_mask, outgoing))
    first, last = edge_columns(ocean, land_mask)
    west = shift_gx(last, 1)
    east = shift_gx(first, -1)
    part, rows, w1, b1c, b2c = ocean_part(
        ocean, land_mask, w1.swapaxes(2, 3), b1.reshape(1, HID), b2.reshape(1, OUT)
    )
    m3, strip = margins(land_mask, west, east, rows)

    coarse, ccols, cwest, ceast, low, mid, top, tops = coarse_sums(
        incoming, strip
    )
    south = shift_gy(top, 1)
    north = shift_gy(low, -1)
    tops = lax.all_to_all(tops, "gx", split_axis=0, concat_axis=0, tiled=True)
    out = main_conv(
        part, m3, coarse, first, last, west, east, ccols, cwest, ceast, w1, b1c, w2, b2c,
    )
    return patch_rows(
        fold_pair, south, low, mid, top, north, tops, strip, w1, b1c, w2, b2c, out
    )


def solution(mesh):
    return jax.shard_map(
        per_device,
        mesh=mesh,
        in_specs=(
            P("gy", None, "gx"),
            P(("gy", "gx"), None, None),
            P(("gy", "gx"), None),
            P(("gy", "gx")),
            P(("gy", "gx")),
            P("gy", "gx"),
            P(),
            P(),
            P(),
            P(),
            P(),
        ),
        out_specs=P("gy", None, "gx"),
        check_vma=False,
    )
```
